32 devices in a mesh: dp: 4 (over y, core), expert: 2 (over x), tensor: 4 (over z).
Axes of the slice: x: 2, y: 2, z: 4, core: 2. Of those that a mesh axis runs over, the one named last changes fastest.
Arguments:
- inputs: bfloat16 [1576, 768], P(('dp', 'expert')), may hold values from -6 to 6
- first_gain: float32 [768], replicated, may hold values from 0.5 to 1.5
- first_bias: float32 [768], replicated, may hold values from -2 to 2
- attention_in: bfloat16 [3, 768, 768], P(None, None, 'tensor')
- attention_out: bfloat16 [768, 768], P('tensor'), may hold values from -0.875 to 0.875
- second_gain: float32 [768], replicated, may hold values from 0.5 to 1.5
- second_bias: float32 [768], replicated, may hold values from -2 to 2
- router_weight: float32 [768, 4], replicated
- expert_in: bfloat16 [4, 768, 3072], P('expert', None, 'tensor'), may hold values from -0.21875 to 0.21875
- expert_out: bfloat16 [4, 3072, 768], P('expert', 'tensor'), may hold values from -1.75 to 1.75
- expert_ids: int32 [1576, 2], P(('dp', 'expert')), may hold values from 0 to 3, as said below
- slot_index: int32 [1576, 2], P(('dp', 'expert')), may hold values from 0 to 98, as said below
- cotangent: bfloat16 [1576, 768], P(('dp', 'expert')), may hold values from -6 to 6
Outputs:
- layer_out: float32 [1576, 768], P(('dp', 'expert'))
- input_grad: float32 [1576, 768], P(('dp', 'expert'))
- first_gain_grad: float32 [768], P(('dp', 'expert'))
- first_bias_grad: float32 [768], P(('dp', 'expert'))
- attention_in_grad: float32 [3, 768, 768], P(None, ('dp', 'expert'), 'tensor')
- attention_out_grad: float32 [768, 768], P('tensor', ('dp', 'expert'))
- second_gain_grad: float32 [768], P(('dp', 'expert'))
- second_bias_grad: float32 [768], P(('dp', 'expert'))
- router_grad: float32 [768, 4], P(('dp', 'expert'))
- expert_in_grad: float32 [4, 768, 3072], P('expert', 'dp', 'tensor')
- expert_out_grad: float32 [4, 3072, 768], P('expert', 'tensor', 'dp')
The draws below stay inside these ranges and needn't reach their ends.
Inputs may be any that keep to these rules, and one draw needn't show every extreme that they name: `expert_ids`: the two experts of a token differ. `slot_index`: among the 197 tokens of one index of dp and expert, the choices naming one expert hold slots 0, 1, 2 and so on, all first choices before all second choices, rows in order within each; a choice ranked 98 or later holds 98 and is dropped. Some expert fills all 98 slots from every index of dp and expert.
All inputs are finite; a program needn't handle non-finite values.
Results may differ from the reference program's by a relative error of at most 0.02.
Values may be sent and summed in bfloat16 or wider, within the bound.
A program may use at most 128 MiB of HBM per device.

```python
import math
import jax
import jax.numpy as jnp
from jax import lax

D = 768
HEADS = 12
HEAD_DIM = 64
FF = 3072
SEQ = 197
IMG_DEV = 1
ROWS = 197
TOKENS = 1576
EXPERTS = 4
CAP = 98


def routing_draw(key):
    base = jax.random.fold_in(key, 11)
    key_order, key_heavy, key_first, key_second = jax.random.split(base, 4)
    order = jax.random.permutation(key_order, EXPERTS).astype(jnp.int32)
    heavy = jax.random.randint(key_heavy, (TOKENS,), 0, 4)
    first = jnp.where(heavy == 0, 0, jax.random.randint(key_first, (TOKENS,), 1, EXPERTS))
    second = (first + jax.random.randint(key_second, (TOKENS,), 1, EXPERTS)) % EXPERTS
    chosen = order[jnp.stack([first, second], axis=1)].astype(jnp.int32)
    blocks = TOKENS // ROWS
    ordered = jnp.concatenate([chosen[:, 0].reshape(blocks, ROWS), chosen[:, 1].reshape(blocks, ROWS)], axis=1)
    onehot = (ordered[:, :, None] == jnp.arange(EXPERTS, dtype=jnp.int32)).astype(jnp.int32)
    ranks = jnp.sum(jnp.cumsum(onehot, axis=1) * onehot, axis=2) - 1
    ranks = jnp.minimum(ranks, CAP)
    slots = jnp.stack([ranks[:, :ROWS].reshape(TOKENS), ranks[:, ROWS:].reshape(TOKENS)], axis=1)
    return (chosen, slots.astype(jnp.int32))


def draw_expert_ids(key, part):
    chosen, slots = routing_draw(key)
    return chosen


def draw_slot_index(key, part):
    chosen, slots = routing_draw(key)
    return slots


def draw_attention_in(key, part):
    width = HEADS * HEAD_DIM
    key_base = jax.random.fold_in(key, 3)
    base = jax.random.normal(key_base, (3, D, width), jnp.float32) / math.sqrt(D)
    return base.astype(jnp.bfloat16)


def draw_router_weight(key, part):
    key_base = jax.random.fold_in(jax.random.fold_in(key, 5), 0)
    return jax.random.normal(key_base, (D, EXPERTS), jnp.float32) * (1.5 / math.sqrt(D))


def block_levels(rng, dims, pieces, least, largest):
    level, own = 1.0, jax.random.fold_in(rng, 6)
    for position, parts in pieces:
        steps = jnp.exp(jax.random.uniform(jax.random.fold_in(own, position), (parts,), jnp.float32, least / len(pieces), largest / len(pieces)))
        level = level * jnp.repeat(steps, dims[position] // parts).reshape([-1 if axis == position else 1 for axis in range(len(dims))])
    return level


def noise(rng, extent, scale, most, pieces=(), kind=jnp.bfloat16):
    level = block_levels(rng, extent, pieces, -0.22, 0.18) if pieces else 1.0
    array = jax.random.normal(rng, extent, jnp.float32) * scale * level
    return jnp.minimum(jnp.maximum(array, -most), most).astype(kind)


def setup_inputs(seed: int = 0) -> dict:
    seeds = jax.random.split(jax.random.key(seed), 14)
    return {
        "inputs": noise(seeds[0], (TOKENS, D), 1.0, 6.0, ((0, 8),)),
        "first_gain": jnp.clip(1.0 + 0.1 * jax.random.normal(seeds[1], (D,), jnp.float32), 0.5, 1.5),
        "first_bias": noise(seeds[2], (D,), 0.3, 2.0, (), jnp.float32),
        "attention_in": draw_attention_in(jax.random.fold_in(seeds[13], 71), 0),
        "attention_out": noise(seeds[4], (HEADS * HEAD_DIM, D), (HEADS * HEAD_DIM // 16) ** -0.5, 0.875, ((0, 4),)),
        "second_gain": jnp.clip(1.0 + 0.1 * jax.random.normal(seeds[5], (D,), jnp.float32), 0.5, 1.5),
        "second_bias": noise(seeds[6], (D,), 0.3, 2.0, (), jnp.float32),
        "router_weight": draw_router_weight(jax.random.fold_in(seeds[13], 71), 0),
        "expert_in": noise(seeds[8], (EXPERTS, D, FF), D ** -0.5, 0.21875, ((0, 2), (2, 4))),
        "expert_out": noise(seeds[9], (EXPERTS, FF, D), (max(1, FF // 256)) ** -0.5, 1.75, ((0, 2), (1, 4))),
        "expert_ids": draw_expert_ids(jax.random.fold_in(seeds[13], 71), 0),
        "slot_index": draw_slot_index(jax.random.fold_in(seeds[13], 71), 0),
        "cotangent": noise(seeds[12], (TOKENS, D), 1.0, 6.0, ((0, 8),)),
    }


EPS = 1e-06
GELU_C = math.sqrt(2.0 / math.pi)

def normalize(values):
    centre = lax.optimization_barrier(jnp.mean(values, axis=-1, keepdims=True))
    centred = values - centre
    spread = lax.optimization_barrier(jnp.mean(centred * centred, axis=-1, keepdims=True))
    scale = lax.rsqrt(spread + EPS)
    return (centred * scale, scale)

def norm_back(grad_out, normed, scale, gain):
    scaled = grad_out * gain
    first_mean = lax.optimization_barrier(jnp.mean(scaled, axis=-1, keepdims=True))
    second_mean = lax.optimization_barrier(jnp.mean(scaled * normed, axis=-1, keepdims=True))
    return scale * (scaled - first_mean - normed * second_mean)

def gelu_parts(pre):
    inner = GELU_C * (pre + 0.044715 * pre * pre * pre)
    tangent = jnp.tanh(inner)
    value = 0.5 * pre * (1.0 + tangent)
    slope = 0.5 * (1.0 + tangent) + 0.5 * pre * (1.0 - tangent * tangent) * GELU_C * (1.0 + 3.0 * 0.044715 * pre * pre)
    return (value, slope)

def reference(inputs, first_gain, first_bias, attention_in, attention_out, second_gain, second_bias, router_weight, expert_in, expert_out, expert_ids, slot_index, cotangent):
    fl = jnp.float32
    bf = jnp.bfloat16
    tokens = inputs.shape[0]
    sources = tokens // ROWS
    width = HEADS * HEAD_DIM
    scaling = HEAD_DIM ** (-0.5)
    x_full = inputs.astype(fl)
    normed1, scale1 = normalize(x_full)
    first = (normed1 * first_gain + first_bias).astype(bf)
    project = [jnp.dot(first, attention_in[which], preferred_element_type=fl).astype(bf) for which in range(3)]

    def blocked(matrix):
        return matrix.reshape(sources, IMG_DEV, SEQ, HEADS, HEAD_DIM)

    def attend(block):
        query, keys, values = [part.astype(fl) for part in block]
        scores = jnp.einsum('iqhd,ikhd->ihqk', query, keys) * scaling
        peak = lax.optimization_barrier(jnp.max(scores, axis=-1, keepdims=True))
        logsum = peak[..., 0] + jnp.log(lax.optimization_barrier(jnp.sum(jnp.exp(scores - peak), axis=-1)))
        probs = jnp.exp(scores - logsum[..., None])
        weights = probs.astype(bf).astype(fl)
        context = jnp.einsum('ihqk,ikhd->iqhd', weights, values).astype(bf)
        return (context, logsum)
    context_b, logsums = lax.map(attend, (blocked(project[0]), blocked(project[1]), blocked(project[2])))
    context = context_b.reshape(tokens, width)
    attended = jnp.dot(context, attention_out, preferred_element_type=fl)
    resid = x_full + attended
    normed2, scale2 = normalize(resid)
    second = (normed2 * second_gain + second_bias).astype(bf)
    logits = jnp.dot(second.astype(fl), router_weight, precision=lax.Precision.HIGHEST)
    route = jax.nn.softmax(logits, axis=-1)
    valid = (slot_index < CAP).astype(fl)
    gate = jnp.take_along_axis(route, expert_ids, axis=1) * valid
    source = jnp.broadcast_to((jnp.arange(tokens, dtype=jnp.int32) // ROWS)[:, None], (tokens, 2))

    def to_slots(rows_both):
        holder = jnp.zeros((EXPERTS, sources, CAP + 1, D), bf)
        holder = holder.at[expert_ids, source, slot_index].set(rows_both)
        return holder[:, :, :CAP].reshape(EXPERTS, sources * CAP, D)

    def from_slots(slotted):
        padded = jnp.concatenate([slotted.reshape(EXPERTS, sources, CAP, D), jnp.zeros((EXPERTS, sources, 1, D), bf)], axis=2)
        return padded[expert_ids, source, slot_index].astype(fl)
    buffer = to_slots(jnp.broadcast_to(second[:, None, :], (tokens, 2, D)))

    def expert_forward(item):
        rows_e, weight_a, weight_b = item
        pre = jnp.dot(rows_e, weight_a, preferred_element_type=fl)
        value, unused = gelu_parts(pre)
        return jnp.dot(value.astype(bf), weight_b, preferred_element_type=fl).astype(bf)
    outputs = lax.map(expert_forward, (buffer, expert_in, expert_out))
    picked = from_slots(outputs)
    layer_out = resid + lax.optimization_barrier(jnp.sum(gate[..., None] * picked, axis=1))
    grad_out = cotangent.astype(fl)
    gate_grad = lax.optimization_barrier(jnp.sum(grad_out[:, None, :] * picked, axis=-1)) * valid
    y_grad = (gate[..., None] * grad_out[:, None, :]).astype(bf)
    grad_buffer = to_slots(y_grad)

    def expert_backward(item):
        rows_e, grads_e, weight_a, weight_b = item
        pre = jnp.dot(rows_e, weight_a, preferred_element_type=fl)
        value, slope = gelu_parts(pre)
        hidden = value.astype(bf)
        hidden_grad = jnp.dot(grads_e, weight_b.T, preferred_element_type=fl)
        pre_grad = (hidden_grad * slope).astype(bf)
        grad_b = jnp.dot(hidden.T, grads_e, preferred_element_type=fl)
        grad_a = jnp.dot(rows_e.T, pre_grad, preferred_element_type=fl)
        back = jnp.dot(pre_grad, weight_a.T, preferred_element_type=fl).astype(bf)
        return (grad_a, grad_b, back)
    expert_in_grad, expert_out_grad, back_buffer = lax.map(expert_backward, (buffer, grad_buffer, expert_in, expert_out))
    back_rows = lax.optimization_barrier(jnp.sum(from_slots(back_buffer), axis=1))
    choose = (expert_ids[:, :, None] == jnp.arange(EXPERTS, dtype=jnp.int32)).astype(fl)
    route_grad = lax.optimization_barrier(jnp.sum(gate_grad[:, :, None] * choose, axis=1))
    logit_grad = route * (route_grad - lax.optimization_barrier(jnp.sum(route * route_grad, axis=-1, keepdims=True)))
    router_grad = jnp.dot(second.astype(fl).T, logit_grad, precision=lax.Precision.HIGHEST)
    second_grad = back_rows + jnp.dot(logit_grad, router_weight.T, precision=lax.Precision.HIGHEST)
    second_gain_grad = lax.optimization_barrier(jnp.sum(second_grad * normed2, axis=0))
    second_bias_grad = lax.optimization_barrier(jnp.sum(second_grad, axis=0))
    resid_grad = grad_out + norm_back(second_grad, normed2, scale2, second_gain)
    resid_low = resid_grad.astype(bf)
    attention_out_grad = jnp.dot(context.T, resid_low, preferred_element_type=fl)
    context_grad = jnp.dot(resid_low, attention_out.T, preferred_element_type=fl).astype(bf)

    def attend_back(block):
        query, keys, values, context_h, context_g, logsum = block
        query, keys, values, context_h, context_g = [part.astype(fl) for part in (query, keys, values, context_h, context_g)]
        scores = jnp.einsum('iqhd,ikhd->ihqk', query, keys) * scaling
        probs = jnp.exp(scores - logsum[..., None])
        weights = probs.astype(bf).astype(fl)
        values_grad = jnp.einsum('ihqk,iqhd->ikhd', weights, context_g).astype(bf)
        probs_grad = jnp.einsum('iqhd,ikhd->ihqk', context_g, values)
        delta = jnp.transpose(lax.optimization_barrier(jnp.sum(context_g * context_h, axis=-1)), (0, 2, 1))
        score_grad = (probs * (probs_grad - delta[..., None]) * scaling).astype(bf).astype(fl)
        query_grad = jnp.einsum('ihqk,ikhd->iqhd', score_grad, keys).astype(bf)
        keys_grad = jnp.einsum('ihqk,iqhd->ikhd', score_grad, query).astype(bf)
        return (query_grad, keys_grad, values_grad)
    grads_qkv = lax.map(attend_back, (blocked(project[0]), blocked(project[1]), blocked(project[2]), context_b, blocked(context_grad), logsums))
    grads_flat = [part.reshape(tokens, width) for part in grads_qkv]
    attention_in_grad = jnp.stack([jnp.dot(first.T, part, preferred_element_type=fl) for part in grads_flat])
    first_grad = jnp.dot(grads_flat[0], attention_in[0].T, preferred_element_type=fl)
    first_grad = first_grad + jnp.dot(grads_flat[1], attention_in[1].T, preferred_element_type=fl)
    first_grad = first_grad + jnp.dot(grads_flat[2], attention_in[2].T, preferred_element_type=fl)
    first_gain_grad = lax.optimization_barrier(jnp.sum(first_grad * normed1, axis=0))
    first_bias_grad = lax.optimization_barrier(jnp.sum(first_grad, axis=0))
    input_grad = resid_grad + norm_back(first_grad, normed1, scale1, first_gain)
    return (layer_out, input_grad, first_gain_grad, first_bias_grad, attention_in_grad, attention_out_grad, second_gain_grad, second_bias_grad, router_grad, expert_in_grad, expert_out_grad)
```

```python
import functools
import math

import jax
import jax.numpy as jnp
from jax import lax
from jax.experimental import pallas as pl
from jax.experimental.pallas import tpu as pltpu
from jax.sharding import PartitionSpec as P

HEAD_DIM = 64
SEQ = 197


EPS = 1e-06
GELU_C = math.sqrt(2.0 / math.pi)


def cut_along(shard, dim, devices):
    shape = shard.shape
    tiles = shard.reshape(*shape[:dim], devices, shape[dim] // devices, *shape[dim + 1 :])
    return jnp.moveaxis(tiles, dim, 0)


def sent_and_summed(shard, axis, dim):
    devices = lax.axis_size(axis)
    tiles = lax.all_to_all(cut_along(shard, dim, devices), axis, 0, 0, tiled=True)
    return jnp.sum(tiles.astype(jnp.float32), axis=0)


def sent_together(arrays, axis, dim, along):
    widths = [math.prod(a.shape[along:]) for a in arrays]
    both = jnp.concatenate(
        [a.reshape(*a.shape[:along], w) for a, w in zip(arrays, widths)], axis=along
    )
    out = sent_and_summed(both, axis, dim)
    tiles = jnp.split(out, [sum(widths[:k]) for k in range(1, len(widths))], axis=along)
    return tuple((b.reshape(*out.shape[:along], *a.shape[along:]) for a, b in zip(arrays, tiles)))


def normalize(values):
    centre = jnp.mean(values, axis=-1, keepdims=True)
    centred = values - centre
    spread = jnp.mean(centred * centred, axis=-1, keepdims=True)
    scale = lax.rsqrt(spread + EPS)
    return (centred * scale, scale)


def norm_back(grad_out, normed, scale, gain):
    scaled = grad_out * gain
    first_mean = jnp.mean(scaled, axis=-1, keepdims=True)
    second_mean = jnp.mean(scaled * normed, axis=-1, keepdims=True)
    return scale * (scaled - first_mean - normed * second_mean)


def gelu_parts(pre):
    inner = GELU_C * (pre + 0.044715 * pre * pre * pre)
    tangent = jnp.tanh(inner)
    value = 0.5 * pre * (1.0 + tangent)
    slope = 0.5 * (1.0 + tangent) + 0.5 * pre * (1.0 - tangent * tangent) * GELU_C * (
        1.0 + 3.0 * 0.044715 * pre * pre
    )
    return (value, slope)


MESH = pl.DeviceIdType.MESH


def greet(axes):
    barrier = pltpu.get_barrier_semaphore()
    peers = 0
    for axis in axes:
        devices = lax.axis_size(axis)
        me = lax.axis_index(axis)
        for k in range(1, devices):
            peer = lax.rem(me + k, devices)
            pl.semaphore_signal(barrier, inc=1, device_id={axis: peer}, device_id_type=MESH)
            peers += 1
    pl.semaphore_wait(barrier, peers)


def group_peer(k):
    owners = lax.axis_size("expert")
    members = lax.axis_size("dp") * owners
    me = lax.axis_index("dp") * owners + lax.axis_index("expert")
    peer = lax.rem(me + k, members)
    return {"dp": peer // owners, "expert": lax.rem(peer, owners)}


def greet_line_and_group(grouped):
    barrier = pltpu.get_barrier_semaphore()
    cuts = lax.axis_size("tensor")
    members = lax.axis_size("dp") * lax.axis_size("expert") if grouped else 1
    for k in range(1, cuts):
        peer = {"tensor": lax.rem(lax.axis_index("tensor") + k, cuts)}
        pl.semaphore_signal(barrier, inc=1, device_id=peer, device_id_type=MESH)
    for k in range(1, members):
        pl.semaphore_signal(barrier, inc=1, device_id=group_peer(k), device_id_type=MESH)
    pl.semaphore_wait(barrier, cuts + members - 2)


def group_copies(source, target, send_sem, recv_sem):
    owners = lax.axis_size("expert")
    members = lax.axis_size("dp") * owners
    me = lax.axis_index("dp") * owners + lax.axis_index("expert")
    copies = []
    for k in range(1, members):
        copy = pltpu.make_async_remote_copy(
            src_ref=source.at[lax.rem(me + k, members)],
            dst_ref=target.at[k],
            send_sem=send_sem.at[k],
            recv_sem=recv_sem.at[k],
            device_id=group_peer(k),
            device_id_type=MESH,
        )
        copy.start()
        copies.append(copy)
    target[0] = source[me]
    return copies


def ends_kernel(gather, *refs):
    source, group_source, target, group_target = refs[:4]
    send_sem, recv_sem, send_group, recv_group = refs[4:]
    devices = lax.axis_size("tensor")
    me = lax.axis_index("tensor")
    greet_line_and_group(True)
    copies = []
    for k in range(1, devices):
        peer = lax.rem(me + k, devices)
        copy = pltpu.make_async_remote_copy(
            src_ref=source if gather else source.at[peer],
            dst_ref=target.at[me] if gather else target.at[k],
            send_sem=send_sem.at[k],
            recv_sem=recv_sem.at[k],
            device_id={"tensor": peer},
            device_id_type=MESH,
        )
        copy.start()
        copies.append(copy)
    copies += group_copies(group_source, group_target, send_group, recv_group)
    if gather:
        target[me] = source[...]
    else:
        target[0] = source[me]
    for copy in copies:
        copy.wait()


def line_and_group(array, group_array, collective_id, gather):
    devices = lax.axis_size("tensor")
    members = group_array.shape[0]
    shape = (devices, *array.shape) if gather else array.shape
    return pl.pallas_call(
        functools.partial(ends_kernel, gather),
        out_shape=[
            jax.ShapeDtypeStruct(shape, array.dtype),
            jax.ShapeDtypeStruct(group_array.shape, group_array.dtype),
        ],
        in_specs=[pl.BlockSpec(memory_space=pltpu.VMEM)] * 2,
        out_specs=[pl.BlockSpec(memory_space=pltpu.VMEM)] * 2,
        scratch_shapes=[pltpu.SemaphoreType.DMA((n,)) for n in (devices, devices, members, members)],
        compiler_params=pltpu.CompilerParams(collective_id=collective_id, has_side_effects=True),
        name=f"ends{collective_id}",
    )(array, group_array)


def scatter_kernel(count, *refs):
    sources, targets = refs[:count], refs[count : 2 * count]
    send_sem, recv_sem = refs[2 * count :]
    devices = lax.axis_size("tensor")
    me = lax.axis_index("tensor")
    greet(("tensor",))
    copies = []
    for k in range(1, devices):
        peer = lax.rem(me + k, devices)
        for a in range(count):
            copy = pltpu.make_async_remote_copy(
                src_ref=sources[a].at[peer],
                dst_ref=targets[a].at[k],
                send_sem=send_sem.at[a, k],
                recv_sem=recv_sem.at[a, k],
                device_id={"tensor": peer},
                device_id_type=MESH,
            )
            copy.start()
            copies.append(copy)
    for a in range(count):
        targets[a][0] = sources[a][me]
    for copy in copies:
        copy.wait()


def scattered(arrays, collective_id):
    devices = lax.axis_size("tensor")
    count = len(arrays)
    return pl.pallas_call(
        functools.partial(scatter_kernel, count),
        out_shape=[jax.ShapeDtypeStruct(a.shape, a.dtype) for a in arrays],
        in_specs=[pl.BlockSpec(memory_space=pltpu.VMEM)] * count,
        out_specs=[pl.BlockSpec(memory_space=pltpu.VMEM)] * count,
        scratch_shapes=[
            pltpu.SemaphoreType.DMA((count, devices)),
            pltpu.SemaphoreType.DMA((count, devices)),
        ],
        compiler_params=pltpu.CompilerParams(collective_id=collective_id, has_side_effects=True),
        name=f"scatter{collective_id}",
    )(*arrays)


def gather_kernel(count, forward, *refs):
    sources, targets = refs[:count], refs[count : 2 * count]
    send_z, recv_z, send_x, recv_x = refs[2 * count :]
    devices = lax.axis_size("tensor")
    me = lax.axis_index("tensor")
    owners = lax.axis_size("expert") if forward else 1
    home = lax.axis_index("expert")
    greet(("tensor", "expert") if forward else ("tensor",))

    def across(a, k, source, place):
        copies = []
        for e in range(1, owners):
            copy = pltpu.make_async_remote_copy(
                src_ref=source,
                dst_ref=targets[a].at[e, place],
                send_sem=send_x.at[a, k, e],
                recv_sem=recv_x.at[a, k, e],
                device_id={"expert": lax.rem(home + e, owners)},
                device_id_type=MESH,
            )
            copy.start()
            copies.append(copy)
        return copies

    along = []
    for k in range(1, devices):
        peer = lax.rem(me + k, devices)
        for a in range(count):
            copy = pltpu.make_async_remote_copy(
                src_ref=sources[a],
                dst_ref=targets[a].at[0, me],
                send_sem=send_z.at[a, k],
                recv_sem=recv_z.at[a, k],
                device_id={"tensor": peer},
                device_id_type=MESH,
            )
            copy.start()
            along.append((a, k, copy))
    crossing = []
    for a in range(count):
        crossing += across(a, 0, sources[a], me)
    for a in range(count):
        targets[a][0, me] = sources[a][...]
    for a, k, copy in along:
        copy.wait()
        place = lax.rem(me + devices - k, devices)
        crossing += across(a, k, targets[a].at[0, place], place)
    for copy in crossing:
        copy.wait()


def gathered(arrays, collective_id, forward=False):
    devices = lax.axis_size("tensor")
    owners = lax.axis_size("expert") if forward else 1
    count = len(arrays)
    sems = [(count, devices)] * 2 + [(count, devices, owners)] * 2
    return pl.pallas_call(
        functools.partial(gather_kernel, count, forward),
        out_shape=[
            jax.ShapeDtypeStruct((owners, devices, *a.shape), a.dtype) for a in arrays
        ],
        in_specs=[pl.BlockSpec(memory_space=pltpu.VMEM)] * count,
        out_specs=[pl.BlockSpec(memory_space=pltpu.VMEM)] * count,
        scratch_shapes=[pltpu.SemaphoreType.DMA(s) for s in sems],
        compiler_params=pltpu.CompilerParams(collective_id=collective_id, has_side_effects=True),
        name=f"gather{collective_id}",
    )(*arrays)


def shifted(array, axis, offset):
    devices = lax.axis_size(axis)
    return lax.ppermute(array, axis, [(d, (d + offset) % devices) for d in range(devices)])


def from_owners(array):
    owners = lax.axis_size("expert")
    return jnp.stack([array] + [shifted(array, "expert", e) for e in range(1, owners)])


def to_owners(array):
    owners = lax.axis_size("expert")
    total = array[0].astype(jnp.float32)
    for e in range(1, owners):
        total = total + shifted(array[e], "expert", owners - e).astype(jnp.float32)
    return total


def rounded_up(value, multiple):
    return -(-value // multiple) * multiple


def experts_kernel(
    experts_all,
    slot_ref,
    spot_ref,
    second_ref,
    cot_ref,
    router_ref,
    in_ref,
    out_ref,
    mixed_ref,
    back_ref,
    share_ref,
    route_ref,
    cut_ref,
    placing_ref,
    gated_ref,
    low_ref,
    grad_ref,
):
    bf16, f32 = jnp.bfloat16, jnp.float32
    exact = lax.Precision.HIGHEST
    owners, padded, _ = second_ref.shape
    experts_here = in_ref.shape[0]
    lanes = router_ref.shape[1]
    depth = placing_ref.shape[2]

    def dot(a, b, a_dim, b_dim, precision=None):
        return lax.dot_general(
            a, b, (((a_dim,), (b_dim,)), ((), ())), precision=precision, preferred_element_type=f32
        )

    column = lax.broadcasted_iota(jnp.int32, (padded, lanes), 1)
    for o in range(owners):
        logits = dot(second_ref[o].astype(f32), router_ref[...], 1, 0, exact)
        logits = jnp.where(column < experts_all, logits, -1e30)
        lifted = jnp.exp(logits - jnp.max(logits, axis=-1, keepdims=True))
        lifted = jnp.where(column < experts_all, lifted, 0.0)
        route_ref[o] = lifted / jnp.sum(lifted, axis=-1, keepdims=True)
    slot = lax.broadcasted_iota(jnp.int32, (depth, padded), 0)
    for k in range(experts_here):
        gates, received, slotted = [], [], []
        for o in range(owners):
            picks = slot == slot_ref[k, o][None, :]
            placing = jnp.where(picks, 1.0, 0.0)
            low = placing.astype(bf16)
            placing_ref[k, o] = low
            chances = dot(placing, route_ref[o], 1, 0, exact)
            gates.append(jnp.sum(chances * spot_ref[k][None, :], axis=-1, keepdims=True))
            received.append(dot(low, second_ref[o], 1, 0).astype(bf16))
            slotted.append(dot(low, cot_ref[o], 1, 0))
        gate = jnp.concatenate(gates)
        received = jnp.concatenate(received)
        slotted = jnp.concatenate(slotted)
        y_grad = (gate * slotted).astype(bf16)
        value, slope = gelu_parts(dot(received, in_ref[k], 1, 0))
        hidden = value.astype(bf16)
        partial_y = dot(hidden, out_ref[k], 1, 0)
        gated_ref[k] = (gate * partial_y).astype(bf16)
        slot_grad = jnp.sum(slotted * partial_y, axis=-1, keepdims=True)
        grad_ref[k] = slot_grad * spot_ref[k][None, :]
        pre_grad = (dot(y_grad, out_ref[k], 1, 1) * slope).astype(bf16)
        low_ref[k] = dot(pre_grad, in_ref[k], 1, 1).astype(bf16)
        in_grad = dot(received, pre_grad, 0, 0).astype(bf16)
        out_grad = dot(y_grad, hidden, 0, 0).astype(bf16)
        blocks, _, _, share, _ = cut_ref.shape
        for d in range(blocks):
            cut_ref[d, 0, k] = in_grad[d * share : (d + 1) * share]
            cut_ref[d, 1, k] = out_grad[d * share : (d + 1) * share]
    for o in range(owners):
        span = pl.ds(o * depth, depth)
        here = range(experts_here)
        mixed_ref[o] = sum(
            dot(placing_ref[k, o], gated_ref[k, span], 0, 0) for k in here
        ).astype(bf16)
        back_ref[o] = sum(dot(placing_ref[k, o], low_ref[k, span], 0, 0) for k in here).astype(bf16)
        share_ref[o] = sum(
            dot(placing_ref[k, o].astype(f32), grad_ref[k, span], 0, 0, exact) for k in here
        )


def experts_block(slots, spot, second, cot, router, expert_in, expert_out, experts_all, depth):
    owners, padded, width = second.shape
    here, _, hidden = expert_in.shape
    lanes = router.shape[1]
    blocks = lax.axis_size("dp")
    bf16, f32 = jnp.bfloat16, jnp.float32
    shapes = [
        ((owners, padded, width), bf16),
        ((owners, padded, width), bf16),
        ((owners, padded, lanes), f32),
        ((owners, padded, lanes), f32),
        ((blocks, 2, here, width // blocks, hidden), bf16),
    ]
    return pl.pallas_call(
        functools.partial(experts_kernel, experts_all),
        out_shape=[jax.ShapeDtypeStruct(*s) for s in shapes],
        in_specs=[pl.BlockSpec(memory_space=pltpu.VMEM)] * 7,
        out_specs=[pl.BlockSpec(memory_space=pltpu.VMEM)] * 5,
        scratch_shapes=[
            pltpu.VMEM((here, owners, depth, padded), bf16),
            pltpu.VMEM((here, owners * depth, width), bf16),
            pltpu.VMEM((here, owners * depth, width), bf16),
            pltpu.VMEM((here, owners * depth, lanes), f32),
        ],
        compiler_params=pltpu.CompilerParams(
            vmem_limit_bytes=(32 << 20) if owners <= 2 else (60 << 20)
        ),
        name="experts",
    )(slots, spot, second, cot, router, expert_in, expert_out)


def lane_dot(a, b, a_dim, b_dim, precision=None):
    return lax.dot_general(
        a, b, (((a_dim,), (b_dim,)), ((), ())), precision=precision, preferred_element_type=jnp.float32
    )


def block_kernel(dims, *refs):
    tokens, rows, cuts, experts_all, capacity, depth = dims
    bf16, f32 = jnp.bfloat16, jnp.float32
    exact = lax.Precision.HIGHEST
    given = refs[:9]
    (w_hbm, wo_hbm, ein_hbm, eout_hbm) = refs[9:13]
    (finals, e_own, e_peer, g_parts, small_parts) = refs[13:18]
    (
        x_in, cot_in, gain1, bias1, gain2, bias2, router_in, ids_in, slot_in, x32, c32,
        xs, cots, tgt, rt, w_in, wo, ctx, ein, eout, sec, resid, first, n1,
        qkv, probs, back_out, back_in, back_home, back_send, back_got,
        mix_out, mix_in, mix_home, mix_send, mix_got,
        ends, small_sum, share_out, share_in, share_all, low, lg, ebuf, e_got, gbuf, g_got, first_send, first_got,
        small, small_send, small_got, lowers, hid, pgr, rec, ygr, plc, gated,
        load, ss, rs,
    ) = refs[18:]
    d, e, z = lax.axis_index("dp"), lax.axis_index("expert"), lax.axis_index("tensor")
    core, y = lax.rem(d, 2), d // 2
    padded = rows * cuts
    width = x_in.shape[1]
    wide = lambda vector: vector[...][None, :]
    local = wo_hbm.shape[0]
    heads = local // HEAD_DIM
    half = local // 2
    here = ein_hbm.shape[0]
    ctx_rows = ctx.shape[2]
    other_x = {"expert": 1 - e}
    other_core = {"dp": y * 2 + 1 - core}
    other_y = {"dp": (1 - y) * 2 + core}
    diagonal = {"dp": (1 - y) * 2 + core, "expert": 1 - e}
    along = [(k, lax.rem(z + k, cuts)) for k in range(1, cuts)]
    count = [0]
    pending = []

    def send(source, target, device):
        i = count[0]
        count[0] += 1
        copy = pltpu.make_async_remote_copy(
            src_ref=source,
            dst_ref=target,
            send_sem=ss.at[i],
            recv_sem=rs.at[i],
            device_id=device,
            device_id_type=MESH,
        )
        copy.start()
        pending.append(copy)
        return copy

    loads = [
        pltpu.make_async_copy(w_hbm, w_in, load.at[0]),
        pltpu.make_async_copy(wo_hbm.at[pl.ds(0, half)], wo.at[z, 0], load.at[1]),
        pltpu.make_async_copy(wo_hbm.at[pl.ds(half, half)], wo.at[z, 1], load.at[2]),
        pltpu.make_async_copy(ein_hbm, ein, load.at[3]),
        pltpu.make_async_copy(eout_hbm, eout, load.at[4]),
    ]
    here_now = (x_in, cot_in, gain1, bias1, gain2, bias2, router_in, ids_in, slot_in)
    early = [
        pltpu.make_async_copy(source, target, load.at[5 + i])
        for i, (source, target) in enumerate(zip(given, here_now))
    ]
    for copy in early + loads:
        copy.start()
    barrier = pltpu.get_barrier_semaphore()
    others = [
        {"dp": (y if same_y else 1 - y) * 2 + (core if same_core else 1 - core),
         "expert": e if same_e else 1 - e}
        for same_y in (1, 0) for same_core in (1, 0) for same_e in (1, 0)
    ][1:]
    greeted = others + [{"tensor": p} for _, p in along]
    for peer in greeted:
        pl.semaphore_signal(barrier, inc=1, device_id=peer, device_id_type=MESH)

    for copy in early:
        copy.wait()
    edge = tokens // 8 * 8
    for whole, part, low_whole in ((x32, x_in, xs), (c32, cot_in, cots)):
        whole[edge:padded] = jnp.zeros((padded - edge, width), f32)
        whole[0:tokens] = part[...].astype(f32)
        low_whole[0] = whole[...].astype(bf16)
    x_full = x32[...]
    tgt[0] = jnp.full(tgt.shape[1:], -1.0, f32)
    slot = slot_in[...]
    tgt[0, 0:2, 0:tokens] = jnp.where(slot < capacity, ids_in[...] * capacity + slot, -1).astype(f32)
    rt[...] = jnp.zeros_like(rt)
    rt[0:experts_all] = router_in[...]

    pl.semaphore_wait(barrier, len(greeted))
    loads[1].wait()
    loads[2].wait()
    wo_along = [
        (k, send(wo.at[z, core], wo.at[z, core], {"tensor": peer})) for k, peer in along
    ]
    x_copy = send(xs.at[0], xs.at[1], other_x)
    tgt_copy = send(tgt.at[0], tgt.at[1], other_x)
    cot_copy = send(cots.at[0], cots.at[1], other_x)

    normed, _ = normalize(x_full)
    n1[...] = normed
    first_low = (normed * wide(gain1) + wide(bias1)).astype(bf16)
    first[...] = first_low
    loads[0].wait()
    for which in range(3):
        qkv[which] = lane_dot(first_low[:ctx_rows], w_in[which], 1, 1).astype(bf16)
    head = lax.broadcasted_iota(jnp.int32, (ctx_rows, local), 1) // HEAD_DIM
    masks = [jnp.where(head == h, 1.0, 0.0) for h in range(heads)]
    key_at = lax.broadcasted_iota(jnp.int32, (ctx_rows, ctx_rows), 1)
    scaling = HEAD_DIM ** (-0.5)

    def of_head(matrix, h):
        return matrix * masks[h].astype(matrix.dtype)

    query, keys, values = qkv[0], qkv[1], qkv[2]
    total = jnp.zeros((ctx_rows, local), f32)
    for h in range(heads):
        scores = lane_dot(of_head(query, h), keys, 1, 1) * scaling
        scores = jnp.where(key_at < tokens, scores, -1e30)
        peak = jnp.max(scores, axis=-1, keepdims=True)
        logsum = peak + jnp.log(jnp.sum(jnp.exp(scores - peak), axis=-1, keepdims=True))
        chance = jnp.exp(scores - logsum)
        probs[h] = chance
        total += lane_dot(chance.astype(bf16), of_head(values, h), 1, 0)
    ctx[0, z] = total.astype(bf16)

    ctx_along = [(k, send(ctx.at[0, z], ctx.at[0, z], {"tensor": peer})) for k, peer in along]
    ctx_across = [(z, send(ctx.at[0, z], ctx.at[1, z], other_x))]

    wo_core = []
    for k, copy in wo_along:
        copy.wait_recv()
        place = lax.rem(z + cuts - k, cuts)
        wo_core.append(send(wo.at[place, core], wo.at[place, core], other_core))
    for k, copy in ctx_along:
        copy.wait_recv()
        place = lax.rem(z + cuts - k, cuts)
        ctx_across.append((place, send(ctx.at[0, place], ctx.at[1, place], other_x)))
    for copy in wo_core:
        copy.wait_recv()

    split = rt[...]
    splits = []
    for _ in range(3):
        piece = split.astype(bf16)
        splits.append(piece.astype(f32))
        split = split - piece.astype(f32)
    router_low = jnp.concatenate(splits).astype(bf16)
    lanes8 = rt.shape[0]
    expert_row = lax.broadcasted_iota(jnp.int32, (lanes8, padded), 0)
    base = e * here

    def forward(o):
        attended = jnp.zeros((ctx_rows, width), f32)
        for c in range(cuts):
            block = jnp.concatenate([wo[c, 0], wo[c, 1]])
            attended += lane_dot(ctx[o, c], block, 1, 0)
        attended = jnp.concatenate([attended, jnp.zeros((padded - ctx_rows, width), f32)])
        res = xs[o].astype(f32) + attended
        normed2, _ = normalize(res)
        second = (normed2 * wide(gain2) + wide(bias2)).astype(bf16)
        sec[o] = second
        parts = lane_dot(router_low, second, 1, 1)
        logits = parts[:lanes8] + parts[lanes8 : 2 * lanes8] + parts[2 * lanes8 :]
        logits = jnp.where(expert_row < experts_all, logits, -1e30)
        lifted = jnp.exp(logits - jnp.max(logits, axis=0, keepdims=True))
        lifted = jnp.where(expert_row < experts_all, lifted, 0.0)
        return res, lifted / jnp.sum(lifted, axis=0, keepdims=True)

    slot_at = lax.broadcasted_iota(jnp.int32, (depth, padded), 0)

    def picks_of(o, k):
        offset = tgt[o, 0:2, 0:padded].astype(jnp.int32) - (base + k) * capacity
        chosen = jnp.where((offset >= 0) & (offset < capacity), offset, -1)
        return slot_at == jnp.max(chosen, axis=0, keepdims=True)

    def place(o, route):
        placed, gates = [], []
        for k in range(here):
            picks = picks_of(o, k)
            placed.append(jnp.where(picks, 1.0, 0.0))
            row = jnp.sum(jnp.where(expert_row == base + k, route, 0.0), axis=0, keepdims=True)
            gates.append(jnp.sum(jnp.where(picks, row, 0.0), axis=-1, keepdims=True))
        low_place = jnp.concatenate(placed).astype(bf16)
        plc[o] = low_place
        gate = jnp.concatenate(gates)
        received = lane_dot(low_place, sec[o], 1, 0).astype(bf16)
        slotted = lane_dot(low_place, cots[o], 1, 0)
        return gate, received, slotted

    res, route_own = forward(0)
    resid[...] = res
    cot_copy.wait_recv()
    tgt_copy.wait_recv()
    x_copy.wait_recv()
    own = place(0, route_own)
    for _, copy in ctx_across:
        copy.wait_recv()
    _, route_far = forward(1)
    far = place(1, route_far)
    loads[3].wait()
    loads[4].wait()

    def joined(index, k):
        span = slice(k * depth, (k + 1) * depth)
        return jnp.concatenate([own[index][span], far[index][span]])

    shares = [jnp.zeros((lanes8, padded), f32) for _ in range(2)]
    for k in range(here):
        gate, received, slotted = joined(0, k), joined(1, k), joined(2, k)
        y_grad = (gate * slotted).astype(bf16)
        value, slope = gelu_parts(lane_dot(received, ein[k], 1, 0))
        hidden = value.astype(bf16)
        pre_grad = (lane_dot(y_grad, eout[k], 1, 1) * slope).astype(bf16)
        lowered = lane_dot(pre_grad, ein[k], 1, 1).astype(bf16)
        partial_y = lane_dot(hidden, eout[k], 1, 0)
        slot_grad = jnp.sum(slotted * partial_y, axis=-1, keepdims=True)
        weighted = (gate * partial_y).astype(bf16)
        rec[k], ygr[k], hid[k], pgr[k] = received, y_grad, hidden, pre_grad
        for o in range(2):
            span = slice(o * depth, (o + 1) * depth)
            lowers[o, k * depth : (k + 1) * depth] = lowered[span]
            gated[o, k * depth : (k + 1) * depth] = weighted[span]
            row = jnp.sum(
                jnp.where(picks_of(o, k), slot_grad[span], 0.0), axis=0, keepdims=True
            )
            shares[o] += jnp.where(expert_row == base + k, row, 0.0)

    def chunked(target, matrix):
        for c in range(cuts):
            target[c] = matrix[c * rows : (c + 1) * rows].astype(target.dtype)

    chunked(back_out, lane_dot(plc[1], lowers[1], 0, 0))
    order = [lax.rem(z + k, cuts) for k in (2, 1, 3, 0)]
    back_across = [send(back_out.at[c], back_in.at[c], other_x) for c in order]
    share_out[...] = jnp.zeros_like(share_out)
    share_out[:, 0:padded] = shares[1]
    share_across = send(share_out, share_in, other_x)
    chunked(back_home, lane_dot(plc[0], lowers[0], 0, 0))
    chunked(mix_out, lane_dot(plc[1], gated[1], 0, 0))
    chunked(mix_home, lane_dot(plc[0], gated[0], 0, 0))

    def expert_grads(k):
        in_grad = lane_dot(rec[k], pgr[k], 0, 0).astype(bf16)
        out_grad = lane_dot(ygr[k], hid[k], 0, 0).astype(bf16)
        share = width // 4
        for p in range(4):
            span = slice(p * share, (p + 1) * share)
            ebuf[p % 2, p // 2, 0, k] = in_grad[span]
            ebuf[p % 2, p // 2, 1, k] = out_grad[span]

    expert_grads(0)
    share_across.wait_recv()
    share_all[0] = share_in[...]
    share_all[0, :, 0:padded] += shares[0]
    share_along = [send(share_all.at[0], share_all.at[k], {"tensor": peer}) for k, peer in along]
    back_along = []
    for j, copy in enumerate(back_across):
        copy.wait_recv()
        c = order[j]
        back_send[c] = (back_home[c].astype(f32) + back_in[c].astype(f32)).astype(bf16)
        if j < 3:
            k = (2, 1, 3)[j]
            back_along.append(send(back_send.at[c], back_got.at[k], {"tensor": c}))
    mix_across = [send(mix_out.at[c], mix_in.at[c], other_x) for c in order]
    expert_grads(1)
    e_core = send(ebuf.at[1 - core], e_got, other_core)

    for copy in share_along:
        copy.wait_recv()
    route_grad = (share_all[0] + share_all[1] + share_all[2] + share_all[3])[:, 0:padded]
    logit_grad = route_own * (route_grad - jnp.sum(route_own * route_grad, axis=0, keepdims=True))
    chunked(lg, lane_dot(logit_grad, rt[...], 0, 0, exact))
    router_grad = lane_dot(logit_grad, sec[0].astype(f32), 1, 0, exact)
    res_rows = resid[pl.ds(pl.multiple_of(z * rows, 8), rows)]
    normed2, scale2 = normalize(res_rows)
    for copy in back_along:
        copy.wait_recv()
    back = back_send[z].astype(f32)
    for k, _ in along:
        back += back_got[k].astype(f32)
    second_grad = back + lg[z]
    cot_rows = c32[pl.ds(pl.multiple_of(z * rows, 8), rows)]
    resid_grad = cot_rows + norm_back(second_grad, normed2, scale2, wide(gain2))
    lg[z] = resid_grad
    low[z] = resid_grad.astype(bf16)
    low_along = [send(low.at[z], low.at[z], {"tensor": peer}) for _, peer in along]

    small[...] = jnp.zeros_like(small)
    small[0:experts_all] = jnp.where(z == 0, router_grad[:experts_all], 0.0)
    small[experts_all : experts_all + 1] = jnp.sum(second_grad * normed2, axis=0, keepdims=True)
    small[experts_all + 1 : experts_all + 2] = jnp.sum(second_grad, axis=0, keepdims=True)
    e_core.wait_recv()
    for yy in range(2):
        for a in range(2):
            for k in range(here):
                both = ebuf[core, yy, a, k].astype(f32) + e_got[yy, a, k].astype(f32)
                ebuf[core, yy, a, k] = both.astype(bf16)
    e_row = send(ebuf.at[core, 1 - y], e_peer, other_y)
    mix_along = []
    for j, copy in enumerate(mix_across):
        copy.wait_recv()
        c = order[j]
        mix_send[c] = (mix_home[c].astype(f32) + mix_in[c].astype(f32)).astype(bf16)
        if j < 3:
            k = (2, 1, 3)[j]
            mix_along.append(send(mix_send.at[c], mix_got.at[k], {"tensor": c}))

    for copy in low_along:
        copy.wait_recv()
    resid_low = jnp.concatenate([low[c].astype(f32) for c in range(cuts)]).astype(bf16)
    low_top = resid_low[:ctx_rows]
    wo_own = jnp.concatenate([wo[z, 0], wo[z, 1]])
    ctx_grad = lane_dot(low_top, wo_own, 1, 1).astype(bf16)
    ctx_own = ctx[0, z]
    product = ctx_grad.astype(f32) * ctx_own.astype(f32)
    query_grad = jnp.zeros((ctx_rows, local), f32)
    keys_grad = jnp.zeros((ctx_rows, local), f32)
    values_grad = jnp.zeros((ctx_rows, local), f32)
    query, keys, values = qkv[0], qkv[1], qkv[2]
    for h in range(heads):
        chance = probs[h]
        grad_h = of_head(ctx_grad, h)
        delta = jnp.sum(of_head(product, h), axis=-1, keepdims=True)
        values_grad += lane_dot(chance.astype(bf16), grad_h, 0, 0)
        score_grad = (chance * (lane_dot(grad_h, values, 1, 1) - delta) * scaling).astype(bf16)
        query_grad += lane_dot(score_grad, of_head(keys, h), 1, 0)
        keys_grad += lane_dot(score_grad, of_head(query, h), 0, 0)
    grads = [g.astype(bf16) for g in (query_grad, keys_grad, values_grad)]
    partial = sum(lane_dot(grads[k], w_in[k], 1, 0) for k in range(3))
    partial = jnp.concatenate([partial, jnp.zeros((padded - ctx_rows, width), f32)])
    chunked(first_send, partial)
    first_along = [
        send(first_send.at[peer], first_got.at[k], {"tensor": peer})
        for k, peer in [along[1], along[0], along[2]]
    ]
    small[experts_all + 2 : experts_all + 3] = jnp.sum(partial * n1[...], axis=0, keepdims=True)
    small[experts_all + 3 : experts_all + 4] = jnp.sum(partial, axis=0, keepdims=True)
    members = small_send.shape[0]
    cut = width // members
    for m in range(members):
        small_send[m, :, 0:cut] = small[:, m * cut : (m + 1) * cut]
    me = d * 2 + e
    small_across = [
        send(
            small_send.at[device["dp"] * 2 + device["expert"]], small_got.at[k], device
        )
        for k, device in enumerate(others)
    ]
    top = first[0:ctx_rows]
    results = [lane_dot(top, g, 0, 0).astype(bf16) for g in grads]
    results.append(lane_dot(low_top, ctx_own, 0, 0).astype(bf16))
    for m in range(members):
        for k in range(4):
            gbuf[(m // 2) % 2, (m // 4) * 2 + m % 2, :, k * local : (k + 1) * local] = results[k][
                m * cut : (m + 1) * cut
            ]
    g_core = send(gbuf.at[1 - core], g_got, other_core)

    for copy in mix_along:
        copy.wait_recv()
    mixed = mix_send[z].astype(f32)
    for k, _ in along:
        mixed += mix_got[k].astype(f32)
    ends[1] = (resid[pl.ds(pl.multiple_of(z * rows, 8), rows)] + mixed).astype(bf16)
    layer_along = [send(ends.at[1], finals.at[1, z], {"tensor": peer}) for _, peer in along]
    kept = []

    def keep(source, target):
        copy = pltpu.make_async_copy(source, target, load.at[14 + len(kept)])
        copy.start()
        kept.append(copy)

    keep(ends.at[1], finals.at[1, z])
    keep(ebuf.at[core, y], e_own)
    g_core.wait_recv()
    for m in range(members // 2):
        gbuf[core, m] = (gbuf[core, m].astype(f32) + g_got[m].astype(f32)).astype(bf16)
    mine = y * 2 + e
    g_across = [
        send(gbuf.at[core, place_], g_parts.at[k], device)
        for k, place_, device in [
            (1, y * 2 + 1 - e, other_x),
            (2, (1 - y) * 2 + e, other_y),
            (3, (1 - y) * 2 + 1 - e, diagonal),
        ]
    ]
    keep(gbuf.at[core, mine], g_parts.at[0])
    for copy in small_across:
        copy.wait_recv()
    added = small_send[me]
    for k in range(members - 1):
        added += small_got[k]
    small_sum[...] = added
    keep(small_sum, small_parts.at[0])
    small_along = [
        send(small_sum, small_parts.at[k], {"tensor": peer}) for k, peer in along
    ]

    normed_rows, scale_rows = normalize(x32[pl.ds(pl.multiple_of(z * rows, 8), rows)])
    for copy in first_along:
        copy.wait_recv()
    first_grad = first_send[z].astype(f32)
    for k, _ in along:
        first_grad += first_got[k].astype(f32)
    grad_rows = lg[z] + norm_back(first_grad, normed_rows, scale_rows, wide(gain1))
    ends[0] = grad_rows.astype(bf16)
    final_along = [send(ends.at[0], finals.at[0, z], {"tensor": peer}) for _, peer in along]
    keep(ends.at[0], finals.at[0, z])
    for copy in kept:
        copy.wait()
    for copy in layer_along + final_along + g_across + small_along + [e_row]:
        copy.wait_recv()
    for copy in pending:
        copy.wait_send()


def finish_kernel(dims, *refs):
    tokens, experts_all, local = dims
    f32 = jnp.float32
    given = refs[:5]
    layer_out, grad_out, gain1, bias1, att_in_out, att_out_out, gain2, bias2, router = refs[5:14]
    in_out, out_out = refs[14:16]
    finals, e_own, e_peer, g_parts, small_parts = held = refs[16:21]
    layer, grad, att_in, att_out, grad_in, grad_out_w = refs[21:27]
    load, store = refs[27:]
    cuts = finals.shape[1]
    cut = gain1.shape[1]
    loads = [
        pltpu.make_async_copy(given[i], held[i], load.at[i]) for i in range(5)
    ]
    for i in (1, 2, 3, 0, 4):
        loads[i].start()
    stores = []

    def keep(source, target):
        copy = pltpu.make_async_copy(source, target, store.at[len(stores)])
        copy.start()
        stores.append(copy)

    loads[1].wait()
    loads[2].wait()
    grad_in[...] = e_own[0].astype(f32) + e_peer[0].astype(f32)
    keep(grad_in, in_out)
    grad_out_w[...] = e_own[1].astype(f32) + e_peer[1].astype(f32)
    keep(grad_out_w, out_out)
    loads[3].wait()
    parts = sum(g_parts[k].astype(f32) for k in range(g_parts.shape[0]))
    for k in range(3):
        att_in[k] = parts[:, k * local : (k + 1) * local]
    keep(att_in, att_in_out)
    att_out[...] = parts[:, 3 * local :].T
    keep(att_out, att_out_out)
    loads[0].wait()
    for held_out, target, which in ((grad, grad_out, 0), (layer, layer_out, 1)):
        whole = jnp.concatenate([finals[which, c].astype(f32) for c in range(cuts)])
        held_out[...] = whole[:tokens]
        keep(held_out, target)
    loads[4].wait()
    totals = sum(small_parts[k] for k in range(cuts))[:, :cut]
    router[...] = totals[:experts_all]
    for i, target in enumerate((gain2, bias2, gain1, bias1)):
        target[...] = totals[experts_all + i : experts_all + i + 1]
    for copy in stores:
        copy.wait()


def per_device_general(
    inputs,
    first_gain,
    first_bias,
    attention_in,
    attention_out,
    second_gain,
    second_bias,
    router_weight,
    expert_in,
    expert_out,
    expert_ids,
    slot_index,
    cotangent,
):
    bf16, f32 = jnp.bfloat16, jnp.float32
    tokens_here = inputs.shape[0]
    model_width = inputs.shape[1]
    images = tokens_here // SEQ
    local_width = attention_in.shape[2]
    local_heads = local_width // HEAD_DIM
    owners = lax.axis_size("expert")
    cuts = lax.axis_size("tensor")
    experts_here = expert_in.shape[0]
    experts_all = experts_here * owners
    capacity = (2 * tokens_here - 1) // experts_all
    scaling = HEAD_DIM ** (-0.5)
    rows = rounded_up(rounded_up(tokens_here, cuts) // cuts, 8)
    padded = rows * cuts
    lanes = rounded_up(experts_all, 128)
    piece = lax.axis_index("tensor")

    def split_heads(matrix):
        return matrix.reshape(images, SEQ, local_heads, HEAD_DIM)

    def pad_rows(matrix, value=0):
        return jnp.pad(
            matrix, ((0, padded - tokens_here), (0, 0)), constant_values=value
        )

    def my_rows(matrix):
        return lax.dynamic_slice_in_dim(pad_rows(matrix), piece * rows, rows, 0)

    target = jnp.where(slot_index < capacity, expert_ids * capacity + slot_index, -1)
    target_all = from_owners(pad_rows(target, -1).astype(f32).T)
    cot_all = from_owners(pad_rows(cotangent))

    x_full = inputs.astype(f32)
    normed1, scale1 = normalize(x_full)
    first = (normed1 * first_gain + first_bias).astype(bf16)
    project = [
        jnp.dot(first, attention_in[which], preferred_element_type=f32).astype(bf16)
        for which in range(3)
    ]
    query_h, keys_h, values_h = [split_heads(part) for part in project]
    scores = jnp.einsum("iqhd,ikhd->ihqk", query_h, keys_h, preferred_element_type=f32) * scaling
    peak = jnp.max(scores, axis=-1, keepdims=True)
    logsum = peak[..., 0] + jnp.log(jnp.sum(jnp.exp(scores - peak), axis=-1))
    probs = jnp.exp(scores - logsum[..., None])
    weights = probs.astype(bf16)
    context_h = jnp.einsum(
        "ihqk,ikhd->iqhd", weights, values_h, preferred_element_type=f32
    ).astype(bf16)
    context = context_h.reshape(tokens_here, local_width)
    partial_attn = jnp.dot(pad_rows(context), attention_out, preferred_element_type=f32)
    (attn_parts,) = scattered([partial_attn.astype(bf16).reshape(cuts, rows, model_width)], 1)

    attended = jnp.sum(attn_parts.astype(f32), axis=0)
    resid = my_rows(inputs).astype(f32) + attended
    normed2, scale2 = normalize(resid)
    second = (normed2 * second_gain + second_bias).astype(bf16)
    (second_all,) = gathered([second], 2, forward=True)

    base = lax.axis_index("expert") * experts_here
    experts = base + jnp.arange(experts_here, dtype=jnp.int32)
    offset = target_all.astype(jnp.int32)[None] - (experts * capacity)[:, None, None, None]
    slots = jnp.max(jnp.where((offset >= 0) & (offset < capacity), offset, -1), axis=2)
    spot = (experts[:, None] == jnp.arange(lanes, dtype=jnp.int32)).astype(f32)
    mixed, back, share, route_all, expert_cuts = experts_block(
        slots,
        spot,
        second_all.reshape(owners, padded, model_width),
        cot_all,
        jnp.pad(router_weight, ((0, 0), (0, lanes - experts_all))),
        expert_in,
        expert_out,
        experts_all,
        rounded_up(capacity, 16),
    )
    route = lax.dynamic_slice_in_dim(route_all[0], piece * rows, rows, 0)[:, :experts_all]
    mixed_home = to_owners(mixed)
    back_home = to_owners(back)
    route_home = to_owners(share)
    expert_sums = jnp.sum(
        lax.all_to_all(expert_cuts, "dp", 0, 0, tiled=True).astype(f32), axis=0
    )
    expert_in_grad = expert_sums[0]
    expert_out_grad = jnp.swapaxes(expert_sums[1], 1, 2)
    parts = scattered(
        [
            mixed_home.astype(bf16).reshape(cuts, rows, model_width),
            back_home.astype(bf16).reshape(cuts, rows, model_width),
            route_home.reshape(cuts, rows, lanes),
        ],
        3,
    )
    moe, back_rows, route_grad = [jnp.sum(part.astype(f32), axis=0) for part in parts]
    route_grad = route_grad[:, :experts_all]

    layer_rows = resid + moe
    grad_out = my_rows(cotangent).astype(f32)
    logit_grad = route * (route_grad - jnp.sum(route * route_grad, axis=-1, keepdims=True))
    local_router = jnp.dot(
        second.astype(f32).T, logit_grad, precision=lax.Precision.HIGHEST
    )
    second_grad = back_rows + jnp.dot(logit_grad, router_weight.T, precision=lax.Precision.HIGHEST)
    local_second_gain = jnp.sum(second_grad * normed2, axis=0)
    local_second_bias = jnp.sum(second_grad, axis=0)
    resid_grad = grad_out + norm_back(second_grad, normed2, scale2, second_gain)
    (resid_all,) = gathered([resid_grad.astype(bf16)], 4)
    resid_low = resid_all.reshape(padded, model_width)[:tokens_here]

    context_grad = jnp.einsum(
        "rd,hd->rh", resid_low, attention_out, preferred_element_type=f32
    ).astype(bf16)
    context_g = split_heads(context_grad)
    values_grad = jnp.einsum(
        "ihqk,iqhd->ikhd", weights, context_g, preferred_element_type=f32
    ).astype(bf16)
    probs_grad = jnp.einsum("iqhd,ikhd->ihqk", context_g, values_h, preferred_element_type=f32)
    delta = jnp.transpose(
        jnp.sum(context_g.astype(f32) * context_h.astype(f32), axis=-1), (0, 2, 1)
    )
    score_grad = (probs * (probs_grad - delta[..., None]) * scaling).astype(bf16)
    query_grad = jnp.einsum(
        "ihqk,ikhd->iqhd", score_grad, keys_h, preferred_element_type=f32
    ).astype(bf16)
    keys_grad = jnp.einsum(
        "ihqk,iqhd->ikhd", score_grad, query_h, preferred_element_type=f32
    ).astype(bf16)
    grads_flat = [
        part.reshape(tokens_here, local_width) for part in (query_grad, keys_grad, values_grad)
    ]
    partial_first = sum(
        jnp.einsum("rh,dh->rd", grads_flat[k], attention_in[k], preferred_element_type=f32)
        for k in range(3)
    )
    local_first_gain = jnp.sum(partial_first * normed1, axis=0)
    local_first_bias = jnp.sum(partial_first, axis=0)
    members = lax.axis_size("dp") * owners
    share = model_width // members
    small = jnp.concatenate(
        [
            local_router.T,
            jnp.stack([local_first_gain, local_first_bias, local_second_gain, local_second_bias]),
        ]
    )
    tall = rounded_up(small.shape[0], 8)
    small = cut_along(small, 1, members)
    small = jnp.pad(
        small, ((0, 0), (0, tall - small.shape[1]), (0, rounded_up(share, 128) - share))
    )
    first_parts, small_parts = line_and_group(
        pad_rows(partial_first).astype(bf16).reshape(cuts, rows, model_width), small, 5, False
    )
    first_grad = jnp.sum(first_parts.astype(f32), axis=0)
    small_sum = jnp.sum(small_parts, axis=0)
    normed1_rows, scale1_rows = normalize(my_rows(inputs).astype(f32))
    grad_rows = resid_grad + norm_back(first_grad, normed1_rows, scale1_rows, first_gain)
    small_low = small_sum.astype(bf16)
    small_low = jnp.pad(small_low, ((0, rounded_up(tall, 16) - tall), (0, model_width - small_low.shape[1])))
    attention_cuts = jnp.stack(
        [
            jnp.einsum("rd,rh->dh", left, part, preferred_element_type=f32).astype(bf16)
            for left, part in zip([first] * 3 + [resid_low], grads_flat + [context])
        ],
        axis=1,
    ).reshape(members, share, 4, local_width)
    sent_rows = jnp.concatenate([grad_rows.astype(bf16), layer_rows.astype(bf16), small_low])
    grad_all, attention_parts = line_and_group(
        sent_rows, jnp.swapaxes(attention_cuts, 1, 2), 6, True
    )
    input_grad = grad_all[:, :rows].reshape(padded, model_width)[:tokens_here].astype(f32)
    layer_out = grad_all[:, rows : 2 * rows].reshape(padded, model_width)[:tokens_here].astype(f32)
    totals = jnp.sum(grad_all[:, 2 * rows :].astype(f32), axis=0)[:, :share]
    attention_sums = jnp.sum(attention_parts.astype(f32), axis=0)
    attention_in_grad = attention_sums[:3]
    attention_out_grad = attention_sums[3].T
    return (
        layer_out,
        input_grad,
        totals[experts_all],
        totals[experts_all + 1],
        attention_in_grad,
        attention_out_grad,
        totals[experts_all + 2],
        totals[experts_all + 3],
        totals[:experts_all].T,
        expert_in_grad,
        expert_out_grad,
    )


def per_device(
    inputs,
    first_gain,
    first_bias,
    attention_in,
    attention_out,
    second_gain,
    second_bias,
    router_weight,
    expert_in,
    expert_out,
    expert_ids,
    slot_index,
    cotangent,
):
    arguments = (
        inputs,
        first_gain,
        first_bias,
        attention_in,
        attention_out,
        second_gain,
        second_bias,
        router_weight,
        expert_in,
        expert_out,
        expert_ids,
        slot_index,
        cotangent,
    )
    owners, groups, cuts = [lax.axis_size(axis) for axis in ("expert", "dp", "tensor")]
    tokens, width = inputs.shape
    here = expert_in.shape[0]
    experts_all = here * owners
    if (owners, groups, cuts) != (2, 4, 4) or tokens != SEQ or experts_all > 4:
        return per_device_general(*arguments)
    bf16, f32 = jnp.bfloat16, jnp.float32
    capacity = (2 * tokens - 1) // experts_all
    depth = rounded_up(capacity, 16)
    local = attention_in.shape[2]
    heads = local // HEAD_DIM
    rows = rounded_up(rounded_up(tokens, cuts) // cuts, 8)
    padded = rows * cuts
    ctx_rows = rounded_up(tokens, 16)
    members = owners * groups
    cut = width // members
    share = width // groups
    slots = here * depth
    vmem = pl.BlockSpec(memory_space=pltpu.VMEM)
    anywhere = pl.BlockSpec(memory_space=pl.ANY)
    shapes = [
        ((2, cuts, rows, width), bf16),
        ((2, here, share, width), bf16),
        ((2, here, share, width), bf16),
        ((members // 2, cut, 4 * local), bf16),
        ((cuts, 8, 128), f32),
    ]
    slab = (cuts, rows, width)
    vectors = [((width,), f32)] * 4
    scratch = [
        (inputs.shape, bf16),
        (cotangent.shape, bf16),
        *vectors,
        ((experts_all, width), f32),
        ((2, tokens), jnp.int32),
        ((2, tokens), jnp.int32),
        ((padded, width), f32),
        ((padded, width), f32),
        ((2, padded, width), bf16),
        ((2, padded, width), bf16),
        ((2, 8, 256), f32),
        ((8, width), f32),
        ((3, local, width), bf16),
        ((cuts, 2, local // 2, width), bf16),
        ((2, cuts, ctx_rows, local), bf16),
        (expert_in.shape, bf16),
        (expert_out.shape, bf16),
        ((2, padded, width), bf16),
        ((padded, width), f32),
        ((padded, width), bf16),
        ((padded, width), f32),
        ((3, ctx_rows, local), bf16),
        ((heads, ctx_rows, ctx_rows), f32),
        (slab, bf16),
        (slab, bf16),
        (slab, bf16),
        (slab, bf16),
        (slab, bf16),
        (slab, bf16),
        (slab, bf16),
        (slab, bf16),
        (slab, bf16),
        (slab, bf16),
        ((2, rows, width), bf16),
        ((8, 128), f32),
        ((8, 256), f32),
        ((8, 256), f32),
        ((cuts, 8, 256), f32),
        (slab, bf16),
        (slab, f32),
        ((2, 2, 2, here, share, width), bf16),
        ((2, 2, here, share, width), bf16),
        ((2, members // 2, cut, 4 * local), bf16),
        ((members // 2, cut, 4 * local), bf16),
        (slab, bf16),
        (slab, bf16),
        ((8, width), f32),
        ((members, 8, 128), f32),
        ((members, 8, 128), f32),
        ((2, slots, width), bf16),
        ((here, 2 * depth, width), bf16),
        ((here, 2 * depth, width), bf16),
        ((here, 2 * depth, width), bf16),
        ((here, 2 * depth, width), bf16),
        ((2, slots, padded), bf16),
        ((2, slots, width), bf16),
    ]
    sems = [pltpu.SemaphoreType.DMA((n,)) for n in (20, 80, 80)]
    received = pl.pallas_call(
        functools.partial(block_kernel, (tokens, rows, cuts, experts_all, capacity, depth)),
        out_shape=[jax.ShapeDtypeStruct(*s) for s in shapes],
        in_specs=[anywhere] * 13,
        out_specs=[anywhere] * 5,
        scratch_shapes=[pltpu.VMEM(*s) for s in scratch] + sems,
        compiler_params=pltpu.CompilerParams(
            collective_id=0, has_side_effects=True, vmem_limit_bytes=56 << 20
        ),
        name="block",
    )(
        inputs,
        cotangent,
        first_gain,
        first_bias,
        second_gain,
        second_bias,
        router_weight.T,
        expert_ids.T,
        slot_index.T,
        jnp.swapaxes(attention_in, 1, 2),
        attention_out,
        expert_in,
        expert_out,
    )
    results = [
        ((tokens, width), f32),
        ((tokens, width), f32),
        ((1, cut), f32),
        ((1, cut), f32),
        ((3, cut, local), f32),
        ((local, cut), f32),
        ((1, cut), f32),
        ((1, cut), f32),
        ((experts_all, cut), f32),
        ((here, share, width), f32),
        ((here, share, width), f32),
    ]
    large = [results[i] for i in (0, 1, 4, 5, 9, 10)]
    out = pl.pallas_call(
        functools.partial(finish_kernel, (tokens, experts_all, local)),
        out_shape=[jax.ShapeDtypeStruct(*s) for s in results],
        in_specs=[anywhere] * 5,
        out_specs=[anywhere] * 2 + [vmem] * 2 + [anywhere] * 2 + [vmem] * 3 + [anywhere] * 2,
        scratch_shapes=[pltpu.VMEM(*s) for s in shapes + large]
        + [pltpu.SemaphoreType.DMA((n,)) for n in (5, 6)],
        compiler_params=pltpu.CompilerParams(vmem_limit_bytes=56 << 20),
        name="finish",
    )(*received)
    return (
        out[0],
        out[1],
        out[2].reshape(cut),
        out[3].reshape(cut),
        out[4],
        out[5],
        out[6].reshape(cut),
        out[7].reshape(cut),
        out[8].T,
        out[9],
        jnp.swapaxes(out[10], 1, 2),
    )


def solution(mesh):
    in_specs = (
        P(("dp", "expert"), None),
        P(),
        P(),
        P(None, None, "tensor"),
        P("tensor", None),
        P(),
        P(),
        P(),
        P("expert", None, "tensor"),
        P("expert", "tensor", None),
        P(("dp", "expert"), None),
        P(("dp", "expert"), None),
        P(("dp", "expert"), None),
    )
    out_specs = (
        P(("dp", "expert"), None),
        P(("dp", "expert"), None),
        P(("dp", "expert")),
        P(("dp", "expert")),
        P(None, ("dp", "expert"), "tensor"),
        P("tensor", ("dp", "expert")),
        P(("dp", "expert")),
        P(("dp", "expert")),
        P(("dp", "expert"), None),
        P("expert", "dp", "tensor"),
        P("expert", "tensor", "dp"),
    )
    return jax.shard_map(
        per_device, mesh=mesh, in_specs=in_specs, out_specs=out_specs, check_vma=False
    )
```

```python
import functools
import math

import jax
import jax.numpy as jnp
from jax import lax
from jax.experimental import pallas as pl
from jax.experimental.pallas import tpu as pltpu
from jax.sharding import PartitionSpec as P

HEAD_DIM = 64
SEQ = 197


EPS = 1e-06
GELU_C = math.sqrt(2.0 / math.pi)


def cut_along(shard, dim, devices):
    shape = shard.shape
    tiles = shard.reshape(*shape[:dim], devices, shape[dim] // devices, *shape[dim + 1 :])
    return jnp.moveaxis(tiles, dim, 0)


def sent_and_summed(shard, axis, dim):
    devices = lax.axis_size(axis)
    tiles = lax.all_to_all(cut_along(shard, dim, devices), axis, 0, 0, tiled=True)
    return jnp.sum(tiles.astype(jnp.float32), axis=0)


def sent_together(arrays, axis, dim, along):
    widths = [math.prod(a.shape[along:]) for a in arrays]
    both = jnp.concatenate(
        [a.reshape(*a.shape[:along], w) for a, w in zip(arrays, widths)], axis=along
    )
    out = sent_and_summed(both, axis, dim)
    tiles = jnp.split(out, [sum(widths[:k]) for k in range(1, len(widths))], axis=along)
    return tuple((b.reshape(*out.shape[:along], *a.shape[along:]) for a, b in zip(arrays, tiles)))


def normalize(values):
    centre = jnp.mean(values, axis=-1, keepdims=True)
    centred = values - centre
    spread = jnp.mean(centred * centred, axis=-1, keepdims=True)
    scale = lax.rsqrt(spread + EPS)
    return (centred * scale, scale)


def norm_back(grad_out, normed, scale, gain):
    scaled = grad_out * gain
    first_mean = jnp.mean(scaled, axis=-1, keepdims=True)
    second_mean = jnp.mean(scaled * normed, axis=-1, keepdims=True)
    return scale * (scaled - first_mean - normed * second_mean)


def gelu_parts(pre):
    inner = GELU_C * (pre + 0.044715 * pre * pre * pre)
    tangent = jnp.tanh(inner)
    value = 0.5 * pre * (1.0 + tangent)
    slope = 0.5 * (1.0 + tangent) + 0.5 * pre * (1.0 - tangent * tangent) * GELU_C * (
        1.0 + 3.0 * 0.044715 * pre * pre
    )
    return (value, slope)


MESH = pl.DeviceIdType.MESH


def greet(axes):
    barrier = pltpu.get_barrier_semaphore()
    peers = 0
    for axis in axes:
        devices = lax.axis_size(axis)
        me = lax.axis_index(axis)
        for k in range(1, devices):
            peer = lax.rem(me + k, devices)
            pl.semaphore_signal(barrier, inc=1, device_id={axis: peer}, device_id_type=MESH)
            peers += 1
    pl.semaphore_wait(barrier, peers)


def group_peer(k):
    owners = lax.axis_size("expert")
    members = lax.axis_size("dp") * owners
    me = lax.axis_index("dp") * owners + lax.axis_index("expert")
    peer = lax.rem(me + k, members)
    return {"dp": peer // owners, "expert": lax.rem(peer, owners)}


def greet_line_and_group(grouped):
    barrier = pltpu.get_barrier_semaphore()
    cuts = lax.axis_size("tensor")
    members = lax.axis_size("dp") * lax.axis_size("expert") if grouped else 1
    for k in range(1, cuts):
        peer = {"tensor": lax.rem(lax.axis_index("tensor") + k, cuts)}
        pl.semaphore_signal(barrier, inc=1, device_id=peer, device_id_type=MESH)
    for k in range(1, members):
        pl.semaphore_signal(barrier, inc=1, device_id=group_peer(k), device_id_type=MESH)
    pl.semaphore_wait(barrier, cuts + members - 2)


def group_copies(source, target, send_sem, recv_sem):
    owners = lax.axis_size("expert")
    members = lax.axis_size("dp") * owners
    me = lax.axis_index("dp") * owners + lax.axis_index("expert")
    copies = []
    for k in range(1, members):
        copy = pltpu.make_async_remote_copy(
            src_ref=source.at[lax.rem(me + k, members)],
            dst_ref=target.at[k],
            send_sem=send_sem.at[k],
            recv_sem=recv_sem.at[k],
            device_id=group_peer(k),
            device_id_type=MESH,
        )
        copy.start()
        copies.append(copy)
    target[0] = source[me]
    return copies


def ends_kernel(gather, *refs):
    source, group_source, target, group_target = refs[:4]
    send_sem, recv_sem, send_group, recv_group = refs[4:]
    devices = lax.axis_size("tensor")
    me = lax.axis_index("tensor")
    greet_line_and_group(True)
    copies = []
    for k in range(1, devices):
        peer = lax.rem(me + k, devices)
        copy = pltpu.make_async_remote_copy(
            src_ref=source if gather else source.at[peer],
            dst_ref=target.at[me] if gather else target.at[k],
            send_sem=send_sem.at[k],
            recv_sem=recv_sem.at[k],
            device_id={"tensor": peer},
            device_id_type=MESH,
        )
        copy.start()
        copies.append(copy)
    copies += group_copies(group_source, group_target, send_group, recv_group)
    if gather:
        target[me] = source[...]
    else:
        target[0] = source[me]
    for copy in copies:
        copy.wait()


def line_and_group(array, group_array, collective_id, gather):
    devices = lax.axis_size("tensor")
    members = group_array.shape[0]
    shape = (devices, *array.shape) if gather else array.shape
    return pl.pallas_call(
        functools.partial(ends_kernel, gather),
        out_shape=[
            jax.ShapeDtypeStruct(shape, array.dtype),
            jax.ShapeDtypeStruct(group_array.shape, group_array.dtype),
        ],
        in_specs=[pl.BlockSpec(memory_space=pltpu.VMEM)] * 2,
        out_specs=[pl.BlockSpec(memory_space=pltpu.VMEM)] * 2,
        scratch_shapes=[pltpu.SemaphoreType.DMA((n,)) for n in (devices, devices, members, members)],
        compiler_params=pltpu.CompilerParams(collective_id=collective_id, has_side_effects=True),
        name=f"ends{collective_id}",
    )(array, group_array)


def scatter_kernel(count, *refs):
    sources, targets = refs[:count], refs[count : 2 * count]
    send_sem, recv_sem = refs[2 * count :]
    devices = lax.axis_size("tensor")
    me = lax.axis_index("tensor")
    greet(("tensor",))
    copies = []
    for k in range(1, devices):
        peer = lax.rem(me + k, devices)
        for a in range(count):
            copy = pltpu.make_async_remote_copy(
                src_ref=sources[a].at[peer],
                dst_ref=targets[a].at[k],
                send_sem=send_sem.at[a, k],
                recv_sem=recv_sem.at[a, k],
                device_id={"tensor": peer},
                device_id_type=MESH,
            )
            copy.start()
            copies.append(copy)
    for a in range(count):
        targets[a][0] = sources[a][me]
    for copy in copies:
        copy.wait()


def scattered(arrays, collective_id):
    devices = lax.axis_size("tensor")
    count = len(arrays)
    return pl.pallas_call(
        functools.partial(scatter_kernel, count),
        out_shape=[jax.ShapeDtypeStruct(a.shape, a.dtype) for a in arrays],
        in_specs=[pl.BlockSpec(memory_space=pltpu.VMEM)] * count,
        out_specs=[pl.BlockSpec(memory_space=pltpu.VMEM)] * count,
        scratch_shapes=[
            pltpu.SemaphoreType.DMA((count, devices)),
            pltpu.SemaphoreType.DMA((count, devices)),
        ],
        compiler_params=pltpu.CompilerParams(collective_id=collective_id, has_side_effects=True),
        name=f"scatter{collective_id}",
    )(*arrays)


def gather_kernel(count, forward, *refs):
    sources, targets = refs[:count], refs[count : 2 * count]
    send_z, recv_z, send_x, recv_x = refs[2 * count :]
    devices = lax.axis_size("tensor")
    me = lax.axis_index("tensor")
    owners = lax.axis_size("expert") if forward else 1
    home = lax.axis_index("expert")
    greet(("tensor", "expert") if forward else ("tensor",))

    def across(a, k, source, place):
        copies = []
        for e in range(1, owners):
            copy = pltpu.make_async_remote_copy(
                src_ref=source,
                dst_ref=targets[a].at[e, place],
                send_sem=send_x.at[a, k, e],
                recv_sem=recv_x.at[a, k, e],
                device_id={"expert": lax.rem(home + e, owners)},
                device_id_type=MESH,
            )
            copy.start()
            copies.append(copy)
        return copies

    along = []
    for k in range(1, devices):
        peer = lax.rem(me + k, devices)
        for a in range(count):
            copy = pltpu.make_async_remote_copy(
                src_ref=sources[a],
                dst_ref=targets[a].at[0, me],
                send_sem=send_z.at[a, k],
                recv_sem=recv_z.at[a, k],
                device_id={"tensor": peer},
                device_id_type=MESH,
            )
            copy.start()
            along.append((a, k, copy))
    crossing = []
    for a in range(count):
        crossing += across(a, 0, sources[a], me)
    for a in range(count):
        targets[a][0, me] = sources[a][...]
    for a, k, copy in along:
        copy.wait()
        place = lax.rem(me + devices - k, devices)
        crossing += across(a, k, targets[a].at[0, place], place)
    for copy in crossing:
        copy.wait()


def gathered(arrays, collective_id, forward=False):
    devices = lax.axis_size("tensor")
    owners = lax.axis_size("expert") if forward else 1
    count = len(arrays)
    sems = [(count, devices)] * 2 + [(count, devices, owners)] * 2
    return pl.pallas_call(
        functools.partial(gather_kernel, count, forward),
        out_shape=[
            jax.ShapeDtypeStruct((owners, devices, *a.shape), a.dtype) for a in arrays
        ],
        in_specs=[pl.BlockSpec(memory_space=pltpu.VMEM)] * count,
        out_specs=[pl.BlockSpec(memory_space=pltpu.VMEM)] * count,
        scratch_shapes=[pltpu.SemaphoreType.DMA(s) for s in sems],
        compiler_params=pltpu.CompilerParams(collective_id=collective_id, has_side_effects=True),
        name=f"gather{collective_id}",
    )(*arrays)


def shifted(array, axis, offset):
    devices = lax.axis_size(axis)
    return lax.ppermute(array, axis, [(d, (d + offset) % devices) for d in range(devices)])


def from_owners(array):
    owners = lax.axis_size("expert")
    return jnp.stack([array] + [shifted(array, "expert", e) for e in range(1, owners)])


def to_owners(array):
    owners = lax.axis_size("expert")
    total = array[0].astype(jnp.float32)
    for e in range(1, owners):
        total = total + shifted(array[e], "expert", owners - e).astype(jnp.float32)
    return total


def rounded_up(value, multiple):
    return -(-value // multiple) * multiple


def experts_kernel(
    experts_all,
    slot_ref,
    spot_ref,
    second_ref,
    cot_ref,
    router_ref,
    in_ref,
    out_ref,
    mixed_ref,
    back_ref,
    share_ref,
    route_ref,
    cut_ref,
    placing_ref,
    gated_ref,
    low_ref,
    grad_ref,
):
    bf16, f32 = jnp.bfloat16, jnp.float32
    exact = lax.Precision.HIGHEST
    owners, padded, _ = second_ref.shape
    experts_here = in_ref.shape[0]
    lanes = router_ref.shape[1]
    depth = placing_ref.shape[2]

    def dot(a, b, a_dim, b_dim, precision=None):
        return lax.dot_general(
            a, b, (((a_dim,), (b_dim,)), ((), ())), precision=precision, preferred_element_type=f32
        )

    column = lax.broadcasted_iota(jnp.int32, (padded, lanes), 1)
    for o in range(owners):
        logits = dot(second_ref[o].astype(f32), router_ref[...], 1, 0, exact)
        logits = jnp.where(column < experts_all, logits, -1e30)
        lifted = jnp.exp(logits - jnp.max(logits, axis=-1, keepdims=True))
        lifted = jnp.where(column < experts_all, lifted, 0.0)
        route_ref[o] = lifted / jnp.sum(lifted, axis=-1, keepdims=True)
    slot = lax.broadcasted_iota(jnp.int32, (depth, padded), 0)
    for k in range(experts_here):
        gates, received, slotted = [], [], []
        for o in range(owners):
            picks = slot == slot_ref[k, o][None, :]
            placing = jnp.where(picks, 1.0, 0.0)
            low = placing.astype(bf16)
            placing_ref[k, o] = low
            chances = dot(placing, route_ref[o], 1, 0, exact)
            gates.append(jnp.sum(chances * spot_ref[k][None, :], axis=-1, keepdims=True))
            received.append(dot(low, second_ref[o], 1, 0).astype(bf16))
            slotted.append(dot(low, cot_ref[o], 1, 0))
        gate = jnp.concatenate(gates)
        received = jnp.concatenate(received)
        slotted = jnp.concatenate(slotted)
        y_grad = (gate * slotted).astype(bf16)
        value, slope = gelu_parts(dot(received, in_ref[k], 1, 0))
        hidden = value.astype(bf16)
        partial_y = dot(hidden, out_ref[k], 1, 0)
        gated_ref[k] = (gate * partial_y).astype(bf16)
        slot_grad = jnp.sum(slotted * partial_y, axis=-1, keepdims=True)
        grad_ref[k] = slot_grad * spot_ref[k][None, :]
        pre_grad = (dot(y_grad, out_ref[k], 1, 1) * slope).astype(bf16)
        low_ref[k] = dot(pre_grad, in_ref[k], 1, 1).astype(bf16)
        in_grad = dot(received, pre_grad, 0, 0).astype(bf16)
        out_grad = dot(y_grad, hidden, 0, 0).astype(bf16)
        blocks, _, _, share, _ = cut_ref.shape
        for d in range(blocks):
            cut_ref[d, 0, k] = in_grad[d * share : (d + 1) * share]
            cut_ref[d, 1, k] = out_grad[d * share : (d + 1) * share]
    for o in range(owners):
        span = pl.ds(o * depth, depth)
        here = range(experts_here)
        mixed_ref[o] = sum(
            dot(placing_ref[k, o], gated_ref[k, span], 0, 0) for k in here
        ).astype(bf16)
        back_ref[o] = sum(dot(placing_ref[k, o], low_ref[k, span], 0, 0) for k in here).astype(bf16)
        share_ref[o] = sum(
            dot(placing_ref[k, o].astype(f32), grad_ref[k, span], 0, 0, exact) for k in here
        )


def experts_block(slots, spot, second, cot, router, expert_in, expert_out, experts_all, depth):
    owners, padded, width = second.shape
    here, _, hidden = expert_in.shape
    lanes = router.shape[1]
    blocks = lax.axis_size("dp")
    bf16, f32 = jnp.bfloat16, jnp.float32
    shapes = [
        ((owners, padded, width), bf16),
        ((owners, padded, width), bf16),
        ((owners, padded, lanes), f32),
        ((owners, padded, lanes), f32),
        ((blocks, 2, here, width // blocks, hidden), bf16),
    ]
    return pl.pallas_call(
        functools.partial(experts_kernel, experts_all),
        out_shape=[jax.ShapeDtypeStruct(*s) for s in shapes],
        in_specs=[pl.BlockSpec(memory_space=pltpu.VMEM)] * 7,
        out_specs=[pl.BlockSpec(memory_space=pltpu.VMEM)] * 5,
        scratch_shapes=[
            pltpu.VMEM((here, owners, depth, padded), bf16),
            pltpu.VMEM((here, owners * depth, width), bf16),
            pltpu.VMEM((here, owners * depth, width), bf16),
            pltpu.VMEM((here, owners * depth, lanes), f32),
        ],
        compiler_params=pltpu.CompilerParams(
            vmem_limit_bytes=(32 << 20) if owners <= 2 else (60 << 20)
        ),
        name="experts",
    )(slots, spot, second, cot, router, expert_in, expert_out)


def lane_dot(a, b, a_dim, b_dim, precision=None):
    return lax.dot_general(
        a, b, (((a_dim,), (b_dim,)), ((), ())), precision=precision, preferred_element_type=jnp.float32
    )


def block_kernel(dims, *refs):
    tokens, rows, cuts, experts_all, capacity, depth = dims
    bf16, f32 = jnp.bfloat16, jnp.float32
    exact = lax.Precision.HIGHEST
    given = refs[:9]
    (w_hbm, wo_hbm, ein_hbm, eout_hbm) = refs[9:13]
    (final_a, final_b, layers, e_own, e_peer, g_parts, small_parts) = refs[13:20]
    (
        x_in, cot_in, gain1, bias1, gain2, bias2, router_in, ids_in, slot_in, x32, c32,
        xs, cots, cot_out, cot_far, tgt, rt, w_in, wo, ctx, ctx_own, ein, eout, sec, resid, first, n1,
        qkv, probs, back_out, back_in, back_home, back_send, back_got,
        mix_out, mix_in, mix_home, mix_send, mix_got,
        end_layer, end_a, end_b, small_sum, share_out, share_in, share_all, low, lg, cg_out, cg_in, ebuf, e_got, gbuf, g_got, first_a, first_b, first_got_a, first_got_b,
        small, small_send, small_got, lowers, hid, pgr, rec, ygr, plc, gated,
        load, ss, rs,
    ) = refs[20:]
    d, e, z = lax.axis_index("dp"), lax.axis_index("expert"), lax.axis_index("tensor")
    core, y = lax.rem(d, 2), d // 2
    padded = rows * cuts
    width = x_in.shape[1]
    wide = lambda vector: vector[...][None, :]
    local = wo_hbm.shape[0]
    heads = local // HEAD_DIM
    quarter = local // 4
    here = ein_hbm.shape[0]
    ctx_rows = qkv.shape[1]
    ctx_half = ctx_rows // 2
    other_x = {"expert": 1 - e}
    other_core = {"dp": y * 2 + 1 - core}
    other_y = {"dp": (1 - y) * 2 + core}
    diagonal = {"dp": (1 - y) * 2 + core, "expert": 1 - e}
    along = [(k, lax.rem(z + k, cuts)) for k in range(1, cuts)]
    near = z + 1 - 2 * lax.rem(z, 2)
    far = lax.rem(z + 2, cuts)
    last = lax.rem(near + 2, cuts)
    count = [0]
    pending = []

    def send(source, target, device):
        i = count[0]
        count[0] += 1
        copy = pltpu.make_async_remote_copy(
            src_ref=source,
            dst_ref=target,
            send_sem=ss.at[i],
            recv_sem=rs.at[i],
            device_id=device,
            device_id_type=MESH,
        )
        copy.start()
        pending.append(copy)
        return copy

    def spread(source, slab):
        return [send(source, slab(z), {"tensor": peer}) for peer in (near, far)]

    def passed_on(copies, slab):
        copies[1].wait_recv()
        copies.append(send(slab(far), slab(far), {"tensor": near}))

    loads = [
        pltpu.make_async_copy(w_hbm, w_in, load.at[0]),
        pltpu.make_async_copy(wo_hbm, wo.at[z], load.at[1]),
        pltpu.make_async_copy(ein_hbm, ein, load.at[2]),
        pltpu.make_async_copy(eout_hbm, eout, load.at[3]),
    ]
    here_now = (x_in, cot_in, gain1, bias1, gain2, bias2, router_in, ids_in, slot_in)
    early = [
        pltpu.make_async_copy(source, target, load.at[4 + i])
        for i, (source, target) in enumerate(zip(given, here_now))
    ]
    for copy in early + loads:
        copy.start()
    barrier = pltpu.get_barrier_semaphore()
    others = [
        {"dp": (y if same_y else 1 - y) * 2 + (core if same_core else 1 - core),
         "expert": e if same_e else 1 - e}
        for same_y in (1, 0) for same_core in (1, 0) for same_e in (1, 0)
    ][1:]
    greeted = others + [{"tensor": p} for _, p in along]
    for peer in greeted:
        pl.semaphore_signal(barrier, inc=1, device_id=peer, device_id_type=MESH)

    for copy in early:
        copy.wait()
    edge = tokens // 8 * 8
    for whole, part in ((x32, x_in), (c32, cot_in)):
        whole[edge:padded] = jnp.zeros((padded - edge, width), f32)
        whole[0:tokens] = part[...].astype(f32)
    xs[0] = x32[...].astype(bf16)
    xs[1, ctx_rows:padded] = jnp.zeros((padded - ctx_rows, width), bf16)
    cots[...] = c32[...].astype(bf16)
    cot_rows = c32[pl.ds(pl.multiple_of(z * rows, 8), rows)]
    cot_out[...] = cot_rows.astype(bf16)
    x_full = x32[...]
    tgt[0] = jnp.full(tgt.shape[1:], -1.0, f32)
    slot = slot_in[...]
    tgt[0, 0:2, 0:tokens] = jnp.where(slot < capacity, ids_in[...] * capacity + slot, -1).astype(f32)
    rt[...] = jnp.zeros_like(rt)
    rt[0:experts_all] = router_in[...]

    pl.semaphore_wait(barrier, len(greeted))
    loads[1].wait()

    def wo_part(c, part):
        return wo.at[c, pl.ds(pl.multiple_of(part * quarter, 16), quarter)]

    cot_copy = send(cot_out, cot_far.at[z], other_x)
    mine_of_wo = lambda c: wo_part(c, d)
    wo_along = spread(wo_part(z, d), mine_of_wo)
    x_copy = send(xs.at[0, pl.ds(0, ctx_rows)], xs.at[1, pl.ds(0, ctx_rows)], other_x)
    tgt_copy = send(tgt.at[0], tgt.at[1], other_x)

    normed, _ = normalize(x_full)
    n1[...] = normed
    first_low = (normed * wide(gain1) + wide(bias1)).astype(bf16)
    first[...] = first_low
    loads[0].wait()
    for which in range(3):
        qkv[which] = lane_dot(first_low[:ctx_rows], w_in[which], 1, 1).astype(bf16)
    head = lax.broadcasted_iota(jnp.int32, (ctx_rows, local), 1) // HEAD_DIM
    masks = [jnp.where(head == h, 1.0, 0.0) for h in range(heads)]
    key_at = lax.broadcasted_iota(jnp.int32, (ctx_rows, ctx_rows), 1)
    scaling = HEAD_DIM ** (-0.5)

    def of_head(matrix, h):
        return matrix * masks[h].astype(matrix.dtype)

    query, keys, values = qkv[0], qkv[1], qkv[2]
    total = jnp.zeros((ctx_rows, local), f32)
    for h in range(heads):
        scores = lane_dot(of_head(query, h), keys, 1, 1) * scaling
        scores = jnp.where(key_at < tokens, scores, -1e30)
        peak = jnp.max(scores, axis=-1, keepdims=True)
        logsum = peak + jnp.log(jnp.sum(jnp.exp(scores - peak), axis=-1, keepdims=True))
        chance = jnp.exp(scores - logsum)
        probs[h] = chance
        total += lane_dot(chance.astype(bf16), of_head(values, h), 1, 0)
    ctx_own[...] = total.astype(bf16)
    ctx[0, z] = jnp.concatenate([total[:ctx_half], total[ctx_half:]], axis=1).astype(bf16)

    near_ctx = lambda c: ctx.at[0, c]
    ctx_along = spread(ctx.at[0, z], near_ctx)
    ctx_across = [(z, send(ctx.at[0, z], ctx.at[1, z], other_x))]

    far_row = (1 - y) * 2 + core
    wo_row, wo_core = [], []

    def wo_on(place):
        wo_row.append((place, send(wo_part(place, d), wo_part(place, d), other_y)))
        wo_core.append(send(wo_part(place, d), wo_part(place, d), other_core))

    def ctx_on(place):
        ctx_across.append((place, send(ctx.at[0, place], ctx.at[1, place], other_x)))

    wo_along[0].wait_recv()
    wo_on(near)
    passed_on(wo_along, mine_of_wo)
    wo_on(far)
    ctx_along[0].wait_recv()
    ctx_on(near)
    passed_on(ctx_along, near_ctx)
    ctx_on(far)
    wo_along[2].wait_recv()
    wo_on(last)
    cot_copy.wait_recv()
    far_cot = lambda c: cot_far.at[c]
    cot_far_along = spread(cot_far.at[z], far_cot)
    ctx_along[2].wait_recv()
    ctx_on(last)
    for place, copy in wo_row:
        copy.wait_recv()
        wo_core.append(send(wo_part(place, far_row), wo_part(place, far_row), other_core))
    for copy in wo_core:
        copy.wait_recv()

    split = rt[...]
    splits = []
    for _ in range(3):
        piece = split.astype(bf16)
        splits.append(piece.astype(f32))
        split = split - piece.astype(f32)
    router_low = jnp.concatenate(splits).astype(bf16)
    lanes8 = rt.shape[0]
    expert_row = lax.broadcasted_iota(jnp.int32, (lanes8, padded), 0)
    base = e * here

    def forward(o):
        halves = [jnp.zeros((ctx_half, width), f32) for _ in range(2)]
        for c in range(cuts):
            both = ctx[o, c]
            for n in range(2):
                halves[n] += lane_dot(both[:, n * local : (n + 1) * local], wo[c], 1, 0)
        attended = jnp.concatenate([*halves, jnp.zeros((padded - ctx_rows, width), f32)])
        res = xs[o].astype(f32) + attended
        normed2, _ = normalize(res)
        second = (normed2 * wide(gain2) + wide(bias2)).astype(bf16)
        sec[o] = second
        parts = lane_dot(router_low, second, 1, 1)
        logits = parts[:lanes8] + parts[lanes8 : 2 * lanes8] + parts[2 * lanes8 :]
        logits = jnp.where(expert_row < experts_all, logits, -1e30)
        lifted = jnp.exp(logits - jnp.max(logits, axis=0, keepdims=True))
        lifted = jnp.where(expert_row < experts_all, lifted, 0.0)
        return res, lifted / jnp.sum(lifted, axis=0, keepdims=True)

    slot_at = lax.broadcasted_iota(jnp.int32, (depth, padded), 0)

    def picks_of(o, k):
        offset = tgt[o, 0:2, 0:padded].astype(jnp.int32) - (base + k) * capacity
        chosen = jnp.where((offset >= 0) & (offset < capacity), offset, -1)
        return slot_at == jnp.max(chosen, axis=0, keepdims=True)

    def place(o, route):
        placed, gates = [], []
        for k in range(here):
            picks = picks_of(o, k)
            placed.append(jnp.where(picks, 1.0, 0.0))
            row = jnp.sum(jnp.where(expert_row == base + k, route, 0.0), axis=0, keepdims=True)
            gates.append(jnp.sum(jnp.where(picks, row, 0.0), axis=-1, keepdims=True))
        low_place = jnp.concatenate(placed).astype(bf16)
        plc[o] = low_place
        gate = jnp.concatenate(gates)
        received = lane_dot(low_place, sec[o], 1, 0).astype(bf16)
        return gate, received

    res, route_own = forward(0)
    resid[...] = res
    tgt_copy.wait_recv()
    x_copy.wait_recv()
    passed_on(cot_far_along, far_cot)
    own = place(0, route_own)
    for _, copy in ctx_across:
        copy.wait_recv()
    _, route_far = forward(1)
    away = place(1, route_far)
    loads[2].wait()
    loads[3].wait()

    def joined(both, k):
        span = slice(k * depth, (k + 1) * depth)
        return jnp.concatenate([part[span] for part in both])

    fore = []
    for k in range(here):
        received = joined((own[1], away[1]), k)
        value, slope = gelu_parts(lane_dot(received, ein[k], 1, 0))
        hidden = value.astype(bf16)
        rec[k], hid[k] = received, hidden
        partial_y = lane_dot(hidden, eout[k], 1, 0)
        gate = joined((own[0], away[0]), k)
        fore.append((gate, slope, partial_y))
        weighted = (gate * partial_y).astype(bf16)
        for o in range(2):
            gated[o, k * depth : (k + 1) * depth] = weighted[o * depth : (o + 1) * depth]
    for copy in cot_far_along[::2]:
        copy.wait_recv()
    cot_all = jnp.concatenate([cot_far[c].astype(f32) for c in range(cuts)]).astype(bf16)
    slotted_both = [lane_dot(plc[o], cot, 1, 0) for o, cot in enumerate((cots[...], cot_all))]
    shares = [jnp.zeros((lanes8, padded), f32) for _ in range(2)]
    for k in range(here):
        gate, slope, partial_y = fore[k]
        slotted = joined(slotted_both, k)
        y_grad = (gate * slotted).astype(bf16)
        pre_grad = (lane_dot(y_grad, eout[k], 1, 1) * slope).astype(bf16)
        lowered = lane_dot(pre_grad, ein[k], 1, 1).astype(bf16)
        slot_grad = jnp.sum(slotted * partial_y, axis=-1, keepdims=True)
        ygr[k], pgr[k] = y_grad, pre_grad
        for o in range(2):
            span = slice(o * depth, (o + 1) * depth)
            lowers[o, k * depth : (k + 1) * depth] = lowered[span]
            row = jnp.sum(
                jnp.where(picks_of(o, k), slot_grad[span], 0.0), axis=0, keepdims=True
            )
            shares[o] += jnp.where(expert_row == base + k, row, 0.0)

    def chunked(target, matrix):
        for c in range(cuts):
            target[c] = matrix[c * rows : (c + 1) * rows].astype(target.dtype)

    chunked(back_out, lane_dot(plc[1], lowers[1], 0, 0))
    order = [lax.rem(z + k, cuts) for k in (2, 1, 3, 0)]
    back_across = [send(back_out.at[c], back_in.at[c], other_x) for c in order[:2]]
    share_out[...] = jnp.zeros_like(share_out)
    share_out[:, 0:padded] = shares[1]
    share_across = send(share_out, share_in, other_x)
    def expert_grads(k):
        in_grad = lane_dot(rec[k], pgr[k], 0, 0).astype(bf16)
        out_grad = lane_dot(ygr[k], hid[k], 0, 0).astype(bf16)
        share = width // 4
        for p in range(4):
            span = slice(p * share, (p + 1) * share)
            ebuf[p % 2, k, p // 2, 0] = in_grad[span]
            ebuf[p % 2, k, p // 2, 1] = out_grad[span]
        return send(ebuf.at[1 - core, k], e_got.at[k], other_core)

    e_row = []

    def e_on(k):
        e_core[k].wait_recv()
        for yy in range(2):
            for a in range(2):
                both = ebuf[core, k, yy, a].astype(f32) + e_got[k, yy, a].astype(f32)
                ebuf[core, k, yy, a] = both.astype(bf16)
        e_row.append(send(ebuf.at[core, k, 1 - y], e_peer.at[k], other_y))

    e_core = [expert_grads(k) for k in range(here)]
    chunked(back_home, lane_dot(plc[0], lowers[0], 0, 0))
    e_on(0)
    share_across.wait_recv()
    share_all[0] = share_in[...]
    share_all[0, :, 0:padded] += shares[0]
    share_along = [send(share_all.at[0], share_all.at[k], {"tensor": peer}) for k, peer in along]
    back_along = []
    for j, c in enumerate(order):
        back_across[j].wait_recv()
        if j < 2:
            back_across.append(send(back_out.at[order[j + 2]], back_in.at[order[j + 2]], other_x))
        back_send[c] = (back_home[c].astype(f32) + back_in[c].astype(f32)).astype(bf16)
        if j < 3:
            k = (2, 1, 3)[j]
            back_along.append(send(back_send.at[c], back_got.at[k], {"tensor": c}))
    chunked(mix_out, lane_dot(plc[1], gated[1], 0, 0))
    mix_across = [send(mix_out.at[c], mix_in.at[c], other_x) for c in order]
    chunked(mix_home, lane_dot(plc[0], gated[0], 0, 0))
    e_on(1)

    for copy in share_along:
        copy.wait_recv()
    route_grad = (share_all[0] + share_all[1] + share_all[2] + share_all[3])[:, 0:padded]
    logit_grad = route_own * (route_grad - jnp.sum(route_own * route_grad, axis=0, keepdims=True))
    chunked(lg, lane_dot(logit_grad, rt[...], 0, 0, exact))
    router_grad = lane_dot(logit_grad, sec[0].astype(f32), 1, 0, exact)
    res_rows = resid[pl.ds(pl.multiple_of(z * rows, 8), rows)]
    normed2, scale2 = normalize(res_rows)
    for copy in back_along:
        copy.wait_recv()
    back = back_send[z].astype(f32)
    for k, _ in along:
        back += back_got[k].astype(f32)
    second_grad = back + lg[z]
    resid_grad = cot_rows + norm_back(second_grad, normed2, scale2, wide(gain2))
    lg[z] = resid_grad
    low_rows = resid_grad.astype(bf16)
    low[z] = low_rows
    for c in range(cuts):
        cg_out[c] = lane_dot(low_rows, wo[c], 1, 1).astype(bf16)
    cg_along = [send(cg_out.at[peer], cg_in.at[z], {"tensor": peer}) for _, peer in along]
    cg_in[z] = cg_out[z]

    small[...] = jnp.zeros_like(small)
    small[0:experts_all] = jnp.where(z == 0, router_grad[:experts_all], 0.0)
    small[experts_all : experts_all + 1] = jnp.sum(second_grad * normed2, axis=0, keepdims=True)
    small[experts_all + 1 : experts_all + 2] = jnp.sum(second_grad, axis=0, keepdims=True)
    for j, copy in enumerate(mix_across):
        copy.wait_recv()
        c = order[j]
        mix_send[c] = (mix_home[c].astype(f32) + mix_in[c].astype(f32)).astype(bf16)
    mix_along = [
        send(mix_send.at[last], mix_got.at[1], {"tensor": near}),
        send(mix_send.at[near], mix_got.at[0], {"tensor": near}),
    ]
    slab_low = lambda c: low.at[c]
    low_along = spread(low.at[z], slab_low)

    for copy in cg_along:
        copy.wait_recv()
    ctx_grad = jnp.concatenate([cg_in[c].astype(f32) for c in range(cuts)])[:ctx_rows].astype(bf16)
    own_ctx = ctx_own[...]
    product = ctx_grad.astype(f32) * own_ctx.astype(f32)
    query_grad = jnp.zeros((ctx_rows, local), f32)
    keys_grad = jnp.zeros((ctx_rows, local), f32)
    values_grad = jnp.zeros((ctx_rows, local), f32)
    query, keys, values = qkv[0], qkv[1], qkv[2]
    for h in range(heads):
        chance = probs[h]
        grad_h = of_head(ctx_grad, h)
        delta = jnp.sum(of_head(product, h), axis=-1, keepdims=True)
        values_grad += lane_dot(chance.astype(bf16), grad_h, 0, 0)
        score_grad = (chance * (lane_dot(grad_h, values, 1, 1) - delta) * scaling).astype(bf16)
        query_grad += lane_dot(score_grad, of_head(keys, h), 1, 0)
        keys_grad += lane_dot(score_grad, of_head(query, h), 0, 0)
    grads = [g.astype(bf16) for g in (query_grad, keys_grad, values_grad)]
    mix_along[0].wait_recv()
    mix_got[3] = (mix_send[far].astype(f32) + mix_got[1].astype(f32)).astype(bf16)
    mix_along.append(send(mix_got.at[3], mix_got.at[2], {"tensor": far}))
    passed_on(low_along, slab_low)
    partial = sum(lane_dot(grads[k], w_in[k], 1, 0) for k in range(3))
    partial = jnp.concatenate([partial, jnp.zeros((padded - ctx_rows, width), f32)])
    early_rows = first_a.shape[1]
    for c in range(cuts):
        first_a[c] = partial[c * rows : c * rows + early_rows].astype(bf16)
        first_b[c] = partial[c * rows + early_rows : (c + 1) * rows].astype(bf16)
    turns = [along[1], along[0], along[2]]
    first_along = [
        [send(source.at[peer], target.at[k], {"tensor": peer}) for k, peer in turns]
        for source, target in ((first_a, first_got_a), (first_b, first_got_b))
    ]
    small[experts_all + 2 : experts_all + 3] = jnp.sum(partial * n1[...], axis=0, keepdims=True)
    small[experts_all + 3 : experts_all + 4] = jnp.sum(partial, axis=0, keepdims=True)
    members = small_send.shape[0]
    cut = width // members
    for m in range(members):
        small_send[m, :, 0:cut] = small[:, m * cut : (m + 1) * cut]
    me = d * 2 + e
    small_across = [
        send(
            small_send.at[device["dp"] * 2 + device["expert"]], small_got.at[k], device
        )
        for k, device in enumerate(others)
    ]
    top = first[0:ctx_rows]
    results = [lane_dot(top, g, 0, 0).astype(bf16) for g in grads]
    for copy in low_along[::2]:
        copy.wait_recv()
    resid_low = jnp.concatenate([low[c].astype(f32) for c in range(cuts)])
    results.append(lane_dot(resid_low[:ctx_rows].astype(bf16), own_ctx, 0, 0).astype(bf16))
    for m in range(members):
        for k in range(4):
            gbuf[(m // 2) % 2, (m // 4) * 2 + m % 2, :, k * local : (k + 1) * local] = results[k][
                m * cut : (m + 1) * cut
            ]
    g_core = send(gbuf.at[1 - core], g_got, other_core)

    for copy in mix_along[1:]:
        copy.wait_recv()
    mixed = mix_send[z].astype(f32) + mix_got[0].astype(f32) + mix_got[2].astype(f32)
    end_layer[...] = (resid[pl.ds(pl.multiple_of(z * rows, 8), rows)] + mixed).astype(bf16)
    slab_layer = lambda c: layers.at[c]
    layer_along = spread(end_layer, slab_layer)
    kept = []

    def keep(source, target):
        copy = pltpu.make_async_copy(source, target, load.at[13 + len(kept)])
        copy.start()
        kept.append(copy)

    keep(end_layer, layers.at[z])
    for k in range(here):
        keep(ebuf.at[core, k, y], e_own.at[k])
    g_core.wait_recv()
    for m in range(members // 2):
        gbuf[core, m] = (gbuf[core, m].astype(f32) + g_got[m].astype(f32)).astype(bf16)
    mine = y * 2 + e
    g_across = [
        send(gbuf.at[core, place_], g_parts.at[k], device)
        for k, place_, device in [
            (1, y * 2 + 1 - e, other_x),
            (2, (1 - y) * 2 + e, other_y),
            (3, (1 - y) * 2 + 1 - e, diagonal),
        ]
    ]
    keep(gbuf.at[core, mine], g_parts.at[0])
    for copy in small_across:
        copy.wait_recv()
    added = small_send[me]
    for k in range(members - 1):
        added += small_got[k]
    small_sum[...] = added
    keep(small_sum, small_parts.at[0])
    small_along = [
        send(small_sum, small_parts.at[k], {"tensor": peer}) for k, peer in along
    ]

    normed_rows, scale_rows = normalize(x32[pl.ds(pl.multiple_of(z * rows, 8), rows)])
    base_grad = lg[z]
    final_along = []
    for part, (sent, got, end, final) in enumerate(
        [(first_a, first_got_a, end_a, final_a), (first_b, first_got_b, end_b, final_b)]
    ):
        span = slice(0, early_rows) if part == 0 else slice(early_rows, rows)
        for copy in first_along[part]:
            copy.wait_recv()
        first_grad = sent[z].astype(f32)
        for k, _ in along:
            first_grad += got[k].astype(f32)
        grad_rows = base_grad[span] + norm_back(
            first_grad, normed_rows[span], scale_rows[span], wide(gain1)
        )
        end[...] = grad_rows.astype(bf16)
        final_along += [send(end, final.at[z], {"tensor": peer}) for _, peer in along]
        keep(end, final.at[z])
    for copy in kept:
        copy.wait()
    passed_on(layer_along, slab_layer)
    for copy in layer_along[::2] + final_along + g_across + small_along + e_row:
        copy.wait_recv()
    for copy in pending:
        copy.wait_send()


def finish_kernel(dims, *refs):
    tokens, experts_all, local = dims
    f32 = jnp.float32
    given = refs[:7]
    layer_out, grad_out, gain1, bias1, att_in_out, att_out_out, gain2, bias2, router = refs[7:16]
    in_out, out_out = refs[16:18]
    final_a, final_b, layers, e_own, e_peer, g_parts, small_parts = held = refs[18:25]
    layer, grad, att_in, att_out, grad_in, grad_out_w = refs[25:31]
    load, store = refs[31:]
    cuts = layers.shape[0]
    cut = gain1.shape[1]
    loads = [
        pltpu.make_async_copy(given[i], held[i], load.at[i]) for i in range(7)
    ]
    for i in (3, 4, 5, 2, 0, 1, 6):
        loads[i].start()
    stores = []

    def keep(source, target):
        copy = pltpu.make_async_copy(source, target, store.at[len(stores)])
        copy.start()
        stores.append(copy)

    loads[3].wait()
    loads[4].wait()
    for which, (target, out) in enumerate([(grad_in, in_out), (grad_out_w, out_out)]):
        for k in range(target.shape[0]):
            target[k] = e_own[k, which].astype(f32) + e_peer[k, which].astype(f32)
        keep(target, out)
    loads[5].wait()
    parts = sum(g_parts[k].astype(f32) for k in range(g_parts.shape[0]))
    for k in range(3):
        att_in[k] = parts[:, k * local : (k + 1) * local]
    keep(att_in, att_in_out)
    att_out[...] = parts[:, 3 * local :].T
    keep(att_out, att_out_out)
    loads[2].wait()
    whole = jnp.concatenate([layers[c].astype(f32) for c in range(cuts)])
    layer[...] = whole[:tokens]
    keep(layer, layer_out)
    loads[0].wait()
    loads[1].wait()
    whole = jnp.concatenate(
        [part[c].astype(f32) for c in range(cuts) for part in (final_a, final_b)]
    )
    grad[...] = whole[:tokens]
    keep(grad, grad_out)
    loads[6].wait()
    totals = sum(small_parts[k] for k in range(cuts))[:, :cut]
    router[...] = totals[:experts_all]
    for i, target in enumerate((gain2, bias2, gain1, bias1)):
        target[...] = totals[experts_all + i : experts_all + i + 1]
    for copy in stores:
        copy.wait()


def per_device_general(
    inputs,
    first_gain,
    first_bias,
    attention_in,
    attention_out,
    second_gain,
    second_bias,
    router_weight,
    expert_in,
    expert_out,
    expert_ids,
    slot_index,
    cotangent,
):
    bf16, f32 = jnp.bfloat16, jnp.float32
    tokens_here = inputs.shape[0]
    model_width = inputs.shape[1]
    images = tokens_here // SEQ
    local_width = attention_in.shape[2]
    local_heads = local_width // HEAD_DIM
    owners = lax.axis_size("expert")
    cuts = lax.axis_size("tensor")
    experts_here = expert_in.shape[0]
    experts_all = experts_here * owners
    capacity = (2 * tokens_here - 1) // experts_all
    scaling = HEAD_DIM ** (-0.5)
    rows = rounded_up(rounded_up(tokens_here, cuts) // cuts, 8)
    padded = rows * cuts
    lanes = rounded_up(experts_all, 128)
    piece = lax.axis_index("tensor")

    def split_heads(matrix):
        return matrix.reshape(images, SEQ, local_heads, HEAD_DIM)

    def pad_rows(matrix, value=0):
        return jnp.pad(
            matrix, ((0, padded - tokens_here), (0, 0)), constant_values=value
        )

    def my_rows(matrix):
        return lax.dynamic_slice_in_dim(pad_rows(matrix), piece * rows, rows, 0)

    target = jnp.where(slot_index < capacity, expert_ids * capacity + slot_index, -1)
    target_all = from_owners(pad_rows(target, -1).astype(f32).T)
    cot_all = from_owners(pad_rows(cotangent))

    x_full = inputs.astype(f32)
    normed1, scale1 = normalize(x_full)
    first = (normed1 * first_gain + first_bias).astype(bf16)
    project = [
        jnp.dot(first, attention_in[which], preferred_element_type=f32).astype(bf16)
        for which in range(3)
    ]
    query_h, keys_h, values_h = [split_heads(part) for part in project]
    scores = jnp.einsum("iqhd,ikhd->ihqk", query_h, keys_h, preferred_element_type=f32) * scaling
    peak = jnp.max(scores, axis=-1, keepdims=True)
    logsum = peak[..., 0] + jnp.log(jnp.sum(jnp.exp(scores - peak), axis=-1))
    probs = jnp.exp(scores - logsum[..., None])
    weights = probs.astype(bf16)
    context_h = jnp.einsum(
        "ihqk,ikhd->iqhd", weights, values_h, preferred_element_type=f32
    ).astype(bf16)
    context = context_h.reshape(tokens_here, local_width)
    partial_attn = jnp.dot(pad_rows(context), attention_out, preferred_element_type=f32)
    (attn_parts,) = scattered([partial_attn.astype(bf16).reshape(cuts, rows, model_width)], 1)

    attended = jnp.sum(attn_parts.astype(f32), axis=0)
    resid = my_rows(inputs).astype(f32) + attended
    normed2, scale2 = normalize(resid)
    second = (normed2 * second_gain + second_bias).astype(bf16)
    (second_all,) = gathered([second], 2, forward=True)

    base = lax.axis_index("expert") * experts_here
    experts = base + jnp.arange(experts_here, dtype=jnp.int32)
    offset = target_all.astype(jnp.int32)[None] - (experts * capacity)[:, None, None, None]
    slots = jnp.max(jnp.where((offset >= 0) & (offset < capacity), offset, -1), axis=2)
    spot = (experts[:, None] == jnp.arange(lanes, dtype=jnp.int32)).astype(f32)
    mixed, back, share, route_all, expert_cuts = experts_block(
        slots,
        spot,
        second_all.reshape(owners, padded, model_width),
        cot_all,
        jnp.pad(router_weight, ((0, 0), (0, lanes - experts_all))),
        expert_in,
        expert_out,
        experts_all,
        rounded_up(capacity, 16),
    )
    route = lax.dynamic_slice_in_dim(route_all[0], piece * rows, rows, 0)[:, :experts_all]
    mixed_home = to_owners(mixed)
    back_home = to_owners(back)
    route_home = to_owners(share)
    expert_sums = jnp.sum(
        lax.all_to_all(expert_cuts, "dp", 0, 0, tiled=True).astype(f32), axis=0
    )
    expert_in_grad = expert_sums[0]
    expert_out_grad = jnp.swapaxes(expert_sums[1], 1, 2)
    parts = scattered(
        [
            mixed_home.astype(bf16).reshape(cuts, rows, model_width),
            back_home.astype(bf16).reshape(cuts, rows, model_width),
            route_home.reshape(cuts, rows, lanes),
        ],
        3,
    )
    moe, back_rows, route_grad = [jnp.sum(part.astype(f32), axis=0) for part in parts]
    route_grad = route_grad[:, :experts_all]

    layer_rows = resid + moe
    grad_out = my_rows(cotangent).astype(f32)
    logit_grad = route * (route_grad - jnp.sum(route * route_grad, axis=-1, keepdims=True))
    local_router = jnp.dot(
        second.astype(f32).T, logit_grad, precision=lax.Precision.HIGHEST
    )
    second_grad = back_rows + jnp.dot(logit_grad, router_weight.T, precision=lax.Precision.HIGHEST)
    local_second_gain = jnp.sum(second_grad * normed2, axis=0)
    local_second_bias = jnp.sum(second_grad, axis=0)
    resid_grad = grad_out + norm_back(second_grad, normed2, scale2, second_gain)
    (resid_all,) = gathered([resid_grad.astype(bf16)], 4)
    resid_low = resid_all.reshape(padded, model_width)[:tokens_here]

    context_grad = jnp.einsum(
        "rd,hd->rh", resid_low, attention_out, preferred_element_type=f32
    ).astype(bf16)
    context_g = split_heads(context_grad)
    values_grad = jnp.einsum(
        "ihqk,iqhd->ikhd", weights, context_g, preferred_element_type=f32
    ).astype(bf16)
    probs_grad = jnp.einsum("iqhd,ikhd->ihqk", context_g, values_h, preferred_element_type=f32)
    delta = jnp.transpose(
        jnp.sum(context_g.astype(f32) * context_h.astype(f32), axis=-1), (0, 2, 1)
    )
    score_grad = (probs * (probs_grad - delta[..., None]) * scaling).astype(bf16)
    query_grad = jnp.einsum(
        "ihqk,ikhd->iqhd", score_grad, keys_h, preferred_element_type=f32
    ).astype(bf16)
    keys_grad = jnp.einsum(
        "ihqk,iqhd->ikhd", score_grad, query_h, preferred_element_type=f32
    ).astype(bf16)
    grads_flat = [
        part.reshape(tokens_here, local_width) for part in (query_grad, keys_grad, values_grad)
    ]
    partial_first = sum(
        jnp.einsum("rh,dh->rd", grads_flat[k], attention_in[k], preferred_element_type=f32)
        for k in range(3)
    )
    local_first_gain = jnp.sum(partial_first * normed1, axis=0)
    local_first_bias = jnp.sum(partial_first, axis=0)
    members = lax.axis_size("dp") * owners
    share = model_width // members
    small = jnp.concatenate(
        [
            local_router.T,
            jnp.stack([local_first_gain, local_first_bias, local_second_gain, local_second_bias]),
        ]
    )
    tall = rounded_up(small.shape[0], 8)
    small = cut_along(small, 1, members)
    small = jnp.pad(
        small, ((0, 0), (0, tall - small.shape[1]), (0, rounded_up(share, 128) - share))
    )
    first_parts, small_parts = line_and_group(
        pad_rows(partial_first).astype(bf16).reshape(cuts, rows, model_width), small, 5, False
    )
    first_grad = jnp.sum(first_parts.astype(f32), axis=0)
    small_sum = jnp.sum(small_parts, axis=0)
    normed1_rows, scale1_rows = normalize(my_rows(inputs).astype(f32))
    grad_rows = resid_grad + norm_back(first_grad, normed1_rows, scale1_rows, first_gain)
    small_low = small_sum.astype(bf16)
    small_low = jnp.pad(small_low, ((0, rounded_up(tall, 16) - tall), (0, model_width - small_low.shape[1])))
    attention_cuts = jnp.stack(
        [
            jnp.einsum("rd,rh->dh", left, part, preferred_element_type=f32).astype(bf16)
            for left, part in zip([first] * 3 + [resid_low], grads_flat + [context])
        ],
        axis=1,
    ).reshape(members, share, 4, local_width)
    sent_rows = jnp.concatenate([grad_rows.astype(bf16), layer_rows.astype(bf16), small_low])
    grad_all, attention_parts = line_and_group(
        sent_rows, jnp.swapaxes(attention_cuts, 1, 2), 6, True
    )
    input_grad = grad_all[:, :rows].reshape(padded, model_width)[:tokens_here].astype(f32)
    layer_out = grad_all[:, rows : 2 * rows].reshape(padded, model_width)[:tokens_here].astype(f32)
    totals = jnp.sum(grad_all[:, 2 * rows :].astype(f32), axis=0)[:, :share]
    attention_sums = jnp.sum(attention_parts.astype(f32), axis=0)
    attention_in_grad = attention_sums[:3]
    attention_out_grad = attention_sums[3].T
    return (
        layer_out,
        input_grad,
        totals[experts_all],
        totals[experts_all + 1],
        attention_in_grad,
        attention_out_grad,
        totals[experts_all + 2],
        totals[experts_all + 3],
        totals[:experts_all].T,
        expert_in_grad,
        expert_out_grad,
    )


def per_device(
    inputs,
    first_gain,
    first_bias,
    attention_in,
    attention_out,
    second_gain,
    second_bias,
    router_weight,
    expert_in,
    expert_out,
    expert_ids,
    slot_index,
    cotangent,
):
    arguments = (
        inputs,
        first_gain,
        first_bias,
        attention_in,
        attention_out,
        second_gain,
        second_bias,
        router_weight,
        expert_in,
        expert_out,
        expert_ids,
        slot_index,
        cotangent,
    )
    owners, groups, cuts = [lax.axis_size(axis) for axis in ("expert", "dp", "tensor")]
    tokens, width = inputs.shape
    here = expert_in.shape[0]
    experts_all = here * owners
    if (owners, groups, cuts) != (2, 4, 4) or tokens != SEQ or experts_all > 4:
        return per_device_general(*arguments)
    bf16, f32 = jnp.bfloat16, jnp.float32
    capacity = (2 * tokens - 1) // experts_all
    depth = rounded_up(capacity, 16)
    local = attention_in.shape[2]
    heads = local // HEAD_DIM
    rows = rounded_up(rounded_up(tokens, cuts) // cuts, 8)
    padded = rows * cuts
    ctx_rows = rounded_up(tokens, 16)
    members = owners * groups
    cut = width // members
    share = width // groups
    slots = here * depth
    vmem = pl.BlockSpec(memory_space=pltpu.VMEM)
    early_rows = rounded_up(rows // 2, 16)
    anywhere = pl.BlockSpec(memory_space=pl.ANY)
    shapes = [
        ((cuts, early_rows, width), bf16),
        ((cuts, rows - early_rows, width), bf16),
        ((cuts, rows, width), bf16),
        ((here, 2, share, width), bf16),
        ((here, 2, share, width), bf16),
        ((members // 2, cut, 4 * local), bf16),
        ((cuts, 8, 128), f32),
    ]
    slab = (cuts, rows, width)
    vectors = [((width,), f32)] * 4
    scratch = [
        (inputs.shape, bf16),
        (cotangent.shape, bf16),
        *vectors,
        ((experts_all, width), f32),
        ((2, tokens), jnp.int32),
        ((2, tokens), jnp.int32),
        ((padded, width), f32),
        ((padded, width), f32),
        ((2, padded, width), bf16),
        ((padded, width), bf16),
        ((rows, width), bf16),
        (slab, bf16),
        ((2, 8, 256), f32),
        ((8, width), f32),
        ((3, local, width), bf16),
        ((cuts, local, width), bf16),
        ((2, cuts, ctx_rows // 2, 2 * local), bf16),
        ((ctx_rows, local), bf16),
        (expert_in.shape, bf16),
        (expert_out.shape, bf16),
        ((2, padded, width), bf16),
        ((padded, width), f32),
        ((padded, width), bf16),
        ((padded, width), f32),
        ((3, ctx_rows, local), bf16),
        ((heads, ctx_rows, ctx_rows), f32),
        (slab, bf16),
        (slab, bf16),
        (slab, bf16),
        (slab, bf16),
        (slab, bf16),
        (slab, bf16),
        (slab, bf16),
        (slab, bf16),
        (slab, bf16),
        (slab, bf16),
        ((rows, width), bf16),
        ((early_rows, width), bf16),
        ((rows - early_rows, width), bf16),
        ((8, 128), f32),
        ((8, 256), f32),
        ((8, 256), f32),
        ((cuts, 8, 256), f32),
        (slab, bf16),
        (slab, f32),
        ((cuts, rows, local), bf16),
        ((cuts, rows, local), bf16),
        ((2, here, 2, 2, share, width), bf16),
        ((here, 2, 2, share, width), bf16),
        ((2, members // 2, cut, 4 * local), bf16),
        ((members // 2, cut, 4 * local), bf16),
        ((cuts, early_rows, width), bf16),
        ((cuts, rows - early_rows, width), bf16),
        ((cuts, early_rows, width), bf16),
        ((cuts, rows - early_rows, width), bf16),
        ((8, width), f32),
        ((members, 8, 128), f32),
        ((members, 8, 128), f32),
        ((2, slots, width), bf16),
        ((here, 2 * depth, width), bf16),
        ((here, 2 * depth, width), bf16),
        ((here, 2 * depth, width), bf16),
        ((here, 2 * depth, width), bf16),
        ((2, slots, padded), bf16),
        ((2, slots, width), bf16),
    ]
    sems = [pltpu.SemaphoreType.DMA((n,)) for n in (20, 96, 96)]
    received = pl.pallas_call(
        functools.partial(block_kernel, (tokens, rows, cuts, experts_all, capacity, depth)),
        out_shape=[jax.ShapeDtypeStruct(*s) for s in shapes],
        in_specs=[anywhere] * 13,
        out_specs=[anywhere] * 7,
        scratch_shapes=[pltpu.VMEM(*s) for s in scratch] + sems,
        compiler_params=pltpu.CompilerParams(
            collective_id=0, has_side_effects=True, vmem_limit_bytes=56 << 20
        ),
        name="block",
    )(
        inputs,
        cotangent,
        first_gain,
        first_bias,
        second_gain,
        second_bias,
        router_weight.T,
        expert_ids.T,
        slot_index.T,
        jnp.swapaxes(attention_in, 1, 2),
        attention_out,
        expert_in,
        expert_out,
    )
    results = [
        ((tokens, width), f32),
        ((tokens, width), f32),
        ((1, cut), f32),
        ((1, cut), f32),
        ((3, cut, local), f32),
        ((local, cut), f32),
        ((1, cut), f32),
        ((1, cut), f32),
        ((experts_all, cut), f32),
        ((here, share, width), f32),
        ((here, share, width), f32),
    ]
    large = [results[i] for i in (0, 1, 4, 5, 9, 10)]
    out = pl.pallas_call(
        functools.partial(finish_kernel, (tokens, experts_all, local)),
        out_shape=[jax.ShapeDtypeStruct(*s) for s in results],
        in_specs=[anywhere] * 7,
        out_specs=[anywhere] * 2 + [vmem] * 2 + [anywhere] * 2 + [vmem] * 3 + [anywhere] * 2,
        scratch_shapes=[pltpu.VMEM(*s) for s in shapes + large]
        + [pltpu.SemaphoreType.DMA((n,)) for n in (7, 6)],
        compiler_params=pltpu.CompilerParams(vmem_limit_bytes=56 << 20),
        name="finish",
    )(*received)
    return (
        out[0],
        out[1],
        out[2].reshape(cut),
        out[3].reshape(cut),
        out[4],
        out[5],
        out[6].reshape(cut),
        out[7].reshape(cut),
        out[8].T,
        out[9],
        jnp.swapaxes(out[10], 1, 2),
    )


def solution(mesh):
    in_specs = (
        P(("dp", "expert"), None),
        P(),
        P(),
        P(None, None, "tensor"),
        P("tensor", None),
        P(),
        P(),
        P(),
        P("expert", None, "tensor"),
        P("expert", "tensor", None),
        P(("dp", "expert"), None),
        P(("dp", "expert"), None),
        P(("dp", "expert"), None),
    )
    out_specs = (
        P(("dp", "expert"), None),
        P(("dp", "expert"), None),
        P(("dp", "expert")),
        P(("dp", "expert")),
        P(None, ("dp", "expert"), "tensor"),
        P("tensor", ("dp", "expert")),
        P(("dp", "expert")),
        P(("dp", "expert")),
        P(("dp", "expert"), None),
        P("expert", "dp", "tensor"),
        P("expert", "tensor", "dp"),
    )
    return jax.shard_map(
        per_device, mesh=mesh, in_specs=in_specs, out_specs=out_specs, check_vma=False
    )
```

```python
import functools
import math

import jax
import jax.numpy as jnp
from jax import lax
from jax.experimental import pallas as pl
from jax.experimental.pallas import tpu as pltpu
from jax.sharding import PartitionSpec as P

HEAD_DIM = 64
SEQ = 197


EPS = 1e-06
GELU_C = math.sqrt(2.0 / math.pi)


def cut_along(shard, dim, devices):
    shape = shard.shape
    tiles = shard.reshape(*shape[:dim], devices, shape[dim] // devices, *shape[dim + 1 :])
    return jnp.moveaxis(tiles, dim, 0)


def sent_and_summed(shard, axis, dim):
    devices = lax.axis_size(axis)
    tiles = lax.all_to_all(cut_along(shard, dim, devices), axis, 0, 0, tiled=True)
    return jnp.sum(tiles.astype(jnp.float32), axis=0)


def sent_together(arrays, axis, dim, along):
    widths = [math.prod(a.shape[along:]) for a in arrays]
    both = jnp.concatenate(
        [a.reshape(*a.shape[:along], w) for a, w in zip(arrays, widths)], axis=along
    )
    out = sent_and_summed(both, axis, dim)
    tiles = jnp.split(out, [sum(widths[:k]) for k in range(1, len(widths))], axis=along)
    return tuple((b.reshape(*out.shape[:along], *a.shape[along:]) for a, b in zip(arrays, tiles)))


def normalize(values):
    centre = jnp.mean(values, axis=-1, keepdims=True)
    centred = values - centre
    spread = jnp.mean(centred * centred, axis=-1, keepdims=True)
    scale = lax.rsqrt(spread + EPS)
    return (centred * scale, scale)


def norm_back(grad_out, normed, scale, gain):
    scaled = grad_out * gain
    first_mean = jnp.mean(scaled, axis=-1, keepdims=True)
    second_mean = jnp.mean(scaled * normed, axis=-1, keepdims=True)
    return scale * (scaled - first_mean - normed * second_mean)


def gelu_parts(pre):
    inner = GELU_C * (pre + 0.044715 * pre * pre * pre)
    tangent = jnp.tanh(inner)
    value = 0.5 * pre * (1.0 + tangent)
    slope = 0.5 * (1.0 + tangent) + 0.5 * pre * (1.0 - tangent * tangent) * GELU_C * (
        1.0 + 3.0 * 0.044715 * pre * pre
    )
    return (value, slope)


MESH = pl.DeviceIdType.MESH


def greet(axes):
    barrier = pltpu.get_barrier_semaphore()
    peers = 0
    for axis in axes:
        devices = lax.axis_size(axis)
        me = lax.axis_index(axis)
        for k in range(1, devices):
            peer = lax.rem(me + k, devices)
            pl.semaphore_signal(barrier, inc=1, device_id={axis: peer}, device_id_type=MESH)
            peers += 1
    pl.semaphore_wait(barrier, peers)


def group_peer(k):
    owners = lax.axis_size("expert")
    members = lax.axis_size("dp") * owners
    me = lax.axis_index("dp") * owners + lax.axis_index("expert")
    peer = lax.rem(me + k, members)
    return {"dp": peer // owners, "expert": lax.rem(peer, owners)}


def greet_line_and_group(grouped):
    barrier = pltpu.get_barrier_semaphore()
    cuts = lax.axis_size("tensor")
    members = lax.axis_size("dp") * lax.axis_size("expert") if grouped else 1
    for k in range(1, cuts):
        peer = {"tensor": lax.rem(lax.axis_index("tensor") + k, cuts)}
        pl.semaphore_signal(barrier, inc=1, device_id=peer, device_id_type=MESH)
    for k in range(1, members):
        pl.semaphore_signal(barrier, inc=1, device_id=group_peer(k), device_id_type=MESH)
    pl.semaphore_wait(barrier, cuts + members - 2)


def group_copies(source, target, send_sem, recv_sem):
    owners = lax.axis_size("expert")
    members = lax.axis_size("dp") * owners
    me = lax.axis_index("dp") * owners + lax.axis_index("expert")
    copies = []
    for k in range(1, members):
        copy = pltpu.make_async_remote_copy(
            src_ref=source.at[lax.rem(me + k, members)],
            dst_ref=target.at[k],
            send_sem=send_sem.at[k],
            recv_sem=recv_sem.at[k],
            device_id=group_peer(k),
            device_id_type=MESH,
        )
        copy.start()
        copies.append(copy)
    target[0] = source[me]
    return copies


def ends_kernel(gather, *refs):
    source, group_source, target, group_target = refs[:4]
    send_sem, recv_sem, send_group, recv_group = refs[4:]
    devices = lax.axis_size("tensor")
    me = lax.axis_index("tensor")
    greet_line_and_group(True)
    copies = []
    for k in range(1, devices):
        peer = lax.rem(me + k, devices)
        copy = pltpu.make_async_remote_copy(
            src_ref=source if gather else source.at[peer],
            dst_ref=target.at[me] if gather else target.at[k],
            send_sem=send_sem.at[k],
            recv_sem=recv_sem.at[k],
            device_id={"tensor": peer},
            device_id_type=MESH,
        )
        copy.start()
        copies.append(copy)
    copies += group_copies(group_source, group_target, send_group, recv_group)
    if gather:
        target[me] = source[...]
    else:
        target[0] = source[me]
    for copy in copies:
        copy.wait()


def line_and_group(array, group_array, collective_id, gather):
    devices = lax.axis_size("tensor")
    members = group_array.shape[0]
    shape = (devices, *array.shape) if gather else array.shape
    return pl.pallas_call(
        functools.partial(ends_kernel, gather),
        out_shape=[
            jax.ShapeDtypeStruct(shape, array.dtype),
            jax.ShapeDtypeStruct(group_array.shape, group_array.dtype),
        ],
        in_specs=[pl.BlockSpec(memory_space=pltpu.VMEM)] * 2,
        out_specs=[pl.BlockSpec(memory_space=pltpu.VMEM)] * 2,
        scratch_shapes=[pltpu.SemaphoreType.DMA((n,)) for n in (devices, devices, members, members)],
        compiler_params=pltpu.CompilerParams(collective_id=collective_id, has_side_effects=True),
        name=f"ends{collective_id}",
    )(array, group_array)


def scatter_kernel(count, *refs):
    sources, targets = refs[:count], refs[count : 2 * count]
    send_sem, recv_sem = refs[2 * count :]
    devices = lax.axis_size("tensor")
    me = lax.axis_index("tensor")
    greet(("tensor",))
    copies = []
    for k in range(1, devices):
        peer = lax.rem(me + k, devices)
        for a in range(count):
            copy = pltpu.make_async_remote_copy(
                src_ref=sources[a].at[peer],
                dst_ref=targets[a].at[k],
                send_sem=send_sem.at[a, k],
                recv_sem=recv_sem.at[a, k],
                device_id={"tensor": peer},
                device_id_type=MESH,
            )
            copy.start()
            copies.append(copy)
    for a in range(count):
        targets[a][0] = sources[a][me]
    for copy in copies:
        copy.wait()


def scattered(arrays, collective_id):
    devices = lax.axis_size("tensor")
    count = len(arrays)
    return pl.pallas_call(
        functools.partial(scatter_kernel, count),
        out_shape=[jax.ShapeDtypeStruct(a.shape, a.dtype) for a in arrays],
        in_specs=[pl.BlockSpec(memory_space=pltpu.VMEM)] * count,
        out_specs=[pl.BlockSpec(memory_space=pltpu.VMEM)] * count,
        scratch_shapes=[
            pltpu.SemaphoreType.DMA((count, devices)),
            pltpu.SemaphoreType.DMA((count, devices)),
        ],
        compiler_params=pltpu.CompilerParams(collective_id=collective_id, has_side_effects=True),
        name=f"scatter{collective_id}",
    )(*arrays)


def gather_kernel(count, forward, *refs):
    sources, targets = refs[:count], refs[count : 2 * count]
    send_z, recv_z, send_x, recv_x = refs[2 * count :]
    devices = lax.axis_size("tensor")
    me = lax.axis_index("tensor")
    owners = lax.axis_size("expert") if forward else 1
    home = lax.axis_index("expert")
    greet(("tensor", "expert") if forward else ("tensor",))

    def across(a, k, source, place):
        copies = []
        for e in range(1, owners):
            copy = pltpu.make_async_remote_copy(
                src_ref=source,
                dst_ref=targets[a].at[e, place],
                send_sem=send_x.at[a, k, e],
                recv_sem=recv_x.at[a, k, e],
                device_id={"expert": lax.rem(home + e, owners)},
                device_id_type=MESH,
            )
            copy.start()
            copies.append(copy)
        return copies

    along = []
    for k in range(1, devices):
        peer = lax.rem(me + k, devices)
        for a in range(count):
            copy = pltpu.make_async_remote_copy(
                src_ref=sources[a],
                dst_ref=targets[a].at[0, me],
                send_sem=send_z.at[a, k],
                recv_sem=recv_z.at[a, k],
                device_id={"tensor": peer},
                device_id_type=MESH,
            )
            copy.start()
            along.append((a, k, copy))
    crossing = []
    for a in range(count):
        crossing += across(a, 0, sources[a], me)
    for a in range(count):
        targets[a][0, me] = sources[a][...]
    for a, k, copy in along:
        copy.wait()
        place = lax.rem(me + devices - k, devices)
        crossing += across(a, k, targets[a].at[0, place], place)
    for copy in crossing:
        copy.wait()


def gathered(arrays, collective_id, forward=False):
    devices = lax.axis_size("tensor")
    owners = lax.axis_size("expert") if forward else 1
    count = len(arrays)
    sems = [(count, devices)] * 2 + [(count, devices, owners)] * 2
    return pl.pallas_call(
        functools.partial(gather_kernel, count, forward),
        out_shape=[
            jax.ShapeDtypeStruct((owners, devices, *a.shape), a.dtype) for a in arrays
        ],
        in_specs=[pl.BlockSpec(memory_space=pltpu.VMEM)] * count,
        out_specs=[pl.BlockSpec(memory_space=pltpu.VMEM)] * count,
        scratch_shapes=[pltpu.SemaphoreType.DMA(s) for s in sems],
        compiler_params=pltpu.CompilerParams(collective_id=collective_id, has_side_effects=True),
        name=f"gather{collective_id}",
    )(*arrays)


def shifted(array, axis, offset):
    devices = lax.axis_size(axis)
    return lax.ppermute(array, axis, [(d, (d + offset) % devices) for d in range(devices)])


def from_owners(array):
    owners = lax.axis_size("expert")
    return jnp.stack([array] + [shifted(array, "expert", e) for e in range(1, owners)])


def to_owners(array):
    owners = lax.axis_size("expert")
    total = array[0].astype(jnp.float32)
    for e in range(1, owners):
        total = total + shifted(array[e], "expert", owners - e).astype(jnp.float32)
    return total


def rounded_up(value, multiple):
    return -(-value // multiple) * multiple


def experts_kernel(
    experts_all,
    slot_ref,
    spot_ref,
    second_ref,
    cot_ref,
    router_ref,
    in_ref,
    out_ref,
    mixed_ref,
    back_ref,
    share_ref,
    route_ref,
    cut_ref,
    placing_ref,
    gated_ref,
    low_ref,
    grad_ref,
):
    bf16, f32 = jnp.bfloat16, jnp.float32
    exact = lax.Precision.HIGHEST
    owners, padded, _ = second_ref.shape
    experts_here = in_ref.shape[0]
    lanes = router_ref.shape[1]
    depth = placing_ref.shape[2]

    def dot(a, b, a_dim, b_dim, precision=None):
        return lax.dot_general(
            a, b, (((a_dim,), (b_dim,)), ((), ())), precision=precision, preferred_element_type=f32
        )

    column = lax.broadcasted_iota(jnp.int32, (padded, lanes), 1)
    for o in range(owners):
        logits = dot(second_ref[o].astype(f32), router_ref[...], 1, 0, exact)
        logits = jnp.where(column < experts_all, logits, -1e30)
        lifted = jnp.exp(logits - jnp.max(logits, axis=-1, keepdims=True))
        lifted = jnp.where(column < experts_all, lifted, 0.0)
        route_ref[o] = lifted / jnp.sum(lifted, axis=-1, keepdims=True)
    slot = lax.broadcasted_iota(jnp.int32, (depth, padded), 0)
    for k in range(experts_here):
        gates, received, slotted = [], [], []
        for o in range(owners):
            picks = slot == slot_ref[k, o][None, :]
            placing = jnp.where(picks, 1.0, 0.0)
            low = placing.astype(bf16)
            placing_ref[k, o] = low
            chances = dot(placing, route_ref[o], 1, 0, exact)
            gates.append(jnp.sum(chances * spot_ref[k][None, :], axis=-1, keepdims=True))
            received.append(dot(low, second_ref[o], 1, 0).astype(bf16))
            slotted.append(dot(low, cot_ref[o], 1, 0))
        gate = jnp.concatenate(gates)
        received = jnp.concatenate(received)
        slotted = jnp.concatenate(slotted)
        y_grad = (gate * slotted).astype(bf16)
        value, slope = gelu_parts(dot(received, in_ref[k], 1, 0))
        hidden = value.astype(bf16)
        partial_y = dot(hidden, out_ref[k], 1, 0)
        gated_ref[k] = (gate * partial_y).astype(bf16)
        slot_grad = jnp.sum(slotted * partial_y, axis=-1, keepdims=True)
        grad_ref[k] = slot_grad * spot_ref[k][None, :]
        pre_grad = (dot(y_grad, out_ref[k], 1, 1) * slope).astype(bf16)
        low_ref[k] = dot(pre_grad, in_ref[k], 1, 1).astype(bf16)
        in_grad = dot(received, pre_grad, 0, 0).astype(bf16)
        out_grad = dot(y_grad, hidden, 0, 0).astype(bf16)
        blocks, _, _, share, _ = cut_ref.shape
        for d in range(blocks):
            cut_ref[d, 0, k] = in_grad[d * share : (d + 1) * share]
            cut_ref[d, 1, k] = out_grad[d * share : (d + 1) * share]
    for o in range(owners):
        span = pl.ds(o * depth, depth)
        here = range(experts_here)
        mixed_ref[o] = sum(
            dot(placing_ref[k, o], gated_ref[k, span], 0, 0) for k in here
        ).astype(bf16)
        back_ref[o] = sum(dot(placing_ref[k, o], low_ref[k, span], 0, 0) for k in here).astype(bf16)
        share_ref[o] = sum(
            dot(placing_ref[k, o].astype(f32), grad_ref[k, span], 0, 0, exact) for k in here
        )


def experts_block(slots, spot, second, cot, router, expert_in, expert_out, experts_all, depth):
    owners, padded, width = second.shape
    here, _, hidden = expert_in.shape
    lanes = router.shape[1]
    blocks = lax.axis_size("dp")
    bf16, f32 = jnp.bfloat16, jnp.float32
    shapes = [
        ((owners, padded, width), bf16),
        ((owners, padded, width), bf16),
        ((owners, padded, lanes), f32),
        ((owners, padded, lanes), f32),
        ((blocks, 2, here, width // blocks, hidden), bf16),
    ]
    return pl.pallas_call(
        functools.partial(experts_kernel, experts_all),
        out_shape=[jax.ShapeDtypeStruct(*s) for s in shapes],
        in_specs=[pl.BlockSpec(memory_space=pltpu.VMEM)] * 7,
        out_specs=[pl.BlockSpec(memory_space=pltpu.VMEM)] * 5,
        scratch_shapes=[
            pltpu.VMEM((here, owners, depth, padded), bf16),
            pltpu.VMEM((here, owners * depth, width), bf16),
            pltpu.VMEM((here, owners * depth, width), bf16),
            pltpu.VMEM((here, owners * depth, lanes), f32),
        ],
        compiler_params=pltpu.CompilerParams(
            vmem_limit_bytes=(32 << 20) if owners <= 2 else (60 << 20)
        ),
        name="experts",
    )(slots, spot, second, cot, router, expert_in, expert_out)


def lane_dot(a, b, a_dim, b_dim, precision=None):
    return lax.dot_general(
        a, b, (((a_dim,), (b_dim,)), ((), ())), precision=precision, preferred_element_type=jnp.float32
    )


def block_kernel(dims, *refs):
    tokens, rows, cuts, experts_all, capacity, depth = dims
    bf16, f32 = jnp.bfloat16, jnp.float32
    exact = lax.Precision.HIGHEST
    given = refs[:9]
    (w_hbm, wo_hbm, ein_hbm, eout_hbm) = refs[9:13]
    (final_a, final_b, layers, e_sum, g_parts, small_parts) = refs[13:19]
    (
        x_in, cot_in, gain1, bias1, gain2, bias2, router_in, ids_in, slot_in, x32, c32,
        xs, cots, cot_out, cot_far, tgt, rt, w_in, wo, ctx, ctx_own, ein, eout, sec, resid, first, n1,
        qkv, probs, back_out, back_in, back_home, back_send, back_got,
        mix_out, mix_in, mix_part, mix_pair, mix_got,
        end_layer, end_a, end_b, small_sum, share_out, share_in, share_all, low, lg, cg_out, cg_in, ebuf, e_got, e_peer, e_total, gbuf, g_got, first_a, first_b, first_got_a, first_got_b,
        small, small_send, small_got, lowers, hid, pgr, rec, ygr, plc, gated,
        load, ss, rs,
    ) = refs[19:]
    d, e, z = lax.axis_index("dp"), lax.axis_index("expert"), lax.axis_index("tensor")
    core, y = lax.rem(d, 2), d // 2
    padded = rows * cuts
    width = x_in.shape[1]
    wide = lambda vector: vector[...][None, :]
    local = wo_hbm.shape[0]
    heads = local // HEAD_DIM
    quarter = local // 4
    here = ein_hbm.shape[0]
    ctx_rows = qkv.shape[1]
    ctx_half = ctx_rows // 2
    other_x = {"expert": 1 - e}
    other_core = {"dp": y * 2 + 1 - core}
    other_y = {"dp": (1 - y) * 2 + core}
    diagonal = {"dp": (1 - y) * 2 + core, "expert": 1 - e}
    along = [(k, lax.rem(z + k, cuts)) for k in range(1, cuts)]
    near = z + 1 - 2 * lax.rem(z, 2)
    far = lax.rem(z + 2, cuts)
    last = lax.rem(near + 2, cuts)
    count = [0]
    pending = []

    def send(source, target, device):
        i = count[0]
        count[0] += 1
        copy = pltpu.make_async_remote_copy(
            src_ref=source,
            dst_ref=target,
            send_sem=ss.at[i],
            recv_sem=rs.at[i],
            device_id=device,
            device_id_type=MESH,
        )
        copy.start()
        pending.append(copy)
        return copy

    def spread(source, slab):
        return [send(source, slab(z), {"tensor": peer}) for peer in (near, far)]

    def passed_on(copies, slab):
        copies[1].wait_recv()
        copies.append(send(slab(far), slab(far), {"tensor": near}))

    loads = [
        pltpu.make_async_copy(w_hbm, w_in, load.at[0]),
        pltpu.make_async_copy(wo_hbm, wo.at[z], load.at[1]),
        pltpu.make_async_copy(ein_hbm, ein, load.at[2]),
        pltpu.make_async_copy(eout_hbm, eout, load.at[3]),
    ]
    here_now = (x_in, cot_in, gain1, bias1, gain2, bias2, router_in, ids_in, slot_in)
    early = [
        pltpu.make_async_copy(source, target, load.at[4 + i])
        for i, (source, target) in enumerate(zip(given, here_now))
    ]
    for copy in early + loads:
        copy.start()
    barrier = pltpu.get_barrier_semaphore()
    others = [
        {"dp": (y if same_y else 1 - y) * 2 + (core if same_core else 1 - core),
         "expert": e if same_e else 1 - e}
        for same_y in (1, 0) for same_core in (1, 0) for same_e in (1, 0)
    ][1:]
    greeted = others + [{"tensor": p} for _, p in along]
    for peer in greeted:
        pl.semaphore_signal(barrier, inc=1, device_id=peer, device_id_type=MESH)

    for copy in early:
        copy.wait()
    edge = tokens // 8 * 8
    for whole, part in ((x32, x_in), (c32, cot_in)):
        whole[edge:padded] = jnp.zeros((padded - edge, width), f32)
        whole[0:tokens] = part[...].astype(f32)
    xs[0] = x32[...].astype(bf16)
    xs[1, ctx_rows:padded] = jnp.zeros((padded - ctx_rows, width), bf16)
    cots[...] = c32[...].astype(bf16)
    cot_rows = c32[pl.ds(pl.multiple_of(z * rows, 8), rows)]
    cot_out[...] = cot_rows.astype(bf16)
    x_full = x32[...]
    tgt[0] = jnp.full(tgt.shape[1:], -1.0, f32)
    slot = slot_in[...]
    tgt[0, 0:2, 0:tokens] = jnp.where(slot < capacity, ids_in[...] * capacity + slot, -1).astype(f32)
    rt[...] = jnp.zeros_like(rt)
    rt[0:experts_all] = router_in[...]

    pl.semaphore_wait(barrier, len(greeted))
    loads[1].wait()

    def wo_part(c, part):
        return wo.at[c, pl.ds(pl.multiple_of(part * quarter, 16), quarter)]

    cot_copy = send(cot_out, cot_far.at[z], other_x)
    mine_of_wo = lambda c: wo_part(c, d)
    wo_along = spread(wo_part(z, d), mine_of_wo)
    x_copy = send(xs.at[0, pl.ds(0, ctx_rows)], xs.at[1, pl.ds(0, ctx_rows)], other_x)
    tgt_copy = send(tgt.at[0], tgt.at[1], other_x)

    normed, _ = normalize(x_full)
    n1[...] = normed
    first_low = (normed * wide(gain1) + wide(bias1)).astype(bf16)
    first[...] = first_low
    loads[0].wait()
    for which in range(3):
        qkv[which] = lane_dot(first_low[:ctx_rows], w_in[which], 1, 1).astype(bf16)
    head = lax.broadcasted_iota(jnp.int32, (ctx_rows, local), 1) // HEAD_DIM
    masks = [jnp.where(head == h, 1.0, 0.0) for h in range(heads)]
    key_at = lax.broadcasted_iota(jnp.int32, (ctx_rows, ctx_rows), 1)
    scaling = HEAD_DIM ** (-0.5)

    def of_head(matrix, h):
        return matrix * masks[h].astype(matrix.dtype)

    query, keys, values = qkv[0], qkv[1], qkv[2]
    total = jnp.zeros((ctx_rows, local), f32)
    for h in range(heads):
        scores = lane_dot(of_head(query, h), keys, 1, 1) * scaling
        scores = jnp.where(key_at < tokens, scores, -1e30)
        peak = jnp.max(scores, axis=-1, keepdims=True)
        logsum = peak + jnp.log(jnp.sum(jnp.exp(scores - peak), axis=-1, keepdims=True))
        chance = jnp.exp(scores - logsum)
        probs[h] = chance
        total += lane_dot(chance.astype(bf16), of_head(values, h), 1, 0)
    ctx_own[...] = total.astype(bf16)
    ctx[0, z] = jnp.concatenate([total[:ctx_half], total[ctx_half:]], axis=1).astype(bf16)

    near_ctx = lambda c: ctx.at[0, c]
    ctx_along = spread(ctx.at[0, z], near_ctx)
    ctx_across = [(z, send(ctx.at[0, z], ctx.at[1, z], other_x))]

    far_row = (1 - y) * 2 + core
    wo_row, wo_core = [], []

    def wo_on(place):
        wo_row.append((place, send(wo_part(place, d), wo_part(place, d), other_y)))
        wo_core.append(send(wo_part(place, d), wo_part(place, d), other_core))

    def ctx_on(place):
        ctx_across.append((place, send(ctx.at[0, place], ctx.at[1, place], other_x)))

    wo_along[0].wait_recv()
    wo_on(near)
    passed_on(wo_along, mine_of_wo)
    wo_on(far)
    ctx_along[0].wait_recv()
    ctx_on(near)
    passed_on(ctx_along, near_ctx)
    ctx_on(far)
    wo_along[2].wait_recv()
    wo_on(last)
    cot_copy.wait_recv()
    far_cot = lambda c: cot_far.at[c]
    cot_far_along = spread(cot_far.at[z], far_cot)
    ctx_along[2].wait_recv()
    ctx_on(last)
    for place, copy in wo_row:
        copy.wait_recv()
        wo_core.append(send(wo_part(place, far_row), wo_part(place, far_row), other_core))
    for copy in wo_core:
        copy.wait_recv()

    split = rt[...]
    splits = []
    for _ in range(3):
        piece = split.astype(bf16)
        splits.append(piece.astype(f32))
        split = split - piece.astype(f32)
    router_low = jnp.concatenate(splits).astype(bf16)
    lanes8 = rt.shape[0]
    expert_row = lax.broadcasted_iota(jnp.int32, (lanes8, padded), 0)
    base = e * here

    def forward(o):
        halves = [jnp.zeros((ctx_half, width), f32) for _ in range(2)]
        for c in range(cuts):
            both = ctx[o, c]
            for n in range(2):
                halves[n] += lane_dot(both[:, n * local : (n + 1) * local], wo[c], 1, 0)
        attended = jnp.concatenate([*halves, jnp.zeros((padded - ctx_rows, width), f32)])
        res = xs[o].astype(f32) + attended
        normed2, _ = normalize(res)
        second = (normed2 * wide(gain2) + wide(bias2)).astype(bf16)
        sec[o] = second
        parts = lane_dot(router_low, second, 1, 1)
        logits = parts[:lanes8] + parts[lanes8 : 2 * lanes8] + parts[2 * lanes8 :]
        logits = jnp.where(expert_row < experts_all, logits, -1e30)
        lifted = jnp.exp(logits - jnp.max(logits, axis=0, keepdims=True))
        lifted = jnp.where(expert_row < experts_all, lifted, 0.0)
        return res, lifted / jnp.sum(lifted, axis=0, keepdims=True)

    slot_at = lax.broadcasted_iota(jnp.int32, (depth, padded), 0)

    def picks_of(o, k):
        offset = tgt[o, 0:2, 0:padded].astype(jnp.int32) - (base + k) * capacity
        chosen = jnp.where((offset >= 0) & (offset < capacity), offset, -1)
        return slot_at == jnp.max(chosen, axis=0, keepdims=True)

    def place(o, route):
        placed, gates = [], []
        for k in range(here):
            picks = picks_of(o, k)
            placed.append(jnp.where(picks, 1.0, 0.0))
            row = jnp.sum(jnp.where(expert_row == base + k, route, 0.0), axis=0, keepdims=True)
            gates.append(jnp.sum(jnp.where(picks, row, 0.0), axis=-1, keepdims=True))
        low_place = jnp.concatenate(placed).astype(bf16)
        plc[o] = low_place
        gate = jnp.concatenate(gates)
        received = lane_dot(low_place, sec[o], 1, 0).astype(bf16)
        return gate, received

    res, route_own = forward(0)
    resid[...] = res
    tgt_copy.wait_recv()
    x_copy.wait_recv()
    passed_on(cot_far_along, far_cot)
    own = place(0, route_own)
    for _, copy in ctx_across:
        copy.wait_recv()
    _, route_far = forward(1)
    away = place(1, route_far)
    loads[2].wait()
    loads[3].wait()

    def joined(both, k):
        span = slice(k * depth, (k + 1) * depth)
        return jnp.concatenate([part[span] for part in both])

    def chunked(target, matrix):
        for c in range(cuts):
            target[c] = matrix[c * rows : (c + 1) * rows].astype(target.dtype)

    fore = []
    for k in range(here):
        received = joined((own[1], away[1]), k)
        value, slope = gelu_parts(lane_dot(received, ein[k], 1, 0))
        hidden = value.astype(bf16)
        rec[k], hid[k] = received, hidden
        partial_y = lane_dot(hidden, eout[k], 1, 0)
        gate = joined((own[0], away[0]), k)
        fore.append((gate, slope, partial_y))
        weighted = (gate * partial_y).astype(bf16)
        for o in range(2):
            gated[o, k * depth : (k + 1) * depth] = weighted[o * depth : (o + 1) * depth]
    mix_along = []
    for o in range(2):
        chunked(mix_part.at[o], lane_dot(plc[o], gated[o], 0, 0))
        mix_along.append(
            [
                send(mix_part.at[o, last], mix_got.at[o, 1], {"tensor": near}),
                send(mix_part.at[o, near], mix_got.at[o, 0], {"tensor": near}),
            ]
        )
    for copy in cot_far_along[::2]:
        copy.wait_recv()
    cot_all = jnp.concatenate([cot_far[c].astype(f32) for c in range(cuts)]).astype(bf16)
    slotted_both = [lane_dot(plc[o], cot, 1, 0) for o, cot in enumerate((cots[...], cot_all))]
    shares = [jnp.zeros((lanes8, padded), f32) for _ in range(2)]
    for k in range(here):
        gate, slope, partial_y = fore[k]
        slotted = joined(slotted_both, k)
        y_grad = (gate * slotted).astype(bf16)
        pre_grad = (lane_dot(y_grad, eout[k], 1, 1) * slope).astype(bf16)
        lowered = lane_dot(pre_grad, ein[k], 1, 1).astype(bf16)
        slot_grad = jnp.sum(slotted * partial_y, axis=-1, keepdims=True)
        ygr[k], pgr[k] = y_grad, pre_grad
        for o in range(2):
            span = slice(o * depth, (o + 1) * depth)
            lowers[o, k * depth : (k + 1) * depth] = lowered[span]
            row = jnp.sum(
                jnp.where(picks_of(o, k), slot_grad[span], 0.0), axis=0, keepdims=True
            )
            shares[o] += jnp.where(expert_row == base + k, row, 0.0)

    chunked(back_out, lane_dot(plc[1], lowers[1], 0, 0))
    order = [lax.rem(z + k, cuts) for k in (2, 1, 3, 0)]
    back_across = [send(back_out.at[c], back_in.at[c], other_x) for c in order[:2]]
    share_out[...] = jnp.zeros_like(share_out)
    share_out[:, 0:padded] = shares[1]
    share_across = send(share_out, share_in, other_x)
    def expert_grads(k):
        in_grad = lane_dot(rec[k], pgr[k], 0, 0).astype(bf16)
        out_grad = lane_dot(ygr[k], hid[k], 0, 0).astype(bf16)
        share = width // 4
        for p in range(4):
            span = slice(p * share, (p + 1) * share)
            ebuf[p % 2, k, p // 2, 0] = in_grad[span]
            ebuf[p % 2, k, p // 2, 1] = out_grad[span]
        return send(ebuf.at[1 - core, k], e_got.at[k], other_core)

    e_row = []

    def e_on(k):
        e_core[k].wait_recv()
        for yy in range(2):
            for a in range(2):
                both = ebuf[core, k, yy, a].astype(f32) + e_got[k, yy, a].astype(f32)
                ebuf[core, k, yy, a] = both.astype(bf16)
        e_row.append(send(ebuf.at[core, k, 1 - y], e_peer.at[k], other_y))

    e_core = [expert_grads(k) for k in range(here)]
    chunked(back_home, lane_dot(plc[0], lowers[0], 0, 0))
    for o in range(2):
        mix_along[o][0].wait_recv()
        mix_pair[o] = (mix_part[o, far].astype(f32) + mix_got[o, 1].astype(f32)).astype(bf16)
        mix_along[o].append(send(mix_pair.at[o], mix_got.at[o, 2], {"tensor": far}))
    e_on(0)
    share_across.wait_recv()
    share_all[0] = share_in[...]
    share_all[0, :, 0:padded] += shares[0]
    share_along = [send(share_all.at[0], share_all.at[k], {"tensor": peer}) for k, peer in along]
    back_along = []
    for j, c in enumerate(order):
        back_across[j].wait_recv()
        if j < 2:
            back_across.append(send(back_out.at[order[j + 2]], back_in.at[order[j + 2]], other_x))
        back_send[c] = (back_home[c].astype(f32) + back_in[c].astype(f32)).astype(bf16)
        if j < 3:
            k = (2, 1, 3)[j]
            back_along.append(send(back_send.at[c], back_got.at[k], {"tensor": c}))
    mixed = []
    for o in range(2):
        for copy in mix_along[o][1:]:
            copy.wait_recv()
        mixed.append(
            mix_part[o, z].astype(f32) + mix_got[o, 0].astype(f32) + mix_got[o, 2].astype(f32)
        )
    mix_out[...] = mixed[1].astype(bf16)
    mix_across = send(mix_out, mix_in, other_x)
    e_on(1)

    for copy in share_along:
        copy.wait_recv()
    route_grad = (share_all[0] + share_all[1] + share_all[2] + share_all[3])[:, 0:padded]
    logit_grad = route_own * (route_grad - jnp.sum(route_own * route_grad, axis=0, keepdims=True))
    chunked(lg, lane_dot(logit_grad, rt[...], 0, 0, exact))
    router_grad = lane_dot(logit_grad, sec[0].astype(f32), 1, 0, exact)
    res_rows = resid[pl.ds(pl.multiple_of(z * rows, 8), rows)]
    normed2, scale2 = normalize(res_rows)
    for copy in back_along:
        copy.wait_recv()
    back = back_send[z].astype(f32)
    for k, _ in along:
        back += back_got[k].astype(f32)
    second_grad = back + lg[z]
    resid_grad = cot_rows + norm_back(second_grad, normed2, scale2, wide(gain2))
    lg[z] = resid_grad
    low_rows = resid_grad.astype(bf16)
    low[z] = low_rows
    for c in range(cuts):
        cg_out[c] = lane_dot(low_rows, wo[c], 1, 1).astype(bf16)
    cg_along = [send(cg_out.at[peer], cg_in.at[z], {"tensor": peer}) for _, peer in along]
    cg_in[z] = cg_out[z]

    small[...] = jnp.zeros_like(small)
    small[0:experts_all] = jnp.where(z == 0, router_grad[:experts_all], 0.0)
    small[experts_all : experts_all + 1] = jnp.sum(second_grad * normed2, axis=0, keepdims=True)
    small[experts_all + 1 : experts_all + 2] = jnp.sum(second_grad, axis=0, keepdims=True)
    slab_low = lambda c: low.at[c]
    low_along = spread(low.at[z], slab_low)
    mix_across.wait_recv()
    layer_rows = resid[pl.ds(pl.multiple_of(z * rows, 8), rows)] + mixed[0]
    end_layer[...] = (layer_rows + mix_in[...].astype(f32)).astype(bf16)
    slab_layer = lambda c: layers.at[c]
    layer_along = spread(end_layer, slab_layer)

    for copy in cg_along:
        copy.wait_recv()
    ctx_grad = jnp.concatenate([cg_in[c].astype(f32) for c in range(cuts)])[:ctx_rows].astype(bf16)
    own_ctx = ctx_own[...]
    product = ctx_grad.astype(f32) * own_ctx.astype(f32)
    query_grad = jnp.zeros((ctx_rows, local), f32)
    keys_grad = jnp.zeros((ctx_rows, local), f32)
    values_grad = jnp.zeros((ctx_rows, local), f32)
    query, keys, values = qkv[0], qkv[1], qkv[2]
    for h in range(heads):
        chance = probs[h]
        grad_h = of_head(ctx_grad, h)
        delta = jnp.sum(of_head(product, h), axis=-1, keepdims=True)
        values_grad += lane_dot(chance.astype(bf16), grad_h, 0, 0)
        score_grad = (chance * (lane_dot(grad_h, values, 1, 1) - delta) * scaling).astype(bf16)
        query_grad += lane_dot(score_grad, of_head(keys, h), 1, 0)
        keys_grad += lane_dot(score_grad, of_head(query, h), 0, 0)
    grads = [g.astype(bf16) for g in (query_grad, keys_grad, values_grad)]
    passed_on(low_along, slab_low)
    passed_on(layer_along, slab_layer)
    partial = sum(lane_dot(grads[k], w_in[k], 1, 0) for k in range(3))
    partial = jnp.concatenate([partial, jnp.zeros((padded - ctx_rows, width), f32)])
    early_rows = first_a.shape[1]
    for c in range(cuts):
        first_a[c] = partial[c * rows : c * rows + early_rows].astype(bf16)
        first_b[c] = partial[c * rows + early_rows : (c + 1) * rows].astype(bf16)
    turns = [along[1], along[0], along[2]]
    first_along = [
        [send(source.at[peer], target.at[k], {"tensor": peer}) for k, peer in turns]
        for source, target in ((first_a, first_got_a), (first_b, first_got_b))
    ]
    small[experts_all + 2 : experts_all + 3] = jnp.sum(partial * n1[...], axis=0, keepdims=True)
    small[experts_all + 3 : experts_all + 4] = jnp.sum(partial, axis=0, keepdims=True)
    members = small_send.shape[0]
    cut = width // members
    for m in range(members):
        small_send[m, :, 0:cut] = small[:, m * cut : (m + 1) * cut]
    me = d * 2 + e
    small_across = [
        send(
            small_send.at[device["dp"] * 2 + device["expert"]], small_got.at[k], device
        )
        for k, device in enumerate(others)
    ]
    top = first[0:ctx_rows]
    results = [lane_dot(top, g, 0, 0).astype(bf16) for g in grads]
    for copy in low_along[::2]:
        copy.wait_recv()
    resid_low = jnp.concatenate([low[c].astype(f32) for c in range(cuts)])
    results.append(lane_dot(resid_low[:ctx_rows].astype(bf16), own_ctx, 0, 0).astype(bf16))
    for m in range(members):
        for k in range(4):
            gbuf[(m // 2) % 2, (m // 4) * 2 + m % 2, :, k * local : (k + 1) * local] = results[k][
                m * cut : (m + 1) * cut
            ]
    g_core = send(gbuf.at[1 - core], g_got, other_core)

    kept = []

    def keep(source, target):
        copy = pltpu.make_async_copy(source, target, load.at[13 + len(kept)])
        copy.start()
        kept.append(copy)

    keep(end_layer, layers.at[z])
    g_core.wait_recv()
    for m in range(members // 2):
        gbuf[core, m] = (gbuf[core, m].astype(f32) + g_got[m].astype(f32)).astype(bf16)
    mine = y * 2 + e
    g_across = [
        send(gbuf.at[core, place_], g_parts.at[k], device)
        for k, place_, device in [
            (1, y * 2 + 1 - e, other_x),
            (2, (1 - y) * 2 + e, other_y),
            (3, (1 - y) * 2 + 1 - e, diagonal),
        ]
    ]
    keep(gbuf.at[core, mine], g_parts.at[0])
    for copy in small_across:
        copy.wait_recv()
    added = small_send[me]
    for k in range(members - 1):
        added += small_got[k]
    small_sum[...] = added
    keep(small_sum, small_parts.at[0])
    small_along = [
        send(small_sum, small_parts.at[k], {"tensor": peer}) for k, peer in along
    ]

    normed_rows, scale_rows = normalize(x32[pl.ds(pl.multiple_of(z * rows, 8), rows)])
    base_grad = lg[z]
    final_along = []
    for part, (sent, got, end, final) in enumerate(
        [(first_a, first_got_a, end_a, final_a), (first_b, first_got_b, end_b, final_b)]
    ):
        span = slice(0, early_rows) if part == 0 else slice(early_rows, rows)
        for copy in first_along[part]:
            copy.wait_recv()
        first_grad = sent[z].astype(f32)
        for k, _ in along:
            first_grad += got[k].astype(f32)
        grad_rows = base_grad[span] + norm_back(
            first_grad, normed_rows[span], scale_rows[span], wide(gain1)
        )
        end[...] = grad_rows.astype(bf16)
        final_along += [send(end, final.at[z], {"tensor": peer}) for _, peer in along]
        keep(end, final.at[z])
    for k in range(here):
        e_row[k].wait_recv()
        for a in range(2):
            e_total[a, k] = ebuf[core, k, y, a].astype(f32) + e_peer[k, a].astype(f32)
    keep(e_total, e_sum)
    for copy in kept:
        copy.wait()
    for copy in layer_along[::2] + final_along + g_across + small_along:
        copy.wait_recv()
    for copy in pending:
        copy.wait_send()


def finish_kernel(dims, *refs):
    tokens, experts_all, local = dims
    f32 = jnp.float32
    given = refs[:6]
    layer_out, grad_out, gain1, bias1, att_in_out, att_out_out, gain2, bias2, router = refs[6:15]
    in_out, out_out = refs[15:17]
    final_a, final_b, layers, e_sum, g_parts, small_parts = held = refs[17:23]
    layer, grad, att_in, att_out = refs[23:27]
    load, store = refs[27:]
    cuts = layers.shape[0]
    cut = gain1.shape[1]
    loads = [
        pltpu.make_async_copy(given[i], held[i], load.at[i]) for i in range(6)
    ]
    stores = []

    def keep(source, target):
        copy = pltpu.make_async_copy(source, target, store.at[len(stores)])
        copy.start()
        stores.append(copy)

    for i in (3, 2, 0, 1, 4, 5):
        loads[i].start()
    loads[3].wait()
    keep(e_sum.at[0], in_out)
    keep(e_sum.at[1], out_out)
    loads[2].wait()
    whole = jnp.concatenate([layers[c].astype(f32) for c in range(cuts)])
    layer[...] = whole[:tokens]
    keep(layer, layer_out)
    loads[0].wait()
    loads[1].wait()
    whole = jnp.concatenate(
        [part[c].astype(f32) for c in range(cuts) for part in (final_a, final_b)]
    )
    grad[...] = whole[:tokens]
    keep(grad, grad_out)
    loads[4].wait()
    parts = sum(g_parts[k].astype(f32) for k in range(g_parts.shape[0]))
    for k in range(3):
        att_in[k] = parts[:, k * local : (k + 1) * local]
    keep(att_in, att_in_out)
    att_out[...] = parts[:, 3 * local :].T
    keep(att_out, att_out_out)
    loads[5].wait()
    totals = sum(small_parts[k] for k in range(cuts))[:, :cut]
    router[...] = totals[:experts_all]
    for i, target in enumerate((gain2, bias2, gain1, bias1)):
        target[...] = totals[experts_all + i : experts_all + i + 1]
    for copy in stores:
        copy.wait()


def per_device_general(
    inputs,
    first_gain,
    first_bias,
    attention_in,
    attention_out,
    second_gain,
    second_bias,
    router_weight,
    expert_in,
    expert_out,
    expert_ids,
    slot_index,
    cotangent,
):
    bf16, f32 = jnp.bfloat16, jnp.float32
    tokens_here = inputs.shape[0]
    model_width = inputs.shape[1]
    images = tokens_here // SEQ
    local_width = attention_in.shape[2]
    local_heads = local_width // HEAD_DIM
    owners = lax.axis_size("expert")
    cuts = lax.axis_size("tensor")
    experts_here = expert_in.shape[0]
    experts_all = experts_here * owners
    capacity = (2 * tokens_here - 1) // experts_all
    scaling = HEAD_DIM ** (-0.5)
    rows = rounded_up(rounded_up(tokens_here, cuts) // cuts, 8)
    padded = rows * cuts
    lanes = rounded_up(experts_all, 128)
    piece = lax.axis_index("tensor")

    def split_heads(matrix):
        return matrix.reshape(images, SEQ, local_heads, HEAD_DIM)

    def pad_rows(matrix, value=0):
        return jnp.pad(
            matrix, ((0, padded - tokens_here), (0, 0)), constant_values=value
        )

    def my_rows(matrix):
        return lax.dynamic_slice_in_dim(pad_rows(matrix), piece * rows, rows, 0)

    target = jnp.where(slot_index < capacity, expert_ids * capacity + slot_index, -1)
    target_all = from_owners(pad_rows(target, -1).astype(f32).T)
    cot_all = from_owners(pad_rows(cotangent))

    x_full = inputs.astype(f32)
    normed1, scale1 = normalize(x_full)
    first = (normed1 * first_gain + first_bias).astype(bf16)
    project = [
        jnp.dot(first, attention_in[which], preferred_element_type=f32).astype(bf16)
        for which in range(3)
    ]
    query_h, keys_h, values_h = [split_heads(part) for part in project]
    scores = jnp.einsum("iqhd,ikhd->ihqk", query_h, keys_h, preferred_element_type=f32) * scaling
    peak = jnp.max(scores, axis=-1, keepdims=True)
    logsum = peak[..., 0] + jnp.log(jnp.sum(jnp.exp(scores - peak), axis=-1))
    probs = jnp.exp(scores - logsum[..., None])
    weights = probs.astype(bf16)
    context_h = jnp.einsum(
        "ihqk,ikhd->iqhd", weights, values_h, preferred_element_type=f32
    ).astype(bf16)
    context = context_h.reshape(tokens_here, local_width)
    partial_attn = jnp.dot(pad_rows(context), attention_out, preferred_element_type=f32)
    (attn_parts,) = scattered([partial_attn.astype(bf16).reshape(cuts, rows, model_width)], 1)

    attended = jnp.sum(attn_parts.astype(f32), axis=0)
    resid = my_rows(inputs).astype(f32) + attended
    normed2, scale2 = normalize(resid)
    second = (normed2 * second_gain + second_bias).astype(bf16)
    (second_all,) = gathered([second], 2, forward=True)

    base = lax.axis_index("expert") * experts_here
    experts = base + jnp.arange(experts_here, dtype=jnp.int32)
    offset = target_all.astype(jnp.int32)[None] - (experts * capacity)[:, None, None, None]
    slots = jnp.max(jnp.where((offset >= 0) & (offset < capacity), offset, -1), axis=2)
    spot = (experts[:, None] == jnp.arange(lanes, dtype=jnp.int32)).astype(f32)
    mixed, back, share, route_all, expert_cuts = experts_block(
        slots,
        spot,
        second_all.reshape(owners, padded, model_width),
        cot_all,
        jnp.pad(router_weight, ((0, 0), (0, lanes - experts_all))),
        expert_in,
        expert_out,
        experts_all,
        rounded_up(capacity, 16),
    )
    route = lax.dynamic_slice_in_dim(route_all[0], piece * rows, rows, 0)[:, :experts_all]
    mixed_home = to_owners(mixed)
    back_home = to_owners(back)
    route_home = to_owners(share)
    expert_sums = jnp.sum(
        lax.all_to_all(expert_cuts, "dp", 0, 0, tiled=True).astype(f32), axis=0
    )
    expert_in_grad = expert_sums[0]
    expert_out_grad = jnp.swapaxes(expert_sums[1], 1, 2)
    parts = scattered(
        [
            mixed_home.astype(bf16).reshape(cuts, rows, model_width),
            back_home.astype(bf16).reshape(cuts, rows, model_width),
            route_home.reshape(cuts, rows, lanes),
        ],
        3,
    )
    moe, back_rows, route_grad = [jnp.sum(part.astype(f32), axis=0) for part in parts]
    route_grad = route_grad[:, :experts_all]

    layer_rows = resid + moe
    grad_out = my_rows(cotangent).astype(f32)
    logit_grad = route * (route_grad - jnp.sum(route * route_grad, axis=-1, keepdims=True))
    local_router = jnp.dot(
        second.astype(f32).T, logit_grad, precision=lax.Precision.HIGHEST
    )
    second_grad = back_rows + jnp.dot(logit_grad, router_weight.T, precision=lax.Precision.HIGHEST)
    local_second_gain = jnp.sum(second_grad * normed2, axis=0)
    local_second_bias = jnp.sum(second_grad, axis=0)
    resid_grad = grad_out + norm_back(second_grad, normed2, scale2, second_gain)
    (resid_all,) = gathered([resid_grad.astype(bf16)], 4)
    resid_low = resid_all.reshape(padded, model_width)[:tokens_here]

    context_grad = jnp.einsum(
        "rd,hd->rh", resid_low, attention_out, preferred_element_type=f32
    ).astype(bf16)
    context_g = split_heads(context_grad)
    values_grad = jnp.einsum(
        "ihqk,iqhd->ikhd", weights, context_g, preferred_element_type=f32
    ).astype(bf16)
    probs_grad = jnp.einsum("iqhd,ikhd->ihqk", context_g, values_h, preferred_element_type=f32)
    delta = jnp.transpose(
        jnp.sum(context_g.astype(f32) * context_h.astype(f32), axis=-1), (0, 2, 1)
    )
    score_grad = (probs * (probs_grad - delta[..., None]) * scaling).astype(bf16)
    query_grad = jnp.einsum(
        "ihqk,ikhd->iqhd", score_grad, keys_h, preferred_element_type=f32
    ).astype(bf16)
    keys_grad = jnp.einsum(
        "ihqk,iqhd->ikhd", score_grad, query_h, preferred_element_type=f32
    ).astype(bf16)
    grads_flat = [
        part.reshape(tokens_here, local_width) for part in (query_grad, keys_grad, values_grad)
    ]
    partial_first = sum(
        jnp.einsum("rh,dh->rd", grads_flat[k], attention_in[k], preferred_element_type=f32)
        for k in range(3)
    )
    local_first_gain = jnp.sum(partial_first * normed1, axis=0)
    local_first_bias = jnp.sum(partial_first, axis=0)
    members = lax.axis_size("dp") * owners
    share = model_width // members
    small = jnp.concatenate(
        [
            local_router.T,
            jnp.stack([local_first_gain, local_first_bias, local_second_gain, local_second_bias]),
        ]
    )
    tall = rounded_up(small.shape[0], 8)
    small = cut_along(small, 1, members)
    small = jnp.pad(
        small, ((0, 0), (0, tall - small.shape[1]), (0, rounded_up(share, 128) - share))
    )
    first_parts, small_parts = line_and_group(
        pad_rows(partial_first).astype(bf16).reshape(cuts, rows, model_width), small, 5, False
    )
    first_grad = jnp.sum(first_parts.astype(f32), axis=0)
    small_sum = jnp.sum(small_parts, axis=0)
    normed1_rows, scale1_rows = normalize(my_rows(inputs).astype(f32))
    grad_rows = resid_grad + norm_back(first_grad, normed1_rows, scale1_rows, first_gain)
    small_low = small_sum.astype(bf16)
    small_low = jnp.pad(small_low, ((0, rounded_up(tall, 16) - tall), (0, model_width - small_low.shape[1])))
    attention_cuts = jnp.stack(
        [
            jnp.einsum("rd,rh->dh", left, part, preferred_element_type=f32).astype(bf16)
            for left, part in zip([first] * 3 + [resid_low], grads_flat + [context])
        ],
        axis=1,
    ).reshape(members, share, 4, local_width)
    sent_rows = jnp.concatenate([grad_rows.astype(bf16), layer_rows.astype(bf16), small_low])
    grad_all, attention_parts = line_and_group(
        sent_rows, jnp.swapaxes(attention_cuts, 1, 2), 6, True
    )
    input_grad = grad_all[:, :rows].reshape(padded, model_width)[:tokens_here].astype(f32)
    layer_out = grad_all[:, rows : 2 * rows].reshape(padded, model_width)[:tokens_here].astype(f32)
    totals = jnp.sum(grad_all[:, 2 * rows :].astype(f32), axis=0)[:, :share]
    attention_sums = jnp.sum(attention_parts.astype(f32), axis=0)
    attention_in_grad = attention_sums[:3]
    attention_out_grad = attention_sums[3].T
    return (
        layer_out,
        input_grad,
        totals[experts_all],
        totals[experts_all + 1],
        attention_in_grad,
        attention_out_grad,
        totals[experts_all + 2],
        totals[experts_all + 3],
        totals[:experts_all].T,
        expert_in_grad,
        expert_out_grad,
    )


def per_device(
    inputs,
    first_gain,
    first_bias,
    attention_in,
    attention_out,
    second_gain,
    second_bias,
    router_weight,
    expert_in,
    expert_out,
    expert_ids,
    slot_index,
    cotangent,
):
    arguments = (
        inputs,
        first_gain,
        first_bias,
        attention_in,
        attention_out,
        second_gain,
        second_bias,
        router_weight,
        expert_in,
        expert_out,
        expert_ids,
        slot_index,
        cotangent,
    )
    owners, groups, cuts = [lax.axis_size(axis) for axis in ("expert", "dp", "tensor")]
    tokens, width = inputs.shape
    here = expert_in.shape[0]
    experts_all = here * owners
    if (owners, groups, cuts) != (2, 4, 4) or tokens != SEQ or experts_all > 4:
        return per_device_general(*arguments)
    bf16, f32 = jnp.bfloat16, jnp.float32
    capacity = (2 * tokens - 1) // experts_all
    depth = rounded_up(capacity, 16)
    local = attention_in.shape[2]
    heads = local // HEAD_DIM
    rows = rounded_up(rounded_up(tokens, cuts) // cuts, 8)
    padded = rows * cuts
    ctx_rows = rounded_up(tokens, 16)
    members = owners * groups
    cut = width // members
    share = width // groups
    slots = here * depth
    vmem = pl.BlockSpec(memory_space=pltpu.VMEM)
    early_rows = rounded_up(rows // 2, 16)
    anywhere = pl.BlockSpec(memory_space=pl.ANY)
    shapes = [
        ((cuts, early_rows, width), bf16),
        ((cuts, rows - early_rows, width), bf16),
        ((cuts, rows, width), bf16),
        ((2, here, share, width), f32),
        ((members // 2, cut, 4 * local), bf16),
        ((cuts, 8, 128), f32),
    ]
    slab = (cuts, rows, width)
    vectors = [((width,), f32)] * 4
    scratch = [
        (inputs.shape, bf16),
        (cotangent.shape, bf16),
        *vectors,
        ((experts_all, width), f32),
        ((2, tokens), jnp.int32),
        ((2, tokens), jnp.int32),
        ((padded, width), f32),
        ((padded, width), f32),
        ((2, padded, width), bf16),
        ((padded, width), bf16),
        ((rows, width), bf16),
        (slab, bf16),
        ((2, 8, 256), f32),
        ((8, width), f32),
        ((3, local, width), bf16),
        ((cuts, local, width), bf16),
        ((2, cuts, ctx_rows // 2, 2 * local), bf16),
        ((ctx_rows, local), bf16),
        (expert_in.shape, bf16),
        (expert_out.shape, bf16),
        ((2, padded, width), bf16),
        ((padded, width), f32),
        ((padded, width), bf16),
        ((padded, width), f32),
        ((3, ctx_rows, local), bf16),
        ((heads, ctx_rows, ctx_rows), f32),
        (slab, bf16),
        (slab, bf16),
        (slab, bf16),
        (slab, bf16),
        (slab, bf16),
        ((rows, width), bf16),
        ((rows, width), bf16),
        ((2, *slab), bf16),
        ((2, rows, width), bf16),
        ((2, 3, rows, width), bf16),
        ((rows, width), bf16),
        ((early_rows, width), bf16),
        ((rows - early_rows, width), bf16),
        ((8, 128), f32),
        ((8, 256), f32),
        ((8, 256), f32),
        ((cuts, 8, 256), f32),
        (slab, bf16),
        (slab, f32),
        ((cuts, rows, local), bf16),
        ((cuts, rows, local), bf16),
        ((2, here, 2, 2, share, width), bf16),
        ((here, 2, 2, share, width), bf16),
        ((here, 2, share, width), bf16),
        ((2, here, share, width), f32),
        ((2, members // 2, cut, 4 * local), bf16),
        ((members // 2, cut, 4 * local), bf16),
        ((cuts, early_rows, width), bf16),
        ((cuts, rows - early_rows, width), bf16),
        ((cuts, early_rows, width), bf16),
        ((cuts, rows - early_rows, width), bf16),
        ((8, width), f32),
        ((members, 8, 128), f32),
        ((members, 8, 128), f32),
        ((2, slots, width), bf16),
        ((here, 2 * depth, width), bf16),
        ((here, 2 * depth, width), bf16),
        ((here, 2 * depth, width), bf16),
        ((here, 2 * depth, width), bf16),
        ((2, slots, padded), bf16),
        ((2, slots, width), bf16),
    ]
    sems = [pltpu.SemaphoreType.DMA((n,)) for n in (20, 96, 96)]
    received = pl.pallas_call(
        functools.partial(block_kernel, (tokens, rows, cuts, experts_all, capacity, depth)),
        out_shape=[jax.ShapeDtypeStruct(*s) for s in shapes],
        in_specs=[anywhere] * 13,
        out_specs=[anywhere] * 6,
        scratch_shapes=[pltpu.VMEM(*s) for s in scratch] + sems,
        compiler_params=pltpu.CompilerParams(
            collective_id=0, has_side_effects=True, vmem_limit_bytes=56 << 20
        ),
        name="block",
    )(
        inputs,
        cotangent,
        first_gain,
        first_bias,
        second_gain,
        second_bias,
        router_weight.T,
        expert_ids.T,
        slot_index.T,
        jnp.swapaxes(attention_in, 1, 2),
        attention_out,
        expert_in,
        expert_out,
    )
    results = [
        ((tokens, width), f32),
        ((tokens, width), f32),
        ((1, cut), f32),
        ((1, cut), f32),
        ((3, cut, local), f32),
        ((local, cut), f32),
        ((1, cut), f32),
        ((1, cut), f32),
        ((experts_all, cut), f32),
        ((here, share, width), f32),
        ((here, share, width), f32),
    ]
    large = [results[i] for i in (0, 1, 4, 5)]
    out = pl.pallas_call(
        functools.partial(finish_kernel, (tokens, experts_all, local)),
        out_shape=[jax.ShapeDtypeStruct(*s) for s in results],
        in_specs=[anywhere] * 6,
        out_specs=[anywhere] * 2 + [vmem] * 2 + [anywhere] * 2 + [vmem] * 3 + [anywhere] * 2,
        scratch_shapes=[pltpu.VMEM(*s) for s in shapes + large]
        + [pltpu.SemaphoreType.DMA((n,)) for n in (6, 6)],
        compiler_params=pltpu.CompilerParams(vmem_limit_bytes=56 << 20),
        name="finish",
    )(*received)
    return (
        out[0],
        out[1],
        out[2].reshape(cut),
        out[3].reshape(cut),
        out[4],
        out[5],
        out[6].reshape(cut),
        out[7].reshape(cut),
        out[8].T,
        out[9],
        jnp.swapaxes(out[10], 1, 2),
    )


def solution(mesh):
    in_specs = (
        P(("dp", "expert"), None),
        P(),
        P(),
        P(None, None, "tensor"),
        P("tensor", None),
        P(),
        P(),
        P(),
        P("expert", None, "tensor"),
        P("expert", "tensor", None),
        P(("dp", "expert"), None),
        P(("dp", "expert"), None),
        P(("dp", "expert"), None),
    )
    out_specs = (
        P(("dp", "expert"), None),
        P(("dp", "expert"), None),
        P(("dp", "expert")),
        P(("dp", "expert")),
        P(None, ("dp", "expert"), "tensor"),
        P("tensor", ("dp", "expert")),
        P(("dp", "expert")),
        P(("dp", "expert")),
        P(("dp", "expert"), None),
        P("expert", "dp", "tensor"),
        P("expert", "tensor", "dp"),
    )
    return jax.shard_map(
        per_device, mesh=mesh, in_specs=in_specs, out_specs=out_specs, check_vma=False
    )
```

```python
import functools
import math

import jax
import jax.numpy as jnp
from jax import lax
from jax.experimental import pallas as pl
from jax.experimental.pallas import tpu as pltpu
from jax.sharding import PartitionSpec as P

HEAD_DIM = 64
SEQ = 197


EPS = 1e-06
GELU_C = math.sqrt(2.0 / math.pi)


def cut_along(shard, dim, devices):
    shape = shard.shape
    tiles = shard.reshape(*shape[:dim], devices, shape[dim] // devices, *shape[dim + 1 :])
    return jnp.moveaxis(tiles, dim, 0)


def sent_and_summed(shard, axis, dim):
    devices = lax.axis_size(axis)
    tiles = lax.all_to_all(cut_along(shard, dim, devices), axis, 0, 0, tiled=True)
    return jnp.sum(tiles.astype(jnp.float32), axis=0)


def sent_together(arrays, axis, dim, along):
    widths = [math.prod(a.shape[along:]) for a in arrays]
    both = jnp.concatenate(
        [a.reshape(*a.shape[:along], w) for a, w in zip(arrays, widths)], axis=along
    )
    out = sent_and_summed(both, axis, dim)
    tiles = jnp.split(out, [sum(widths[:k]) for k in range(1, len(widths))], axis=along)
    return tuple((b.reshape(*out.shape[:along], *a.shape[along:]) for a, b in zip(arrays, tiles)))


def normalize(values):
    centre = jnp.mean(values, axis=-1, keepdims=True)
    centred = values - centre
    spread = jnp.mean(centred * centred, axis=-1, keepdims=True)
    scale = lax.rsqrt(spread + EPS)
    return (centred * scale, scale)


def norm_back(grad_out, normed, scale, gain):
    scaled = grad_out * gain
    first_mean = jnp.mean(scaled, axis=-1, keepdims=True)
    second_mean = jnp.mean(scaled * normed, axis=-1, keepdims=True)
    return scale * (scaled - first_mean - normed * second_mean)


def gelu_parts(pre):
    inner = GELU_C * (pre + 0.044715 * pre * pre * pre)
    tangent = jnp.tanh(inner)
    value = 0.5 * pre * (1.0 + tangent)
    slope = 0.5 * (1.0 + tangent) + 0.5 * pre * (1.0 - tangent * tangent) * GELU_C * (
        1.0 + 3.0 * 0.044715 * pre * pre
    )
    return (value, slope)


MESH = pl.DeviceIdType.MESH


def greet(axes):
    barrier = pltpu.get_barrier_semaphore()
    peers = 0
    for axis in axes:
        devices = lax.axis_size(axis)
        me = lax.axis_index(axis)
        for k in range(1, devices):
            peer = lax.rem(me + k, devices)
            pl.semaphore_signal(barrier, inc=1, device_id={axis: peer}, device_id_type=MESH)
            peers += 1
    pl.semaphore_wait(barrier, peers)


def group_peer(k):
    owners = lax.axis_size("expert")
    members = lax.axis_size("dp") * owners
    me = lax.axis_index("dp") * owners + lax.axis_index("expert")
    peer = lax.rem(me + k, members)
    return {"dp": peer // owners, "expert": lax.rem(peer, owners)}


def greet_line_and_group(grouped):
    barrier = pltpu.get_barrier_semaphore()
    cuts = lax.axis_size("tensor")
    members = lax.axis_size("dp") * lax.axis_size("expert") if grouped else 1
    for k in range(1, cuts):
        peer = {"tensor": lax.rem(lax.axis_index("tensor") + k, cuts)}
        pl.semaphore_signal(barrier, inc=1, device_id=peer, device_id_type=MESH)
    for k in range(1, members):
        pl.semaphore_signal(barrier, inc=1, device_id=group_peer(k), device_id_type=MESH)
    pl.semaphore_wait(barrier, cuts + members - 2)


def group_copies(source, target, send_sem, recv_sem):
    owners = lax.axis_size("expert")
    members = lax.axis_size("dp") * owners
    me = lax.axis_index("dp") * owners + lax.axis_index("expert")
    copies = []
    for k in range(1, members):
        copy = pltpu.make_async_remote_copy(
            src_ref=source.at[lax.rem(me + k, members)],
            dst_ref=target.at[k],
            send_sem=send_sem.at[k],
            recv_sem=recv_sem.at[k],
            device_id=group_peer(k),
            device_id_type=MESH,
        )
        copy.start()
        copies.append(copy)
    target[0] = source[me]
    return copies


def ends_kernel(gather, *refs):
    source, group_source, target, group_target = refs[:4]
    send_sem, recv_sem, send_group, recv_group = refs[4:]
    devices = lax.axis_size("tensor")
    me = lax.axis_index("tensor")
    greet_line_and_group(True)
    copies = []
    for k in range(1, devices):
        peer = lax.rem(me + k, devices)
        copy = pltpu.make_async_remote_copy(
            src_ref=source if gather else source.at[peer],
            dst_ref=target.at[me] if gather else target.at[k],
            send_sem=send_sem.at[k],
            recv_sem=recv_sem.at[k],
            device_id={"tensor": peer},
            device_id_type=MESH,
        )
        copy.start()
        copies.append(copy)
    copies += group_copies(group_source, group_target, send_group, recv_group)
    if gather:
        target[me] = source[...]
    else:
        target[0] = source[me]
    for copy in copies:
        copy.wait()


def line_and_group(array, group_array, collective_id, gather):
    devices = lax.axis_size("tensor")
    members = group_array.shape[0]
    shape = (devices, *array.shape) if gather else array.shape
    return pl.pallas_call(
        functools.partial(ends_kernel, gather),
        out_shape=[
            jax.ShapeDtypeStruct(shape, array.dtype),
            jax.ShapeDtypeStruct(group_array.shape, group_array.dtype),
        ],
        in_specs=[pl.BlockSpec(memory_space=pltpu.VMEM)] * 2,
        out_specs=[pl.BlockSpec(memory_space=pltpu.VMEM)] * 2,
        scratch_shapes=[pltpu.SemaphoreType.DMA((n,)) for n in (devices, devices, members, members)],
        compiler_params=pltpu.CompilerParams(collective_id=collective_id, has_side_effects=True),
        name=f"ends{collective_id}",
    )(array, group_array)


def scatter_kernel(count, *refs):
    sources, targets = refs[:count], refs[count : 2 * count]
    send_sem, recv_sem = refs[2 * count :]
    devices = lax.axis_size("tensor")
    me = lax.axis_index("tensor")
    greet(("tensor",))
    copies = []
    for k in range(1, devices):
        peer = lax.rem(me + k, devices)
        for a in range(count):
            copy = pltpu.make_async_remote_copy(
                src_ref=sources[a].at[peer],
                dst_ref=targets[a].at[k],
                send_sem=send_sem.at[a, k],
                recv_sem=recv_sem.at[a, k],
                device_id={"tensor": peer},
                device_id_type=MESH,
            )
            copy.start()
            copies.append(copy)
    for a in range(count):
        targets[a][0] = sources[a][me]
    for copy in copies:
        copy.wait()


def scattered(arrays, collective_id):
    devices = lax.axis_size("tensor")
    count = len(arrays)
    return pl.pallas_call(
        functools.partial(scatter_kernel, count),
        out_shape=[jax.ShapeDtypeStruct(a.shape, a.dtype) for a in arrays],
        in_specs=[pl.BlockSpec(memory_space=pltpu.VMEM)] * count,
        out_specs=[pl.BlockSpec(memory_space=pltpu.VMEM)] * count,
        scratch_shapes=[
            pltpu.SemaphoreType.DMA((count, devices)),
            pltpu.SemaphoreType.DMA((count, devices)),
        ],
        compiler_params=pltpu.CompilerParams(collective_id=collective_id, has_side_effects=True),
        name=f"scatter{collective_id}",
    )(*arrays)


def gather_kernel(count, forward, *refs):
    sources, targets = refs[:count], refs[count : 2 * count]
    send_z, recv_z, send_x, recv_x = refs[2 * count :]
    devices = lax.axis_size("tensor")
    me = lax.axis_index("tensor")
    owners = lax.axis_size("expert") if forward else 1
    home = lax.axis_index("expert")
    greet(("tensor", "expert") if forward else ("tensor",))

    def across(a, k, source, place):
        copies = []
        for e in range(1, owners):
            copy = pltpu.make_async_remote_copy(
                src_ref=source,
                dst_ref=targets[a].at[e, place],
                send_sem=send_x.at[a, k, e],
                recv_sem=recv_x.at[a, k, e],
                device_id={"expert": lax.rem(home + e, owners)},
                device_id_type=MESH,
            )
            copy.start()
            copies.append(copy)
        return copies

    along = []
    for k in range(1, devices):
        peer = lax.rem(me + k, devices)
        for a in range(count):
            copy = pltpu.make_async_remote_copy(
                src_ref=sources[a],
                dst_ref=targets[a].at[0, me],
                send_sem=send_z.at[a, k],
                recv_sem=recv_z.at[a, k],
                device_id={"tensor": peer},
                device_id_type=MESH,
            )
            copy.start()
            along.append((a, k, copy))
    crossing = []
    for a in range(count):
        crossing += across(a, 0, sources[a], me)
    for a in range(count):
        targets[a][0, me] = sources[a][...]
    for a, k, copy in along:
        copy.wait()
        place = lax.rem(me + devices - k, devices)
        crossing += across(a, k, targets[a].at[0, place], place)
    for copy in crossing:
        copy.wait()


def gathered(arrays, collective_id, forward=False):
    devices = lax.axis_size("tensor")
    owners = lax.axis_size("expert") if forward else 1
    count = len(arrays)
    sems = [(count, devices)] * 2 + [(count, devices, owners)] * 2
    return pl.pallas_call(
        functools.partial(gather_kernel, count, forward),
        out_shape=[
            jax.ShapeDtypeStruct((owners, devices, *a.shape), a.dtype) for a in arrays
        ],
        in_specs=[pl.BlockSpec(memory_space=pltpu.VMEM)] * count,
        out_specs=[pl.BlockSpec(memory_space=pltpu.VMEM)] * count,
        scratch_shapes=[pltpu.SemaphoreType.DMA(s) for s in sems],
        compiler_params=pltpu.CompilerParams(collective_id=collective_id, has_side_effects=True),
        name=f"gather{collective_id}",
    )(*arrays)


def shifted(array, axis, offset):
    devices = lax.axis_size(axis)
    return lax.ppermute(array, axis, [(d, (d + offset) % devices) for d in range(devices)])


def from_owners(array):
    owners = lax.axis_size("expert")
    return jnp.stack([array] + [shifted(array, "expert", e) for e in range(1, owners)])


def to_owners(array):
    owners = lax.axis_size("expert")
    total = array[0].astype(jnp.float32)
    for e in range(1, owners):
        total = total + shifted(array[e], "expert", owners - e).astype(jnp.float32)
    return total


def rounded_up(value, multiple):
    return -(-value // multiple) * multiple


def experts_kernel(
    experts_all,
    slot_ref,
    spot_ref,
    second_ref,
    cot_ref,
    router_ref,
    in_ref,
    out_ref,
    mixed_ref,
    back_ref,
    share_ref,
    route_ref,
    cut_ref,
    placing_ref,
    gated_ref,
    low_ref,
    grad_ref,
):
    bf16, f32 = jnp.bfloat16, jnp.float32
    exact = lax.Precision.HIGHEST
    owners, padded, _ = second_ref.shape
    experts_here = in_ref.shape[0]
    lanes = router_ref.shape[1]
    depth = placing_ref.shape[2]

    def dot(a, b, a_dim, b_dim, precision=None):
        return lax.dot_general(
            a, b, (((a_dim,), (b_dim,)), ((), ())), precision=precision, preferred_element_type=f32
        )

    column = lax.broadcasted_iota(jnp.int32, (padded, lanes), 1)
    for o in range(owners):
        logits = dot(second_ref[o].astype(f32), router_ref[...], 1, 0, exact)
        logits = jnp.where(column < experts_all, logits, -1e30)
        lifted = jnp.exp(logits - jnp.max(logits, axis=-1, keepdims=True))
        lifted = jnp.where(column < experts_all, lifted, 0.0)
        route_ref[o] = lifted / jnp.sum(lifted, axis=-1, keepdims=True)
    slot = lax.broadcasted_iota(jnp.int32, (depth, padded), 0)
    for k in range(experts_here):
        gates, received, slotted = [], [], []
        for o in range(owners):
            picks = slot == slot_ref[k, o][None, :]
            placing = jnp.where(picks, 1.0, 0.0)
            low = placing.astype(bf16)
            placing_ref[k, o] = low
            chances = dot(placing, route_ref[o], 1, 0, exact)
            gates.append(jnp.sum(chances * spot_ref[k][None, :], axis=-1, keepdims=True))
            received.append(dot(low, second_ref[o], 1, 0).astype(bf16))
            slotted.append(dot(low, cot_ref[o], 1, 0))
        gate = jnp.concatenate(gates)
        received = jnp.concatenate(received)
        slotted = jnp.concatenate(slotted)
        y_grad = (gate * slotted).astype(bf16)
        value, slope = gelu_parts(dot(received, in_ref[k], 1, 0))
        hidden = value.astype(bf16)
        partial_y = dot(hidden, out_ref[k], 1, 0)
        gated_ref[k] = (gate * partial_y).astype(bf16)
        slot_grad = jnp.sum(slotted * partial_y, axis=-1, keepdims=True)
        grad_ref[k] = slot_grad * spot_ref[k][None, :]
        pre_grad = (dot(y_grad, out_ref[k], 1, 1) * slope).astype(bf16)
        low_ref[k] = dot(pre_grad, in_ref[k], 1, 1).astype(bf16)
        in_grad = dot(received, pre_grad, 0, 0).astype(bf16)
        out_grad = dot(y_grad, hidden, 0, 0).astype(bf16)
        blocks, _, _, share, _ = cut_ref.shape
        for d in range(blocks):
            cut_ref[d, 0, k] = in_grad[d * share : (d + 1) * share]
            cut_ref[d, 1, k] = out_grad[d * share : (d + 1) * share]
    for o in range(owners):
        span = pl.ds(o * depth, depth)
        here = range(experts_here)
        mixed_ref[o] = sum(
            dot(placing_ref[k, o], gated_ref[k, span], 0, 0) for k in here
        ).astype(bf16)
        back_ref[o] = sum(dot(placing_ref[k, o], low_ref[k, span], 0, 0) for k in here).astype(bf16)
        share_ref[o] = sum(
            dot(placing_ref[k, o].astype(f32), grad_ref[k, span], 0, 0, exact) for k in here
        )


def experts_block(slots, spot, second, cot, router, expert_in, expert_out, experts_all, depth):
    owners, padded, width = second.shape
    here, _, hidden = expert_in.shape
    lanes = router.shape[1]
    blocks = lax.axis_size("dp")
    bf16, f32 = jnp.bfloat16, jnp.float32
    shapes = [
        ((owners, padded, width), bf16),
        ((owners, padded, width), bf16),
        ((owners, padded, lanes), f32),
        ((owners, padded, lanes), f32),
        ((blocks, 2, here, width // blocks, hidden), bf16),
    ]
    return pl.pallas_call(
        functools.partial(experts_kernel, experts_all),
        out_shape=[jax.ShapeDtypeStruct(*s) for s in shapes],
        in_specs=[pl.BlockSpec(memory_space=pltpu.VMEM)] * 7,
        out_specs=[pl.BlockSpec(memory_space=pltpu.VMEM)] * 5,
        scratch_shapes=[
            pltpu.VMEM((here, owners, depth, padded), bf16),
            pltpu.VMEM((here, owners * depth, width), bf16),
            pltpu.VMEM((here, owners * depth, width), bf16),
            pltpu.VMEM((here, owners * depth, lanes), f32),
        ],
        compiler_params=pltpu.CompilerParams(
            vmem_limit_bytes=(32 << 20) if owners <= 2 else (60 << 20)
        ),
        name="experts",
    )(slots, spot, second, cot, router, expert_in, expert_out)


def lane_dot(a, b, a_dim, b_dim, precision=None):
    return lax.dot_general(
        a, b, (((a_dim,), (b_dim,)), ((), ())), precision=precision, preferred_element_type=jnp.float32
    )


def block_kernel(dims, *refs):
    tokens, rows, cuts, experts_all, capacity, depth = dims
    bf16, f32 = jnp.bfloat16, jnp.float32
    exact = lax.Precision.HIGHEST
    given = refs[:9]
    (w_hbm, wo_hbm, ein_hbm, eout_hbm) = refs[9:13]
    (final_a, final_b, layers, e_sum, g_parts, small_parts) = refs[13:19]
    (
        x_in, cot_in, gain1, bias1, gain2, bias2, router_in, ids_in, slot_in, x32, c32,
        xs, cots, cot_out, cot_far, tgt, rt, w_in, wo, ctx, ctx_own, ein, eout, sec, resid, first, n1,
        qkv, probs, back_out, back_in, back_home, back_send, back_got,
        mix_out, mix_in, mix_part, mix_pair, mix_got,
        end_layer, end_a, end_b, small_sum, share_out, share_in, share_all, low, lg, cg_out, cg_in, ebuf, e_got, e_peer, e_total, gbuf, g_got, first_a, first_b, first_got_a, first_got_b,
        small, small_send, small_got, lowers, hid, pgr, rec, ygr, plc, gated,
        load, ss, rs,
    ) = refs[19:]
    d, e, z = lax.axis_index("dp"), lax.axis_index("expert"), lax.axis_index("tensor")
    core, y = lax.rem(d, 2), d // 2
    padded = rows * cuts
    width = x_in.shape[1]
    wide = lambda vector: vector[...][None, :]
    local = wo_hbm.shape[0]
    heads = local // HEAD_DIM
    quarter = local // 4
    here = ein_hbm.shape[0]
    ctx_rows = qkv.shape[1]
    ctx_half = ctx_rows // 2
    other_x = {"expert": 1 - e}
    other_core = {"dp": y * 2 + 1 - core}
    other_y = {"dp": (1 - y) * 2 + core}
    diagonal = {"dp": (1 - y) * 2 + core, "expert": 1 - e}
    along = [(k, lax.rem(z + k, cuts)) for k in range(1, cuts)]
    near = z + 1 - 2 * lax.rem(z, 2)
    far = lax.rem(z + 2, cuts)
    last = lax.rem(near + 2, cuts)
    count = [0]
    pending = []

    def send(source, target, device):
        i = count[0]
        count[0] += 1
        copy = pltpu.make_async_remote_copy(
            src_ref=source,
            dst_ref=target,
            send_sem=ss.at[i],
            recv_sem=rs.at[i],
            device_id=device,
            device_id_type=MESH,
        )
        copy.start()
        pending.append(copy)
        return copy

    def spread(source, slab):
        return [send(source, slab(z), {"tensor": peer}) for peer in (near, far)]

    def passed_on(copies, slab):
        copies[1].wait_recv()
        copies.append(send(slab(far), slab(far), {"tensor": near}))

    loads = [
        pltpu.make_async_copy(w_hbm, w_in, load.at[0]),
        pltpu.make_async_copy(wo_hbm, wo.at[z], load.at[1]),
        pltpu.make_async_copy(ein_hbm, ein, load.at[2]),
        pltpu.make_async_copy(eout_hbm, eout, load.at[3]),
    ]
    here_now = (x_in, cot_in, gain1, bias1, gain2, bias2, router_in, ids_in, slot_in)
    early = [
        pltpu.make_async_copy(source, target, load.at[4 + i])
        for i, (source, target) in enumerate(zip(given, here_now))
    ]
    for copy in early + loads:
        copy.start()
    barrier = pltpu.get_barrier_semaphore()
    others = [
        {"dp": (y if same_y else 1 - y) * 2 + (core if same_core else 1 - core),
         "expert": e if same_e else 1 - e}
        for same_y in (1, 0) for same_core in (1, 0) for same_e in (1, 0)
    ][1:]
    greeted = others + [{"tensor": p} for _, p in along]
    for peer in greeted:
        pl.semaphore_signal(barrier, inc=1, device_id=peer, device_id_type=MESH)

    for copy in early:
        copy.wait()
    edge = tokens // 8 * 8
    for whole, part in ((x32, x_in), (c32, cot_in)):
        whole[edge:padded] = jnp.zeros((padded - edge, width), f32)
        whole[0:tokens] = part[...].astype(f32)
    xs[0] = x32[...].astype(bf16)
    xs[1, ctx_rows:padded] = jnp.zeros((padded - ctx_rows, width), bf16)
    cots[...] = c32[...].astype(bf16)
    cot_rows = c32[pl.ds(pl.multiple_of(z * rows, 8), rows)]
    cot_out[...] = cot_rows.astype(bf16)
    x_full = x32[...]
    tgt[0] = jnp.full(tgt.shape[1:], -1.0, f32)
    slot = slot_in[...]
    tgt[0, 0:2, 0:tokens] = jnp.where(slot < capacity, ids_in[...] * capacity + slot, -1).astype(f32)
    rt[...] = jnp.zeros_like(rt)
    rt[0:experts_all] = router_in[...]

    pl.semaphore_wait(barrier, len(greeted))
    loads[1].wait()

    def wo_part(c, part):
        return wo.at[c, pl.ds(pl.multiple_of(part * quarter, 16), quarter)]

    cot_copy = send(cot_out, cot_far.at[z], other_x)
    mine_of_wo = lambda c: wo_part(c, d)
    wo_along = spread(wo_part(z, d), mine_of_wo)
    x_copy = send(xs.at[0, pl.ds(0, ctx_rows)], xs.at[1, pl.ds(0, ctx_rows)], other_x)
    tgt_copy = send(tgt.at[0], tgt.at[1], other_x)

    normed, _ = normalize(x_full)
    n1[...] = normed
    first_low = (normed * wide(gain1) + wide(bias1)).astype(bf16)
    first[...] = first_low
    loads[0].wait()
    for which in range(3):
        qkv[which] = lane_dot(first_low[:ctx_rows], w_in[which], 1, 1).astype(bf16)
    head = lax.broadcasted_iota(jnp.int32, (ctx_rows, local), 1) // HEAD_DIM
    masks = [jnp.where(head == h, 1.0, 0.0) for h in range(heads)]
    key_at = lax.broadcasted_iota(jnp.int32, (ctx_rows, ctx_rows), 1)
    scaling = HEAD_DIM ** (-0.5)

    def of_head(matrix, h):
        return matrix * masks[h].astype(matrix.dtype)

    query, keys, values = qkv[0], qkv[1], qkv[2]
    total = jnp.zeros((ctx_rows, local), f32)
    for h in range(heads):
        scores = lane_dot(of_head(query, h), keys, 1, 1) * scaling
        scores = jnp.where(key_at < tokens, scores, -1e30)
        peak = jnp.max(scores, axis=-1, keepdims=True)
        logsum = peak + jnp.log(jnp.sum(jnp.exp(scores - peak), axis=-1, keepdims=True))
        chance = jnp.exp(scores - logsum)
        probs[h] = chance
        total += lane_dot(chance.astype(bf16), of_head(values, h), 1, 0)
    ctx_own[...] = total.astype(bf16)
    ctx[0, z] = jnp.concatenate([total[:ctx_half], total[ctx_half:]], axis=1).astype(bf16)

    near_ctx = lambda c: ctx.at[0, c]
    ctx_along = spread(ctx.at[0, z], near_ctx)
    ctx_across = [(z, send(ctx.at[0, z], ctx.at[1, z], other_x))]

    far_row = (1 - y) * 2 + core
    wo_row, wo_core = [], []

    def wo_on(place):
        wo_row.append((place, send(wo_part(place, d), wo_part(place, d), other_y)))
        wo_core.append(send(wo_part(place, d), wo_part(place, d), other_core))

    def ctx_on(place):
        ctx_across.append((place, send(ctx.at[0, place], ctx.at[1, place], other_x)))

    wo_along[0].wait_recv()
    wo_on(near)
    passed_on(wo_along, mine_of_wo)
    wo_on(far)
    ctx_along[0].wait_recv()
    ctx_on(near)
    passed_on(ctx_along, near_ctx)
    ctx_on(far)
    wo_along[2].wait_recv()
    wo_on(last)
    cot_copy.wait_recv()
    far_cot = lambda c: cot_far.at[c]
    cot_far_along = spread(cot_far.at[z], far_cot)
    ctx_along[2].wait_recv()
    ctx_on(last)
    for place, copy in wo_row:
        copy.wait_recv()
        wo_core.append(send(wo_part(place, far_row), wo_part(place, far_row), other_core))
    for copy in wo_core:
        copy.wait_recv()

    split = rt[...]
    splits = []
    for _ in range(3):
        piece = split.astype(bf16)
        splits.append(piece.astype(f32))
        split = split - piece.astype(f32)
    router_low = jnp.concatenate(splits).astype(bf16)
    lanes8 = rt.shape[0]
    expert_row = lax.broadcasted_iota(jnp.int32, (lanes8, padded), 0)
    base = e * here

    def forward(o):
        halves = [jnp.zeros((ctx_half, width), f32) for _ in range(2)]
        for c in range(cuts):
            both = ctx[o, c]
            for n in range(2):
                halves[n] += lane_dot(both[:, n * local : (n + 1) * local], wo[c], 1, 0)
        attended = jnp.concatenate([*halves, jnp.zeros((padded - ctx_rows, width), f32)])
        res = xs[o].astype(f32) + attended
        normed2, _ = normalize(res)
        second = (normed2 * wide(gain2) + wide(bias2)).astype(bf16)
        sec[o] = second
        parts = lane_dot(router_low, second, 1, 1)
        logits = parts[:lanes8] + parts[lanes8 : 2 * lanes8] + parts[2 * lanes8 :]
        logits = jnp.where(expert_row < experts_all, logits, -1e30)
        lifted = jnp.exp(logits - jnp.max(logits, axis=0, keepdims=True))
        lifted = jnp.where(expert_row < experts_all, lifted, 0.0)
        return res, lifted / jnp.sum(lifted, axis=0, keepdims=True)

    slot_at = lax.broadcasted_iota(jnp.int32, (depth, padded), 0)

    def picks_of(o, k):
        offset = tgt[o, 0:2, 0:padded].astype(jnp.int32) - (base + k) * capacity
        chosen = jnp.where((offset >= 0) & (offset < capacity), offset, -1)
        return slot_at == jnp.max(chosen, axis=0, keepdims=True)

    def place(o, route):
        placed, gates = [], []
        for k in range(here):
            picks = picks_of(o, k)
            placed.append(jnp.where(picks, 1.0, 0.0))
            row = jnp.sum(jnp.where(expert_row == base + k, route, 0.0), axis=0, keepdims=True)
            gates.append(jnp.sum(jnp.where(picks, row, 0.0), axis=-1, keepdims=True))
        low_place = jnp.concatenate(placed).astype(bf16)
        plc[o] = low_place
        gate = jnp.concatenate(gates)
        received = lane_dot(low_place, sec[o], 1, 0).astype(bf16)
        return gate, received

    res, route_own = forward(0)
    resid[...] = res
    tgt_copy.wait_recv()
    x_copy.wait_recv()
    passed_on(cot_far_along, far_cot)
    own = place(0, route_own)
    for _, copy in ctx_across:
        copy.wait_recv()
    _, route_far = forward(1)
    away = place(1, route_far)
    loads[2].wait()
    loads[3].wait()

    def joined(both, k):
        span = slice(k * depth, (k + 1) * depth)
        return jnp.concatenate([part[span] for part in both])

    def chunked(target, matrix):
        for c in range(cuts):
            target[c] = matrix[c * rows : (c + 1) * rows].astype(target.dtype)

    fore = []
    for k in range(here):
        received = joined((own[1], away[1]), k)
        value, slope = gelu_parts(lane_dot(received, ein[k], 1, 0))
        hidden = value.astype(bf16)
        rec[k], hid[k] = received, hidden
        partial_y = lane_dot(hidden, eout[k], 1, 0)
        gate = joined((own[0], away[0]), k)
        fore.append((gate, slope, partial_y))
        weighted = (gate * partial_y).astype(bf16)
        for o in range(2):
            gated[o, k * depth : (k + 1) * depth] = weighted[o * depth : (o + 1) * depth]
    mix_along = []
    for o in range(2):
        chunked(mix_part.at[o], lane_dot(plc[o], gated[o], 0, 0))
        mix_along.append(
            [
                send(mix_part.at[o, last], mix_got.at[o, 1], {"tensor": near}),
                send(mix_part.at[o, near], mix_got.at[o, 0], {"tensor": near}),
            ]
        )
    for copy in cot_far_along[::2]:
        copy.wait_recv()
    cot_all = jnp.concatenate([cot_far[c].astype(f32) for c in range(cuts)]).astype(bf16)
    slotted_both = [lane_dot(plc[o], cot, 1, 0) for o, cot in enumerate((cots[...], cot_all))]
    shares = [jnp.zeros((lanes8, padded), f32) for _ in range(2)]
    for k in range(here):
        gate, slope, partial_y = fore[k]
        slotted = joined(slotted_both, k)
        y_grad = (gate * slotted).astype(bf16)
        pre_grad = (lane_dot(y_grad, eout[k], 1, 1) * slope).astype(bf16)
        lowered = lane_dot(pre_grad, ein[k], 1, 1).astype(bf16)
        slot_grad = jnp.sum(slotted * partial_y, axis=-1, keepdims=True)
        ygr[k], pgr[k] = y_grad, pre_grad
        for o in range(2):
            span = slice(o * depth, (o + 1) * depth)
            lowers[o, k * depth : (k + 1) * depth] = lowered[span]
            row = jnp.sum(
                jnp.where(picks_of(o, k), slot_grad[span], 0.0), axis=0, keepdims=True
            )
            shares[o] += jnp.where(expert_row == base + k, row, 0.0)

    chunked(back_out, lane_dot(plc[1], lowers[1], 0, 0))
    order = [lax.rem(z + k, cuts) for k in (2, 1, 3, 0)]
    back_across = [send(back_out.at[c], back_in.at[c], other_x) for c in order[:3]]
    share_out[...] = jnp.zeros_like(share_out)
    share_out[:, 0:padded] = shares[1]
    share_across = send(share_out, share_in, other_x)
    def expert_grads(k):
        in_grad = lane_dot(rec[k], pgr[k], 0, 0).astype(bf16)
        out_grad = lane_dot(ygr[k], hid[k], 0, 0).astype(bf16)
        share = width // 4
        for p in range(4):
            span = slice(p * share, (p + 1) * share)
            ebuf[p % 2, k, p // 2, 0] = in_grad[span]
            ebuf[p % 2, k, p // 2, 1] = out_grad[span]
        return send(ebuf.at[1 - core, k], e_got.at[k], other_core)

    e_row = []

    def e_on(k):
        e_core[k].wait_recv()
        for yy in range(2):
            for a in range(2):
                both = ebuf[core, k, yy, a].astype(f32) + e_got[k, yy, a].astype(f32)
                ebuf[core, k, yy, a] = both.astype(bf16)
        e_row.append(send(ebuf.at[core, k, 1 - y], e_peer.at[k], other_y))

    e_core = [expert_grads(k) for k in range(here)]
    chunked(back_home, lane_dot(plc[0], lowers[0], 0, 0))
    for o in range(2):
        mix_along[o][0].wait_recv()
        mix_pair[o] = (mix_part[o, far].astype(f32) + mix_got[o, 1].astype(f32)).astype(bf16)
        mix_along[o].append(send(mix_pair.at[o], mix_got.at[o, 2], {"tensor": far}))
    e_on(0)
    share_across.wait_recv()
    share_all[0] = share_in[...]
    share_all[0, :, 0:padded] += shares[0]
    share_along = [send(share_all.at[0], share_all.at[k], {"tensor": peer}) for k, peer in along]
    back_along = []
    for j, c in enumerate(order):
        back_across[j].wait_recv()
        if j < 1:
            back_across.append(send(back_out.at[order[j + 3]], back_in.at[order[j + 3]], other_x))
        back_send[c] = (back_home[c].astype(f32) + back_in[c].astype(f32)).astype(bf16)
        if j < 3:
            k = (2, 1, 3)[j]
            back_along.append(send(back_send.at[c], back_got.at[k], {"tensor": c}))
    mixed = []
    for o in range(2):
        for copy in mix_along[o][1:]:
            copy.wait_recv()
        mixed.append(
            mix_part[o, z].astype(f32) + mix_got[o, 0].astype(f32) + mix_got[o, 2].astype(f32)
        )
    mix_out[...] = mixed[1].astype(bf16)
    mix_across = send(mix_out, mix_in, other_x)
    e_on(1)

    for copy in share_along:
        copy.wait_recv()
    route_grad = (share_all[0] + share_all[1] + share_all[2] + share_all[3])[:, 0:padded]
    logit_grad = route_own * (route_grad - jnp.sum(route_own * route_grad, axis=0, keepdims=True))
    chunked(lg, lane_dot(logit_grad, rt[...], 0, 0, exact))
    router_grad = lane_dot(logit_grad, sec[0].astype(f32), 1, 0, exact)
    res_rows = resid[pl.ds(pl.multiple_of(z * rows, 8), rows)]
    normed2, scale2 = normalize(res_rows)
    for copy in back_along:
        copy.wait_recv()
    back = back_send[z].astype(f32)
    for k, _ in along:
        back += back_got[k].astype(f32)
    second_grad = back + lg[z]
    resid_grad = cot_rows + norm_back(second_grad, normed2, scale2, wide(gain2))
    lg[z] = resid_grad
    low_rows = resid_grad.astype(bf16)
    low[z] = low_rows
    for c in range(cuts):
        cg_out[c] = lane_dot(low_rows, wo[c], 1, 1).astype(bf16)
    cg_along = [send(cg_out.at[peer], cg_in.at[z], {"tensor": peer}) for _, peer in along]
    cg_in[z] = cg_out[z]

    small[...] = jnp.zeros_like(small)
    small[0:experts_all] = jnp.where(z == 0, router_grad[:experts_all], 0.0)
    small[experts_all : experts_all + 1] = jnp.sum(second_grad * normed2, axis=0, keepdims=True)
    small[experts_all + 1 : experts_all + 2] = jnp.sum(second_grad, axis=0, keepdims=True)
    slab_low = lambda c: low.at[c]
    low_along = spread(low.at[z], slab_low)
    mix_across.wait_recv()
    layer_rows = resid[pl.ds(pl.multiple_of(z * rows, 8), rows)] + mixed[0]
    end_layer[...] = (layer_rows + mix_in[...].astype(f32)).astype(bf16)
    slab_layer = lambda c: layers.at[c]
    layer_along = spread(end_layer, slab_layer)

    for copy in cg_along:
        copy.wait_recv()
    ctx_grad = jnp.concatenate([cg_in[c].astype(f32) for c in range(cuts)])[:ctx_rows].astype(bf16)
    own_ctx = ctx_own[...]
    product = ctx_grad.astype(f32) * own_ctx.astype(f32)
    query_grad = jnp.zeros((ctx_rows, local), f32)
    keys_grad = jnp.zeros((ctx_rows, local), f32)
    values_grad = jnp.zeros((ctx_rows, local), f32)
    query, keys, values = qkv[0], qkv[1], qkv[2]
    for h in range(heads):
        chance = probs[h]
        grad_h = of_head(ctx_grad, h)
        delta = jnp.sum(of_head(product, h), axis=-1, keepdims=True)
        values_grad += lane_dot(chance.astype(bf16), grad_h, 0, 0)
        score_grad = (chance * (lane_dot(grad_h, values, 1, 1) - delta) * scaling).astype(bf16)
        query_grad += lane_dot(score_grad, of_head(keys, h), 1, 0)
        keys_grad += lane_dot(score_grad, of_head(query, h), 0, 0)
    grads = [g.astype(bf16) for g in (query_grad, keys_grad, values_grad)]
    passed_on(low_along, slab_low)
    passed_on(layer_along, slab_layer)
    partial = sum(lane_dot(grads[k], w_in[k], 1, 0) for k in range(3))
    partial = jnp.concatenate([partial, jnp.zeros((padded - ctx_rows, width), f32)])
    early_rows = first_a.shape[1]
    for c in range(cuts):
        first_a[c] = partial[c * rows : c * rows + early_rows].astype(bf16)
        first_b[c] = partial[c * rows + early_rows : (c + 1) * rows].astype(bf16)
    turns = [along[1], along[0], along[2]]
    first_along = [
        [send(source.at[peer], target.at[k], {"tensor": peer}) for k, peer in turns]
        for source, target in ((first_a, first_got_a), (first_b, first_got_b))
    ]
    small[experts_all + 2 : experts_all + 3] = jnp.sum(partial * n1[...], axis=0, keepdims=True)
    small[experts_all + 3 : experts_all + 4] = jnp.sum(partial, axis=0, keepdims=True)
    members = small_send.shape[0]
    cut = width // members
    for m in range(members):
        small_send[m, :, 0:cut] = small[:, m * cut : (m + 1) * cut]
    me = d * 2 + e
    small_across = [
        send(
            small_send.at[device["dp"] * 2 + device["expert"]], small_got.at[k], device
        )
        for k, device in enumerate(others)
    ]
    top = first[0:ctx_rows]
    results = [lane_dot(top, g, 0, 0).astype(bf16) for g in grads]
    for copy in low_along[::2]:
        copy.wait_recv()
    resid_low = jnp.concatenate([low[c].astype(f32) for c in range(cuts)])
    results.append(lane_dot(resid_low[:ctx_rows].astype(bf16), own_ctx, 0, 0).astype(bf16))
    for m in range(members):
        for k in range(4):
            gbuf[(m // 2) % 2, (m // 4) * 2 + m % 2, :, k * local : (k + 1) * local] = results[k][
                m * cut : (m + 1) * cut
            ]
    g_core = send(gbuf.at[1 - core], g_got, other_core)

    kept = []

    def keep(source, target):
        copy = pltpu.make_async_copy(source, target, load.at[13 + len(kept)])
        copy.start()
        kept.append(copy)

    keep(end_layer, layers.at[z])
    g_core.wait_recv()
    for m in range(members // 2):
        gbuf[core, m] = (gbuf[core, m].astype(f32) + g_got[m].astype(f32)).astype(bf16)
    mine = y * 2 + e
    g_across = [
        send(gbuf.at[core, place_], g_parts.at[k], device)
        for k, place_, device in [
            (1, y * 2 + 1 - e, other_x),
            (2, (1 - y) * 2 + e, other_y),
            (3, (1 - y) * 2 + 1 - e, diagonal),
        ]
    ]
    keep(gbuf.at[core, mine], g_parts.at[0])
    for copy in small_across:
        copy.wait_recv()
    added = small_send[me]
    for k in range(members - 1):
        added += small_got[k]
    small_sum[...] = added
    keep(small_sum, small_parts.at[0])
    small_along = [
        send(small_sum, small_parts.at[k], {"tensor": peer}) for k, peer in along
    ]

    normed_rows, scale_rows = normalize(x32[pl.ds(pl.multiple_of(z * rows, 8), rows)])
    base_grad = lg[z]
    final_along = []
    for part, (sent, got, end, final) in enumerate(
        [(first_a, first_got_a, end_a, final_a), (first_b, first_got_b, end_b, final_b)]
    ):
        span = slice(0, early_rows) if part == 0 else slice(early_rows, rows)
        for copy in first_along[part]:
            copy.wait_recv()
        first_grad = sent[z].astype(f32)
        for k, _ in along:
            first_grad += got[k].astype(f32)
        grad_rows = base_grad[span] + norm_back(
            first_grad, normed_rows[span], scale_rows[span], wide(gain1)
        )
        end[...] = grad_rows.astype(bf16)
        final_along += [send(end, final.at[z], {"tensor": peer}) for _, peer in along]
        keep(end, final.at[z])
    for k in range(here):
        e_row[k].wait_recv()
        for a in range(2):
            e_total[a, k] = ebuf[core, k, y, a].astype(f32) + e_peer[k, a].astype(f32)
    keep(e_total, e_sum)
    for copy in kept:
        copy.wait()
    for copy in layer_along[::2] + final_along + g_across + small_along:
        copy.wait_recv()
    for copy in pending:
        copy.wait_send()


def finish_kernel(dims, *refs):
    tokens, experts_all, local = dims
    f32 = jnp.float32
    given = refs[:6]
    layer_out, grad_out, gain1, bias1, att_in_out, att_out_out, gain2, bias2, router = refs[6:15]
    in_out, out_out = refs[15:17]
    final_a, final_b, layers, e_sum, g_parts, small_parts = held = refs[17:23]
    layer, grad, att_in, att_out = refs[23:27]
    load, store = refs[27:]
    cuts = layers.shape[0]
    cut = gain1.shape[1]
    loads = [
        pltpu.make_async_copy(given[i], held[i], load.at[i]) for i in range(6)
    ]
    stores = []

    def keep(source, target):
        copy = pltpu.make_async_copy(source, target, store.at[len(stores)])
        copy.start()
        stores.append(copy)

    for i in (3, 2, 0, 1, 4, 5):
        loads[i].start()
    loads[3].wait()
    keep(e_sum.at[0], in_out)
    keep(e_sum.at[1], out_out)
    loads[2].wait()
    whole = jnp.concatenate([layers[c].astype(f32) for c in range(cuts)])
    layer[...] = whole[:tokens]
    keep(layer, layer_out)
    loads[0].wait()
    loads[1].wait()
    whole = jnp.concatenate(
        [part[c].astype(f32) for c in range(cuts) for part in (final_a, final_b)]
    )
    grad[...] = whole[:tokens]
    keep(grad, grad_out)
    loads[4].wait()
    parts = sum(g_parts[k].astype(f32) for k in range(g_parts.shape[0]))
    for k in range(3):
        att_in[k] = parts[:, k * local : (k + 1) * local]
    keep(att_in, att_in_out)
    att_out[...] = parts[:, 3 * local :].T
    keep(att_out, att_out_out)
    loads[5].wait()
    totals = sum(small_parts[k] for k in range(cuts))[:, :cut]
    router[...] = totals[:experts_all]
    for i, target in enumerate((gain2, bias2, gain1, bias1)):
        target[...] = totals[experts_all + i : experts_all + i + 1]
    for copy in stores:
        copy.wait()


def per_device_general(
    inputs,
    first_gain,
    first_bias,
    attention_in,
    attention_out,
    second_gain,
    second_bias,
    router_weight,
    expert_in,
    expert_out,
    expert_ids,
    slot_index,
    cotangent,
):
    bf16, f32 = jnp.bfloat16, jnp.float32
    tokens_here = inputs.shape[0]
    model_width = inputs.shape[1]
    images = tokens_here // SEQ
    local_width = attention_in.shape[2]
    local_heads = local_width // HEAD_DIM
    owners = lax.axis_size("expert")
    cuts = lax.axis_size("tensor")
    experts_here = expert_in.shape[0]
    experts_all = experts_here * owners
    capacity = (2 * tokens_here - 1) // experts_all
    scaling = HEAD_DIM ** (-0.5)
    rows = rounded_up(rounded_up(tokens_here, cuts) // cuts, 8)
    padded = rows * cuts
    lanes = rounded_up(experts_all, 128)
    piece = lax.axis_index("tensor")

    def split_heads(matrix):
        return matrix.reshape(images, SEQ, local_heads, HEAD_DIM)

    def pad_rows(matrix, value=0):
        return jnp.pad(
            matrix, ((0, padded - tokens_here), (0, 0)), constant_values=value
        )

    def my_rows(matrix):
        return lax.dynamic_slice_in_dim(pad_rows(matrix), piece * rows, rows, 0)

    target = jnp.where(slot_index < capacity, expert_ids * capacity + slot_index, -1)
    target_all = from_owners(pad_rows(target, -1).astype(f32).T)
    cot_all = from_owners(pad_rows(cotangent))

    x_full = inputs.astype(f32)
    normed1, scale1 = normalize(x_full)
    first = (normed1 * first_gain + first_bias).astype(bf16)
    project = [
        jnp.dot(first, attention_in[which], preferred_element_type=f32).astype(bf16)
        for which in range(3)
    ]
    query_h, keys_h, values_h = [split_heads(part) for part in project]
    scores = jnp.einsum("iqhd,ikhd->ihqk", query_h, keys_h, preferred_element_type=f32) * scaling
    peak = jnp.max(scores, axis=-1, keepdims=True)
    logsum = peak[..., 0] + jnp.log(jnp.sum(jnp.exp(scores - peak), axis=-1))
    probs = jnp.exp(scores - logsum[..., None])
    weights = probs.astype(bf16)
    context_h = jnp.einsum(
        "ihqk,ikhd->iqhd", weights, values_h, preferred_element_type=f32
    ).astype(bf16)
    context = context_h.reshape(tokens_here, local_width)
    partial_attn = jnp.dot(pad_rows(context), attention_out, preferred_element_type=f32)
    (attn_parts,) = scattered([partial_attn.astype(bf16).reshape(cuts, rows, model_width)], 1)

    attended = jnp.sum(attn_parts.astype(f32), axis=0)
    resid = my_rows(inputs).astype(f32) + attended
    normed2, scale2 = normalize(resid)
    second = (normed2 * second_gain + second_bias).astype(bf16)
    (second_all,) = gathered([second], 2, forward=True)

    base = lax.axis_index("expert") * experts_here
    experts = base + jnp.arange(experts_here, dtype=jnp.int32)
    offset = target_all.astype(jnp.int32)[None] - (experts * capacity)[:, None, None, None]
    slots = jnp.max(jnp.where((offset >= 0) & (offset < capacity), offset, -1), axis=2)
    spot = (experts[:, None] == jnp.arange(lanes, dtype=jnp.int32)).astype(f32)
    mixed, back, share, route_all, expert_cuts = experts_block(
        slots,
        spot,
        second_all.reshape(owners, padded, model_width),
        cot_all,
        jnp.pad(router_weight, ((0, 0), (0, lanes - experts_all))),
        expert_in,
        expert_out,
        experts_all,
        rounded_up(capacity, 16),
    )
    route = lax.dynamic_slice_in_dim(route_all[0], piece * rows, rows, 0)[:, :experts_all]
    mixed_home = to_owners(mixed)
    back_home = to_owners(back)
    route_home = to_owners(share)
    expert_sums = jnp.sum(
        lax.all_to_all(expert_cuts, "dp", 0, 0, tiled=True).astype(f32), axis=0
    )
    expert_in_grad = expert_sums[0]
    expert_out_grad = jnp.swapaxes(expert_sums[1], 1, 2)
    parts = scattered(
        [
            mixed_home.astype(bf16).reshape(cuts, rows, model_width),
            back_home.astype(bf16).reshape(cuts, rows, model_width),
            route_home.reshape(cuts, rows, lanes),
        ],
        3,
    )
    moe, back_rows, route_grad = [jnp.sum(part.astype(f32), axis=0) for part in parts]
    route_grad = route_grad[:, :experts_all]

    layer_rows = resid + moe
    grad_out = my_rows(cotangent).astype(f32)
    logit_grad = route * (route_grad - jnp.sum(route * route_grad, axis=-1, keepdims=True))
    local_router = jnp.dot(
        second.astype(f32).T, logit_grad, precision=lax.Precision.HIGHEST
    )
    second_grad = back_rows + jnp.dot(logit_grad, router_weight.T, precision=lax.Precision.HIGHEST)
    local_second_gain = jnp.sum(second_grad * normed2, axis=0)
    local_second_bias = jnp.sum(second_grad, axis=0)
    resid_grad = grad_out + norm_back(second_grad, normed2, scale2, second_gain)
    (resid_all,) = gathered([resid_grad.astype(bf16)], 4)
    resid_low = resid_all.reshape(padded, model_width)[:tokens_here]

    context_grad = jnp.einsum(
        "rd,hd->rh", resid_low, attention_out, preferred_element_type=f32
    ).astype(bf16)
    context_g = split_heads(context_grad)
    values_grad = jnp.einsum(
        "ihqk,iqhd->ikhd", weights, context_g, preferred_element_type=f32
    ).astype(bf16)
    probs_grad = jnp.einsum("iqhd,ikhd->ihqk", context_g, values_h, preferred_element_type=f32)
    delta = jnp.transpose(
        jnp.sum(context_g.astype(f32) * context_h.astype(f32), axis=-1), (0, 2, 1)
    )
    score_grad = (probs * (probs_grad - delta[..., None]) * scaling).astype(bf16)
    query_grad = jnp.einsum(
        "ihqk,ikhd->iqhd", score_grad, keys_h, preferred_element_type=f32
    ).astype(bf16)
    keys_grad = jnp.einsum(
        "ihqk,iqhd->ikhd", score_grad, query_h, preferred_element_type=f32
    ).astype(bf16)
    grads_flat = [
        part.reshape(tokens_here, local_width) for part in (query_grad, keys_grad, values_grad)
    ]
    partial_first = sum(
        jnp.einsum("rh,dh->rd", grads_flat[k], attention_in[k], preferred_element_type=f32)
        for k in range(3)
    )
    local_first_gain = jnp.sum(partial_first * normed1, axis=0)
    local_first_bias = jnp.sum(partial_first, axis=0)
    members = lax.axis_size("dp") * owners
    share = model_width // members
    small = jnp.concatenate(
        [
            local_router.T,
            jnp.stack([local_first_gain, local_first_bias, local_second_gain, local_second_bias]),
        ]
    )
    tall = rounded_up(small.shape[0], 8)
    small = cut_along(small, 1, members)
    small = jnp.pad(
        small, ((0, 0), (0, tall - small.shape[1]), (0, rounded_up(share, 128) - share))
    )
    first_parts, small_parts = line_and_group(
        pad_rows(partial_first).astype(bf16).reshape(cuts, rows, model_width), small, 5, False
    )
    first_grad = jnp.sum(first_parts.astype(f32), axis=0)
    small_sum = jnp.sum(small_parts, axis=0)
    normed1_rows, scale1_rows = normalize(my_rows(inputs).astype(f32))
    grad_rows = resid_grad + norm_back(first_grad, normed1_rows, scale1_rows, first_gain)
    small_low = small_sum.astype(bf16)
    small_low = jnp.pad(small_low, ((0, rounded_up(tall, 16) - tall), (0, model_width - small_low.shape[1])))
    attention_cuts = jnp.stack(
        [
            jnp.einsum("rd,rh->dh", left, part, preferred_element_type=f32).astype(bf16)
            for left, part in zip([first] * 3 + [resid_low], grads_flat + [context])
        ],
        axis=1,
    ).reshape(members, share, 4, local_width)
    sent_rows = jnp.concatenate([grad_rows.astype(bf16), layer_rows.astype(bf16), small_low])
    grad_all, attention_parts = line_and_group(
        sent_rows, jnp.swapaxes(attention_cuts, 1, 2), 6, True
    )
    input_grad = grad_all[:, :rows].reshape(padded, model_width)[:tokens_here].astype(f32)
    layer_out = grad_all[:, rows : 2 * rows].reshape(padded, model_width)[:tokens_here].astype(f32)
    totals = jnp.sum(grad_all[:, 2 * rows :].astype(f32), axis=0)[:, :share]
    attention_sums = jnp.sum(attention_parts.astype(f32), axis=0)
    attention_in_grad = attention_sums[:3]
    attention_out_grad = attention_sums[3].T
    return (
        layer_out,
        input_grad,
        totals[experts_all],
        totals[experts_all + 1],
        attention_in_grad,
        attention_out_grad,
        totals[experts_all + 2],
        totals[experts_all + 3],
        totals[:experts_all].T,
        expert_in_grad,
        expert_out_grad,
    )


def per_device(
    inputs,
    first_gain,
    first_bias,
    attention_in,
    attention_out,
    second_gain,
    second_bias,
    router_weight,
    expert_in,
    expert_out,
    expert_ids,
    slot_index,
    cotangent,
):
    arguments = (
        inputs,
        first_gain,
        first_bias,
        attention_in,
        attention_out,
        second_gain,
        second_bias,
        router_weight,
        expert_in,
        expert_out,
        expert_ids,
        slot_index,
        cotangent,
    )
    owners, groups, cuts = [lax.axis_size(axis) for axis in ("expert", "dp", "tensor")]
    tokens, width = inputs.shape
    here = expert_in.shape[0]
    experts_all = here * owners
    if (owners, groups, cuts) != (2, 4, 4) or tokens != SEQ or experts_all > 4:
        return per_device_general(*arguments)
    bf16, f32 = jnp.bfloat16, jnp.float32
    capacity = (2 * tokens - 1) // experts_all
    depth = rounded_up(capacity, 16)
    local = attention_in.shape[2]
    heads = local // HEAD_DIM
    rows = rounded_up(rounded_up(tokens, cuts) // cuts, 8)
    padded = rows * cuts
    ctx_rows = rounded_up(tokens, 16)
    members = owners * groups
    cut = width // members
    share = width // groups
    slots = here * depth
    vmem = pl.BlockSpec(memory_space=pltpu.VMEM)
    early_rows = rounded_up(rows // 2, 16)
    anywhere = pl.BlockSpec(memory_space=pl.ANY)
    shapes = [
        ((cuts, early_rows, width), bf16),
        ((cuts, rows - early_rows, width), bf16),
        ((cuts, rows, width), bf16),
        ((2, here, share, width), f32),
        ((members // 2, cut, 4 * local), bf16),
        ((cuts, 8, 128), f32),
    ]
    slab = (cuts, rows, width)
    vectors = [((width,), f32)] * 4
    scratch = [
        (inputs.shape, bf16),
        (cotangent.shape, bf16),
        *vectors,
        ((experts_all, width), f32),
        ((2, tokens), jnp.int32),
        ((2, tokens), jnp.int32),
        ((padded, width), f32),
        ((padded, width), f32),
        ((2, padded, width), bf16),
        ((padded, width), bf16),
        ((rows, width), bf16),
        (slab, bf16),
        ((2, 8, 256), f32),
        ((8, width), f32),
        ((3, local, width), bf16),
        ((cuts, local, width), bf16),
        ((2, cuts, ctx_rows // 2, 2 * local), bf16),
        ((ctx_rows, local), bf16),
        (expert_in.shape, bf16),
        (expert_out.shape, bf16),
        ((2, padded, width), bf16),
        ((padded, width), f32),
        ((padded, width), bf16),
        ((padded, width), f32),
        ((3, ctx_rows, local), bf16),
        ((heads, ctx_rows, ctx_rows), f32),
        (slab, bf16),
        (slab, bf16),
        (slab, bf16),
        (slab, bf16),
        (slab, bf16),
        ((rows, width), bf16),
        ((rows, width), bf16),
        ((2, *slab), bf16),
        ((2, rows, width), bf16),
        ((2, 3, rows, width), bf16),
        ((rows, width), bf16),
        ((early_rows, width), bf16),
        ((rows - early_rows, width), bf16),
        ((8, 128), f32),
        ((8, 256), f32),
        ((8, 256), f32),
        ((cuts, 8, 256), f32),
        (slab, bf16),
        (slab, f32),
        ((cuts, rows, local), bf16),
        ((cuts, rows, local), bf16),
        ((2, here, 2, 2, share, width), bf16),
        ((here, 2, 2, share, width), bf16),
        ((here, 2, share, width), bf16),
        ((2, here, share, width), f32),
        ((2, members // 2, cut, 4 * local), bf16),
        ((members // 2, cut, 4 * local), bf16),
        ((cuts, early_rows, width), bf16),
        ((cuts, rows - early_rows, width), bf16),
        ((cuts, early_rows, width), bf16),
        ((cuts, rows - early_rows, width), bf16),
        ((8, width), f32),
        ((members, 8, 128), f32),
        ((members, 8, 128), f32),
        ((2, slots, width), bf16),
        ((here, 2 * depth, width), bf16),
        ((here, 2 * depth, width), bf16),
        ((here, 2 * depth, width), bf16),
        ((here, 2 * depth, width), bf16),
        ((2, slots, padded), bf16),
        ((2, slots, width), bf16),
    ]
    sems = [pltpu.SemaphoreType.DMA((n,)) for n in (20, 96, 96)]
    received = pl.pallas_call(
        functools.partial(block_kernel, (tokens, rows, cuts, experts_all, capacity, depth)),
        out_shape=[jax.ShapeDtypeStruct(*s) for s in shapes],
        in_specs=[anywhere] * 13,
        out_specs=[anywhere] * 6,
        scratch_shapes=[pltpu.VMEM(*s) for s in scratch] + sems,
        compiler_params=pltpu.CompilerParams(
            collective_id=0, has_side_effects=True, vmem_limit_bytes=56 << 20
        ),
        name="block",
    )(
        inputs,
        cotangent,
        first_gain,
        first_bias,
        second_gain,
        second_bias,
        router_weight.T,
        expert_ids.T,
        slot_index.T,
        jnp.swapaxes(attention_in, 1, 2),
        attention_out,
        expert_in,
        expert_out,
    )
    results = [
        ((tokens, width), f32),
        ((tokens, width), f32),
        ((1, cut), f32),
        ((1, cut), f32),
        ((3, cut, local), f32),
        ((local, cut), f32),
        ((1, cut), f32),
        ((1, cut), f32),
        ((experts_all, cut), f32),
        ((here, share, width), f32),
        ((here, share, width), f32),
    ]
    large = [results[i] for i in (0, 1, 4, 5)]
    out = pl.pallas_call(
        functools.partial(finish_kernel, (tokens, experts_all, local)),
        out_shape=[jax.ShapeDtypeStruct(*s) for s in results],
        in_specs=[anywhere] * 6,
        out_specs=[anywhere] * 2 + [vmem] * 2 + [anywhere] * 2 + [vmem] * 3 + [anywhere] * 2,
        scratch_shapes=[pltpu.VMEM(*s) for s in shapes + large]
        + [pltpu.SemaphoreType.DMA((n,)) for n in (6, 6)],
        compiler_params=pltpu.CompilerParams(vmem_limit_bytes=56 << 20),
        name="finish",
    )(*received)
    return (
        out[0],
        out[1],
        out[2].reshape(cut),
        out[3].reshape(cut),
        out[4],
        out[5],
        out[6].reshape(cut),
        out[7].reshape(cut),
        out[8].T,
        out[9],
        jnp.swapaxes(out[10], 1, 2),
    )


def solution(mesh):
    in_specs = (
        P(("dp", "expert"), None),
        P(),
        P(),
        P(None, None, "tensor"),
        P("tensor", None),
        P(),
        P(),
        P(),
        P("expert", None, "tensor"),
        P("expert", "tensor", None),
        P(("dp", "expert"), None),
        P(("dp", "expert"), None),
        P(("dp", "expert"), None),
    )
    out_specs = (
        P(("dp", "expert"), None),
        P(("dp", "expert"), None),
        P(("dp", "expert")),
        P(("dp", "expert")),
        P(None, ("dp", "expert"), "tensor"),
        P("tensor", ("dp", "expert")),
        P(("dp", "expert")),
        P(("dp", "expert")),
        P(("dp", "expert"), None),
        P("expert", "dp", "tensor"),
        P("expert", "tensor", "dp"),
    )
    return jax.shard_map(
        per_device, mesh=mesh, in_specs=in_specs, out_specs=out_specs, check_vma=False
    )
```
